32 devices in a mesh: gx: 8 (over z, core), gy: 4 (over y, x).
Axes of the slice: x: 2, y: 2, z: 4, core: 2. Of those that a mesh axis runs over, the one named last changes fastest.
Arguments:
- base_state: float32 [3, 32, 32, 128], P(None, 'gx', 'gy'), may hold values from -5 to 5
- adjoint_block: float32 [32, 3, 32, 32, 128], P(None, None, 'gx', 'gy'), may hold values from -2500 to 2500
Outputs:
- q_block: float32 [32, 3, 32, 32, 128], P(None, None, 'gx', 'gy')
- r_factor: float32 [32, 32], replicated
The draws below stay inside these ranges and needn't reach their ends.
All inputs are finite; a program needn't handle non-finite values.
Results may differ from the reference program's by a relative error of at most 0.00015.
Values sent between devices are 32-bit elements; how exact they have to be, the bound alone decides.
A program may use at most 64 MiB of HBM per device.

```python
import math
import jax
import jax.numpy as jnp
from jax import lax

VECS = 32
NZ = 128
NX = 32
NY = 32


def draw_adjoint_block(key, part):
    keys = jax.random.split(jax.random.fold_in(key, 17), 7)
    shape = (VECS, 3, NX, NY, NZ)
    field_shape = (1, 3, NX, NY, NZ)
    noise = jnp.clip(jax.random.normal(keys[0], shape, jnp.float32), -5.0, 5.0)
    spread = 1.0
    common_one = jnp.clip(jax.random.normal(keys[1], field_shape, jnp.float32), -4.0, 4.0)
    common_two = jnp.clip(jax.random.normal(keys[2], field_shape, jnp.float32), -4.0, 4.0)
    mix_one = jax.random.uniform(keys[3], (VECS, 1, 1, 1, 1), jnp.float32, -spread, spread)
    mix_two = jax.random.uniform(keys[4], (VECS, 1, 1, 1, 1), jnp.float32, -spread, spread)
    row_scale = jnp.exp(jax.random.uniform(keys[5], (VECS, 1, 1, 1, 1), jnp.float32, 0.0, math.log(10.0)))
    along_x = jnp.arange(NX, dtype=jnp.float32)[:, None] / float(NX)
    along_y = jnp.arange(NY, dtype=jnp.float32)[None, :] / float(NY)
    exponent = 0.5 * along_x + 0.5 * along_y
    rough = jax.random.uniform(keys[6], (1, 1, NX, NY, 1), jnp.float32, 0.7, 1.4)
    spatial = jnp.exp(math.log(10.0) * exponent)[None, None, :, :, None] * rough
    return row_scale * spatial * (noise + mix_one * common_one + mix_two * common_two)


def steps_of(stream_key, dims, cuts, low, top_value):
    factor_of, own = 1.0, jax.random.fold_in(stream_key, 6)
    for dim, blocks in cuts:
        draws = jnp.exp(jax.random.uniform(jax.random.fold_in(own, dim), (blocks,), jnp.float32, low / len(cuts), top_value / len(cuts)))
        factor_of = factor_of * jnp.repeat(draws, dims[dim] // blocks).reshape([-1 if axis == dim else 1 for axis in range(len(dims))])
    return factor_of


def normal_values(rng, shape, scale, reach, pieces=(), kind=jnp.bfloat16):
    drawn = scale * jax.random.normal(rng, shape, jnp.float32)
    if pieces:
        drawn = drawn * steps_of(rng, shape, pieces, -0.22, 0.18)
    return jnp.clip(drawn, -reach, reach).astype(kind)


def setup_inputs(seed: int = 0) -> dict:
    arg_keys = jax.random.split(jax.random.key(seed), 3)
    return {
        "base_state": normal_values(arg_keys[0], (3, NX, NY, NZ), 1.0, 5.0, ((1, 8), (2, 4)), jnp.float32),
        "adjoint_block": draw_adjoint_block(jax.random.fold_in(arg_keys[2], 71), 0),
    }


ADVECT = 0.1
DIFFUSE = 0.08
DRIVE_SCALE = 0.25
WAVENUMBER = 4.0

def advance(padded, column_index, ny_total):
    centre = padded[:, 1:-1, 1:-1, :]
    eastern = padded[:, 2:, 1:-1, :]
    western = padded[:, :-2, 1:-1, :]
    northern = padded[:, 1:-1, 2:, :]
    southern = padded[:, 1:-1, :-2, :]
    upward = jnp.roll(centre, -1, axis=3)
    downward = jnp.roll(centre, 1, axis=3)
    laplacian = eastern + western + northern + southern + upward + downward - 6.0 * centre
    advection = centre[0:1] * (eastern - western) + centre[1:2] * (northern - southern) + centre[2:3] * (upward - downward)
    phases = 2.0 * math.pi * WAVENUMBER * column_index.astype(jnp.float32) / float(ny_total)
    forcing = DRIVE_SCALE * jnp.sin(phases)
    nothing = jnp.zeros_like(forcing)
    driven = jnp.stack([forcing, nothing, nothing])[:, None, :, None]
    return centre + DIFFUSE * laplacian - ADVECT * advection + driven

def adjoint(base_ext, block_ext):
    inner = block_ext[:, :, 1:-1, 1:-1, :]
    base_inner = base_ext[:, 1:-1, 1:-1, :]
    base_east = base_ext[:, 2:, 1:-1, :]
    base_west = base_ext[:, :-2, 1:-1, :]
    base_north = base_ext[:, 1:-1, 2:, :]
    base_south = base_ext[:, 1:-1, :-2, :]
    block_east = block_ext[:, :, 2:, 1:-1, :]
    block_west = block_ext[:, :, :-2, 1:-1, :]
    block_north = block_ext[:, :, 1:-1, 2:, :]
    block_south = block_ext[:, :, 1:-1, :-2, :]
    carried = base_inner[2] * inner
    flux = base_east[0] * block_east - base_west[0] * block_west
    flux = flux + base_north[1] * block_north - base_south[1] * block_south
    flux = flux + jnp.roll(carried, -1, axis=-1) - jnp.roll(carried, 1, axis=-1)
    grad_x = base_east - base_west
    grad_y = base_north - base_south
    grad_z = jnp.roll(base_inner, -1, axis=3) - jnp.roll(base_inner, 1, axis=3)
    coupling = jnp.stack([jnp.sum(inner * grad_x, axis=1), jnp.sum(inner * grad_y, axis=1), jnp.sum(inner * grad_z, axis=1)], axis=1)
    laplacian = block_east + block_west + block_north + block_south + jnp.roll(inner, -1, axis=-1) + jnp.roll(inner, 1, axis=-1) - 6.0 * inner
    return inner + ADVECT * (flux - coupling) + DIFFUSE * laplacian

def reference(base_state, adjoint_block):
    ny_total = base_state.shape[2]
    widths = ((0, 0), (1, 1), (1, 1), (0, 0))
    padded = jnp.pad(base_state, widths, mode='wrap')
    advanced = advance(padded, jnp.arange(ny_total, dtype=jnp.int32), ny_total)
    base_ext = jnp.pad(advanced, widths, mode='wrap')

    def one_vector(vector):
        extended = jnp.pad(vector, widths, mode='wrap')[None]
        return adjoint(base_ext, extended)[0]
    updated = lax.map(one_vector, adjoint_block)
    vectors = updated.shape[0]
    flat = updated.reshape(vectors, -1)
    gram = jnp.dot(flat.astype(jnp.float32), flat.T.astype(jnp.float32), precision=lax.Precision.HIGHEST, preferred_element_type=jnp.float32) / float(flat.shape[1])
    lower = jnp.linalg.cholesky(gram)
    inverse = lax.linalg.triangular_solve(lower, jnp.eye(vectors, dtype=jnp.float32), left_side=True, lower=True)
    q_block = jnp.dot(inverse.astype(jnp.float32), flat.astype(jnp.float32), precision=lax.Precision.HIGHEST, preferred_element_type=jnp.float32).reshape(updated.shape)
    return (q_block, lower.T)
```

```python
import functools
import math

import jax
import jax.numpy as jnp
from jax import lax
from jax.experimental import pallas as pl
from jax.experimental.pallas import tpu as pltpu
from jax.sharding import PartitionSpec as P

ADVECT = 0.1
DIFFUSE = 0.08
DRIVE_SCALE = 0.25
WAVENUMBER = 4.0
MESH = pl.DeviceIdType.MESH


WIDE = 2
SIDES = ((-1, 0), (1, 0), (0, -1), (0, 1), (-1, -1), (-1, 1), (1, -1), (1, 1))


def neighbour(nx, ny, dx, dy):
    return (lax.rem(lax.axis_index("gx") + dx + nx, nx), lax.rem(lax.axis_index("gy") + dy + ny, ny))


def meet(nx, ny):
    barrier = pltpu.get_barrier_semaphore()
    for dx, dy in SIDES:
        pl.semaphore_signal(barrier, inc=1, device_id=neighbour(nx, ny, dx, dy), device_id_type=MESH)
    return barrier, len(SIDES)


def rounds(nx, ny):
    steps, reach = [], 1
    while 2 * reach < nx:
        steps.append((reach, 0))
        reach *= 2
    reach = 1
    while 2 * reach < ny:
        steps.append((0, reach))
        reach *= 2
    return steps


def tell(nx, ny, heard, n):
    dx, dy = rounds(nx, ny)[n]
    for sign in (-1, 1):
        pl.semaphore_signal(
            heard.at[n], inc=1, device_id=neighbour(nx, ny, sign * dx, sign * dy), device_id_type=MESH)


def each(low, high, body):
    if high - low <= 64:
        for i in range(low, high):
            body(i)
        return

    def run(i, carry):
        body(i)
        return carry

    lax.fori_loop(low, high, run, 0)


def advance_rows(bext, forcing, x, wide_y):
    rows = wide_y + 2
    centre = [bext[c, x + 1, 1 : 1 + rows, :] for c in range(3)]
    advanced = []
    for c in range(3):
        east, west = bext[c, x + 2, 1 : 1 + rows, :], bext[c, x, 1 : 1 + rows, :]
        north, south = bext[c, x + 1, 2 : 2 + rows, :], bext[c, x + 1, 0:rows, :]
        up, down = pltpu.roll(centre[c], 127, axis=1), pltpu.roll(centre[c], 1, axis=1)
        laplacian = east + west + north + south + up + down - 6.0 * centre[c]
        advection = centre[0] * (east - west) + centre[1] * (north - south) + centre[2] * (up - down)
        value = centre[c] + DIFFUSE * laplacian - ADVECT * advection
        advanced.append(value + forcing if c == 0 else value)
    return advanced


def step_kernel(
    nx, ny, entries, base_in, a_in, rows_in, high, low, total, base, a2, in_sem, edges, bx, by, bc, bext, adv, coef, at,
    split, natural, slots, base_send, base_recv, halo_send, halo_recv, heard, gram_send, gram_recv,
):
    wide_x, wide_y = base.shape[1], base.shape[2]
    vectors = at.shape[3]
    stride = 3 * wide_x * wide_y
    gx, gy = lax.axis_index("gx"), lax.axis_index("gy")
    devices, me = nx * ny, gx * ny + gy
    barrier, met = meet(nx, ny)
    base_load = pltpu.make_async_copy(base_in, base, in_sem.at[0])
    load = pltpu.make_async_copy(a_in, a2, in_sem.at[1])
    base_load.start()
    load.start()

    def move(c):
        def plane_of(x, carry):
            for y in range(wide_y):
                at[c, x + 1, y + 1] = a2[pl.ds((c * wide_x + x) * wide_y + y, vectors, stride=stride), :]
            return carry
        lax.fori_loop(0, wide_x, plane_of, 0)

    def base_copy(i):
        dx, dy = SIDES[i]
        near_x = pl.ds(0, WIDE) if dx < 0 else pl.ds(wide_x - WIDE, WIDE)
        side = 0 if dy < 0 else 1
        if dy == 0:
            src, dst = base.at[:, near_x], bx.at[(1 - dx) // 2]
        elif dx == 0:
            src, dst = edges.at[side], by.at[1 - side]
        else:
            src, dst = edges.at[side, near_x], bc.at[(1 - dx) // 2, 1 - side]
        return pltpu.make_async_remote_copy(
            src, dst, base_send.at[i], base_recv.at[i],
            device_id=neighbour(nx, ny, dx, dy), device_id_type=MESH)

    inner_x, inner_y = pl.ds(1, wide_x), pl.ds(1, wide_y)

    def halo_start(c, i):
        dx, dy = SIDES[i]
        peer = neighbour(nx, ny, dx, dy)
        if dx:
            near, far = (0, wide_x + 1) if dx < 0 else (wide_x - 1, 0)
            pairs = [(rows_in.at[:, c, near, y, 0], at.at[c, far, y + 1]) for y in range(wide_y)]
        else:
            near, far = (0, wide_y + 1) if dy < 0 else (wide_y - 1, 0)
            pairs = [(rows_in.at[:, c, x, near, 0], at.at[c, x + 1, far]) for x in range(wide_x)]
        for src, dst in pairs:
            pltpu.make_async_remote_copy(
                src, dst, halo_send.at[c, i], halo_recv.at[c, i], device_id=peer, device_id_type=MESH).start()

    def halo(c, i):
        dx, dy = SIDES[i]
        if dx:
            whole = at.at[c, wide_x + 1 if dx < 0 else 0, inner_y]
        else:
            whole = at.at[c, inner_x, wide_y + 1 if dy < 0 else 0]
        return pltpu.make_async_remote_copy(
            whole, whole, halo_send.at[c, i], halo_recv.at[c, i],
            device_id=neighbour(nx, ny, dx, dy), device_id_type=MESH)

    base_load.wait()
    for side, start in ((0, 0), (1, wide_y - WIDE)):
        for c in range(3):
            edges[side, :, c] = base[c, :, start : start + WIDE, :]
    pl.semaphore_wait(barrier, met)
    for i in range(8):
        base_copy(i).start()
    for c in range(3):
        for i in range(4):
            halo_start(c, i)
    tells = len(rounds(nx, ny))

    def spread(n):
        if n:
            pl.semaphore_wait(heard.at[n - 1], 2)
        if n < tells:
            tell(nx, ny, heard, n)

    spread(0)
    load.wait()
    for c in range(3):
        move(c)

    for c in range(3):
        bext[c, WIDE : WIDE + wide_x, WIDE : WIDE + wide_y, :] = base[c]
    for i in range(8):
        base_copy(i).wait_recv()
    near, far = WIDE + wide_x, WIDE + wide_y
    for c in range(3):
        for sx, start_x in ((0, 0), (1, near)):
            bext[c, start_x : start_x + WIDE, WIDE:far, :] = bx[sx, c]
            for sy, start_y in ((0, 0), (1, far)):
                bext[c, start_x : start_x + WIDE, start_y : start_y + WIDE, :] = bc[sx, sy, :, c]
        for sy, start_y in ((0, 0), (1, far)):
            bext[c, WIDE:near, start_y : start_y + WIDE, :] = by[sy, :, c]

    ny_total = wide_y * ny
    column = lax.broadcasted_iota(jnp.int32, (wide_y + 2, 128), 0) + (gy * wide_y + ny_total - 1)
    phases = 2.0 * math.pi * WAVENUMBER * lax.rem(column, ny_total).astype(jnp.float32) / float(ny_total)
    forcing = DRIVE_SCALE * jnp.sin(phases)
    for x in range(wide_x + 2):
        for c, value in enumerate(advance_rows(bext, forcing, x, wide_y)):
            adv[c, x, 0 : wide_y + 2, :] = value
    for x in range(wide_x):
        inner = [adv[m, x + 1, 1 : 1 + wide_y, :] for m in range(3)]
        coef[0, x] = ADVECT * adv[0, x + 2, 1 : 1 + wide_y, :] + DIFFUSE
        coef[1, x] = DIFFUSE - ADVECT * adv[0, x, 1 : 1 + wide_y, :]
        coef[2, x] = ADVECT * adv[1, x + 1, 2 : 2 + wide_y, :] + DIFFUSE
        coef[3, x] = DIFFUSE - ADVECT * adv[1, x + 1, 0:wide_y, :]
        coef[4, x] = ADVECT * inner[2] + DIFFUSE
        coef[5, x] = DIFFUSE - ADVECT * inner[2]
        for m in range(3):
            slopes = (
                adv[m, x + 2, 1 : 1 + wide_y, :] - adv[m, x, 1 : 1 + wide_y, :],
                adv[m, x + 1, 2 : 2 + wide_y, :] - adv[m, x + 1, 0:wide_y, :],
                pltpu.roll(inner[m], 127, axis=1) - pltpu.roll(inner[m], 1, axis=1),
            )
            for i in range(3):
                own = 1.0 - 6.0 * DIFFUSE if i == m else 0.0
                coef[6 + 3 * i + m, x] = own - ADVECT * slopes[i]

    spread(1)

    def plane_of(c, x):
        columns = []
        for y in range(wide_y):
            k = [coef[n, x, y : y + 1, :] for n in range(6)]
            k += [coef[6 + 3 * c + m, x, y : y + 1, :] for m in range(3)]
            own = [at[m, x + 1, y + 1] for m in range(3)]
            value = k[0] * at[c, x + 2, y + 1] + k[1] * at[c, x, y + 1]
            value += k[2] * at[c, x + 1, y + 2] + k[3] * at[c, x + 1, y]
            value += pltpu.roll(k[4] * own[c], 127, axis=1) + pltpu.roll(k[5] * own[c], 1, axis=1)
            value += k[6] * own[0] + k[7] * own[1] + k[8] * own[2]
            natural[pl.ds(((c * wide_x + x) * vectors) * wide_y + y, vectors, stride=wide_y), :] = value
            columns.append(value)
        updated = jnp.concatenate(columns, axis=1)
        first = updated.astype(jnp.bfloat16)
        second = (updated - first.astype(jnp.float32)).astype(jnp.bfloat16)
        split[x, 0:vectors, :] = first
        split[x, vectors : 2 * vectors, :] = second

    gram = jnp.zeros((2 * vectors, 2 * vectors), jnp.float32)
    for c in range(3):
        for i in (2, 3):
            halo(c, i).wait_recv()

        def inside(x, carry, c=c):
            plane_of(c, x)
            return carry

        def outside(n, carry, c=c):
            plane_of(c, n * (wide_x - 1))
            return carry

        lax.fori_loop(1, wide_x - 1, inside, 0)
        for i in (0, 1):
            halo(c, i).wait_recv()
        lax.fori_loop(0, 2, outside, 0)
        both = jnp.concatenate([split[x] for x in range(wide_x)], axis=1)
        gram += lax.dot_general(both, both, (((1,), (1,)), ((), ())), preferred_element_type=jnp.float32)
        if c < 2:
            spread(2 + c)
    for n in range(4, tells + 1):
        spread(n)

    gram = gram[:vectors] + gram[vectors:]
    gram = gram[:, :vectors] + gram[:, vectors:]
    slots[me] = jnp.concatenate([gram[8 * i : 8 * i + 8] for i in range(4)], axis=1)

    def give(step):
        there = lax.rem(me + step, devices)
        pltpu.make_async_remote_copy(
            slots.at[me], slots.at[me], gram_send, gram_recv,
            device_id=(there // ny, lax.rem(there, ny)), device_id_type=MESH).start()

    each(1, devices, give)

    def convert(n, carry):
        for part in range(2):
            value = natural[pl.ds(pl.multiple_of((2 * n + part) * vectors * wide_y, 256), vectors * wide_y), :]
            first = value.astype(jnp.bfloat16)
            high[n, :, part * 128 : part * 128 + 128] = first
            low[n, :, part * 128 : part * 128 + 128] = (value - first.astype(jnp.float32)).astype(jnp.bfloat16)
        return carry

    lax.fori_loop(0, high.shape[0], convert, 0)
    others = slots.at[pl.ds(0, devices - 1)]
    gathered = pltpu.make_async_remote_copy(
        others, others, gram_send, gram_recv, device_id=neighbour(nx, ny, 0, 1), device_id_type=MESH)
    gathered.wait_recv()
    if devices <= 64:
        level = [slots[i] for i in range(devices)]
        while len(level) > 1:
            level = [sum(level[i : i + 2][1:], level[i]) for i in range(0, len(level), 2)]
        summed = level[0]
    else:
        summed = lax.fori_loop(1, devices, lambda i, value: value + slots[i], slots[0])
    total[...] = summed / entries
    gathered.wait_send()
    for i in range(8):
        base_copy(i).wait_send()
    for c in range(3):
        for i in range(4):
            halo(c, i).wait_send()


def eliminate(packed):
    shape = packed.shape
    row, lane = lax.broadcasted_iota(jnp.int32, shape, 0), lax.broadcasted_iota(jnp.int32, shape, 1)
    left = [packed] + [pltpu.roll(packed, 128 - 32 * i, axis=1) for i in range(1, 4)]
    right = [[(lane // 8 + 16 * h == row + 8 * i).astype(jnp.float32) for h in range(2)] for i in range(4)]
    pivots = []
    for p in range(4):
        rest = range(p, 4)
        columns = [
            {i: jnp.broadcast_to(left[i][:, k : k + 1], shape) for i in rest} for k in range(8 * p, 8 * p + 8)]
        pivot = jnp.ones(shape, jnp.float32)
        for j in range(8):
            here = columns[j][p][j : j + 1, :]
            pivot = jnp.where(row == j, here, pivot)
            inverse = 1.0 / here
            factor = {i: columns[j][i] * inverse for i in rest}
            factor[p] = jnp.where(row > j, factor[p], 0.0)
            for l in range(j + 1, 8):
                across = columns[l][p][j : j + 1, :]
                for i in rest:
                    columns[l][i] = columns[l][i] - factor[i] * across
            across = left[p][j : j + 1, :]
            for i in rest:
                left[i] = left[i] - factor[i] * across
            for h in range(2 if p >= 2 else 1):
                across = right[p][h][j : j + 1, :]
                for i in rest:
                    right[i][h] = right[i][h] - factor[i] * across
        pivots.append(pivot)
    upper = []
    for i in range(4):
        scale = lax.rsqrt(pivots[i])
        upper.append(jnp.where(lane >= row + 8 * i, left[i] * scale, 0.0)[:, :32])
        right[i] = [part * scale for part in right[i]]
    return upper, right


def factor_kernel(total, high, low, q, upper, weights, result, factor, out_sem, factor_sem):
    pairs = high.shape[0]
    vectors, wide_y = q.shape[0], q.shape[2]
    above, inverse = eliminate(total[...])
    for i in range(4):
        factor[8 * i : 8 * i + 8, :] = above[i]
    store_factor = pltpu.make_async_copy(factor, upper, factor_sem)
    store_factor.start()
    shape = (8, 128)
    row, lane = lax.broadcasted_iota(jnp.int32, shape, 0), lax.broadcasted_iota(jnp.int32, shape, 1)
    same = (lane % 8 == row).astype(jnp.float32)
    for u in range(vectors // 2):
        for h in range(2):
            block = inverse[u // 4][h]
            r = 2 * u % 8
            value = jnp.concatenate([block[r : r + 1, :] * same, block[r + 1 : r + 2, :] * same], axis=0)
            first = value.astype(jnp.bfloat16)
            second = (value - first.astype(jnp.float32)).astype(jnp.bfloat16)
            for place, part in enumerate((first, second, first)):
                weights[16 * u : 16 * u + 16, 256 * place + 128 * h : 256 * place + 128 * h + 128] = part

    def store(n):
        part = pl.ds(2 * n, 2)
        return pltpu.make_async_copy(result.at[:, part], q.at[:, part], out_sem.at[n])

    def pair(n, carry):
        first, second = high[n], low[n]
        value = jnp.dot(
            weights[...], jnp.concatenate([first, first, second], axis=0), preferred_element_type=jnp.float32)
        for part in range(2):
            result[:, 2 * n + part] = value[:, part * 128 : part * 128 + 128].reshape(vectors, wide_y, 128)
        store(n).start()
        return carry

    def done(n, carry):
        store(n).wait()
        return carry

    lax.fori_loop(0, pairs, pair, 0)
    lax.fori_loop(0, pairs, done, 0)
    store_factor.wait()


def on_device(base_state, adjoint_block):
    nx, ny = lax.axis_size("gx"), lax.axis_size("gy")
    vectors, _, wide_x, wide_y, lanes = adjoint_block.shape
    assert (vectors, wide_y, lanes) == (32, 8, 128)
    entries = float(3 * wide_x * wide_y * lanes * nx * ny)
    f32, bf16, dma = jnp.float32, jnp.bfloat16, pltpu.SemaphoreType.DMA
    vmem, anywhere = pl.BlockSpec(memory_space=pltpu.VMEM), pl.BlockSpec(memory_space=pl.ANY)
    planes = 3 * wide_x
    rows = vectors * planes * wide_y
    half = (planes // 2, vectors * wide_y, 256)
    high, low, total = pl.pallas_call(
        functools.partial(step_kernel, nx, ny, entries),
        out_shape=(pltpu.VMEM(half, bf16), pltpu.VMEM(half, bf16), pltpu.VMEM((8, 128), f32)),
        in_specs=[anywhere, anywhere, anywhere],
        out_specs=(vmem, vmem, vmem),
        scratch_shapes=[
            pltpu.VMEM(base_state.shape, f32),
            pltpu.VMEM((rows, 128), f32),
            dma((2,)),
            pltpu.VMEM((2, wide_x, 3, WIDE, 128), f32),
            pltpu.VMEM((2, 3, WIDE, wide_y, 128), f32),
            pltpu.VMEM((2, wide_x, 3, WIDE, 128), f32),
            pltpu.VMEM((2, 2, WIDE, 3, WIDE, 128), f32),
            pltpu.VMEM((3, wide_x + 4, wide_y + 8, 128), f32),
            pltpu.VMEM((3, wide_x + 2, wide_y + 8, 128), f32),
            pltpu.VMEM((15, wide_x, wide_y, 128), f32),
            pltpu.VMEM((3, wide_x + 2, wide_y + 2, vectors, 128), f32),
            pltpu.VMEM((wide_x, 2 * vectors, wide_y * 128), bf16),
            pltpu.VMEM((rows, 128), f32),
            pltpu.VMEM((nx * ny, 8, 128), f32),
            dma((8,)), dma((8,)), dma((3, 4)), dma((3, 4)),
            pltpu.SemaphoreType.REGULAR((len(rounds(nx, ny)),)), dma, dma,
        ],
        compiler_params=pltpu.CompilerParams(
            collective_id=0, has_side_effects=True, vmem_limit_bytes=40 * 1024 * 1024),
    )(base_state, adjoint_block.reshape(rows, 128), adjoint_block.reshape(vectors, 3, wide_x, wide_y, 1, 128))
    high, low, total = (pltpu.with_memory_space_constraint(part, pltpu.VMEM) for part in (high, low, total))
    q_shape = (vectors, planes, wide_y, 128)
    q, upper = pl.pallas_call(
        factor_kernel,
        out_shape=(jax.ShapeDtypeStruct(q_shape, f32), jax.ShapeDtypeStruct((vectors, vectors), f32)),
        in_specs=[vmem, vmem, vmem],
        out_specs=(anywhere, anywhere),
        scratch_shapes=[
            pltpu.VMEM((vectors * wide_y, 768), bf16),
            pltpu.VMEM(q_shape, f32),
            pltpu.VMEM((vectors, vectors), f32),
            dma((planes // 2,)), dma,
        ],
        compiler_params=pltpu.CompilerParams(vmem_limit_bytes=40 * 1024 * 1024),
    )(total, high, low)
    return (q.reshape(adjoint_block.shape), upper)


def solution(mesh):
    in_specs = (P(None, "gx", "gy", None), P(None, None, "gx", "gy", None))
    out_specs = (P(None, None, "gx", "gy", None), P())
    return jax.shard_map(
        on_device, mesh=mesh, in_specs=in_specs, out_specs=out_specs, check_vma=False
    )
```

```python
import functools
import math

import jax
import jax.numpy as jnp
from jax import lax
from jax.experimental import pallas as pl
from jax.experimental.pallas import tpu as pltpu
from jax.sharding import PartitionSpec as P

ADVECT = 0.1
DIFFUSE = 0.08
DRIVE_SCALE = 0.25
WAVENUMBER = 4.0
MESH = pl.DeviceIdType.MESH


WIDE = 2
SIDES = ((-1, 0), (1, 0), (0, -1), (0, 1), (-1, -1), (-1, 1), (1, -1), (1, 1))


def neighbour(nx, ny, dx, dy):
    return (lax.rem(lax.axis_index("gx") + dx + nx, nx), lax.rem(lax.axis_index("gy") + dy + ny, ny))


def meet(nx, ny):
    barrier = pltpu.get_barrier_semaphore()
    for dx, dy in SIDES:
        pl.semaphore_signal(barrier, inc=1, device_id=neighbour(nx, ny, dx, dy), device_id_type=MESH)
    return barrier, len(SIDES)


def rounds(nx, ny):
    steps, reach = [], 1
    while 2 * reach < nx:
        steps.append((reach, 0))
        reach *= 2
    reach = 1
    while 2 * reach < ny:
        steps.append((0, reach))
        reach *= 2
    return steps


def tell(nx, ny, heard, n):
    dx, dy = rounds(nx, ny)[n]
    for sign in (-1, 1):
        pl.semaphore_signal(
            heard.at[n], inc=1, device_id=neighbour(nx, ny, sign * dx, sign * dy), device_id_type=MESH)


def each(low, high, body):
    if high - low <= 64:
        for i in range(low, high):
            body(i)
        return

    def run(i, carry):
        body(i)
        return carry

    lax.fori_loop(low, high, run, 0)


def advance_rows(bext, forcing, x, wide_y):
    rows = wide_y + 2
    centre = [bext[c, x + 1, 1 : 1 + rows, :] for c in range(3)]
    advanced = []
    for c in range(3):
        east, west = bext[c, x + 2, 1 : 1 + rows, :], bext[c, x, 1 : 1 + rows, :]
        north, south = bext[c, x + 1, 2 : 2 + rows, :], bext[c, x + 1, 0:rows, :]
        up, down = pltpu.roll(centre[c], 127, axis=1), pltpu.roll(centre[c], 1, axis=1)
        laplacian = east + west + north + south + up + down - 6.0 * centre[c]
        advection = centre[0] * (east - west) + centre[1] * (north - south) + centre[2] * (up - down)
        value = centre[c] + DIFFUSE * laplacian - ADVECT * advection
        advanced.append(value + forcing if c == 0 else value)
    return advanced


def step_kernel(
    nx, ny, entries, base_in, a_in, rows_in, high, low, total, base, a2, in_sem, edges, bx, by, bc, bext, adv, coef, at,
    split, natural, slots, base_send, base_recv, halo_send, halo_recv, heard, gram_send, gram_recv,
):
    wide_x, wide_y = base.shape[1], base.shape[2]
    vectors = at.shape[3]
    stride = 3 * wide_x * wide_y
    gx, gy = lax.axis_index("gx"), lax.axis_index("gy")
    devices, me = nx * ny, gx * ny + gy
    barrier, met = meet(nx, ny)
    base_load = pltpu.make_async_copy(base_in, base, in_sem.at[0])
    load = pltpu.make_async_copy(a_in, a2, in_sem.at[1])
    base_load.start()
    load.start()

    def move(c):
        def plane_of(x, carry):
            for y in range(wide_y):
                at[c, x + 1, y + 1] = a2[pl.ds((c * wide_x + x) * wide_y + y, vectors, stride=stride), :]
            return carry
        lax.fori_loop(0, wide_x, plane_of, 0)

    def base_copy(i):
        dx, dy = SIDES[i]
        near_x = pl.ds(0, WIDE) if dx < 0 else pl.ds(wide_x - WIDE, WIDE)
        side = 0 if dy < 0 else 1
        if dy == 0:
            src, dst = base.at[:, near_x], bx.at[(1 - dx) // 2]
        elif dx == 0:
            src, dst = edges.at[side], by.at[1 - side]
        else:
            src, dst = edges.at[side, near_x], bc.at[(1 - dx) // 2, 1 - side]
        return pltpu.make_async_remote_copy(
            src, dst, base_send.at[i], base_recv.at[i],
            device_id=neighbour(nx, ny, dx, dy), device_id_type=MESH)

    inner_x, inner_y = pl.ds(1, wide_x), pl.ds(1, wide_y)

    def halo_start(c, i):
        dx, dy = SIDES[i]
        peer = neighbour(nx, ny, dx, dy)
        if dx:
            near, far = (0, wide_x + 1) if dx < 0 else (wide_x - 1, 0)
            pairs = [(rows_in.at[:, c, near, y, 0], at.at[c, far, y + 1]) for y in range(wide_y)]
        else:
            near, far = (0, wide_y + 1) if dy < 0 else (wide_y - 1, 0)
            pairs = [(rows_in.at[:, c, x, near, 0], at.at[c, x + 1, far]) for x in range(wide_x)]
        for src, dst in pairs:
            pltpu.make_async_remote_copy(
                src, dst, halo_send.at[c, i], halo_recv.at[c, i], device_id=peer, device_id_type=MESH).start()

    def halo(c, i):
        dx, dy = SIDES[i]
        if dx:
            whole = at.at[c, wide_x + 1 if dx < 0 else 0, inner_y]
        else:
            whole = at.at[c, inner_x, wide_y + 1 if dy < 0 else 0]
        return pltpu.make_async_remote_copy(
            whole, whole, halo_send.at[c, i], halo_recv.at[c, i],
            device_id=neighbour(nx, ny, dx, dy), device_id_type=MESH)

    base_load.wait()
    for side, start in ((0, 0), (1, wide_y - WIDE)):
        for c in range(3):
            edges[side, :, c] = base[c, :, start : start + WIDE, :]
    pl.semaphore_wait(barrier, met)
    for i in range(8):
        base_copy(i).start()
    for c in range(3):
        for i in range(4):
            halo_start(c, i)
    tells = len(rounds(nx, ny))

    def spread(n):
        if n:
            pl.semaphore_wait(heard.at[n - 1], 2)
        if n < tells:
            tell(nx, ny, heard, n)

    spread(0)
    load.wait()
    for c in range(3):
        move(c)

    for c in range(3):
        bext[c, WIDE : WIDE + wide_x, WIDE : WIDE + wide_y, :] = base[c]
    for i in range(8):
        base_copy(i).wait_recv()
    near, far = WIDE + wide_x, WIDE + wide_y
    for c in range(3):
        for sx, start_x in ((0, 0), (1, near)):
            bext[c, start_x : start_x + WIDE, WIDE:far, :] = bx[sx, c]
            for sy, start_y in ((0, 0), (1, far)):
                bext[c, start_x : start_x + WIDE, start_y : start_y + WIDE, :] = bc[sx, sy, :, c]
        for sy, start_y in ((0, 0), (1, far)):
            bext[c, WIDE:near, start_y : start_y + WIDE, :] = by[sy, :, c]

    ny_total = wide_y * ny
    column = lax.broadcasted_iota(jnp.int32, (wide_y + 2, 128), 0) + (gy * wide_y + ny_total - 1)
    phases = 2.0 * math.pi * WAVENUMBER * lax.rem(column, ny_total).astype(jnp.float32) / float(ny_total)
    forcing = DRIVE_SCALE * jnp.sin(phases)
    for x in range(wide_x + 2):
        for c, value in enumerate(advance_rows(bext, forcing, x, wide_y)):
            adv[c, x, 0 : wide_y + 2, :] = value
    for x in range(wide_x):
        inner = [adv[m, x + 1, 1 : 1 + wide_y, :] for m in range(3)]
        coef[0, x] = ADVECT * adv[0, x + 2, 1 : 1 + wide_y, :] + DIFFUSE
        coef[1, x] = DIFFUSE - ADVECT * adv[0, x, 1 : 1 + wide_y, :]
        coef[2, x] = ADVECT * adv[1, x + 1, 2 : 2 + wide_y, :] + DIFFUSE
        coef[3, x] = DIFFUSE - ADVECT * adv[1, x + 1, 0:wide_y, :]
        coef[4, x] = ADVECT * inner[2] + DIFFUSE
        coef[5, x] = DIFFUSE - ADVECT * inner[2]
        for m in range(3):
            slopes = (
                adv[m, x + 2, 1 : 1 + wide_y, :] - adv[m, x, 1 : 1 + wide_y, :],
                adv[m, x + 1, 2 : 2 + wide_y, :] - adv[m, x + 1, 0:wide_y, :],
                pltpu.roll(inner[m], 127, axis=1) - pltpu.roll(inner[m], 1, axis=1),
            )
            for i in range(3):
                own = 1.0 - 6.0 * DIFFUSE if i == m else 0.0
                coef[6 + 3 * i + m, x] = own - ADVECT * slopes[i]

    spread(1)

    def plane_of(c, x):
        columns = []
        for y in range(wide_y):
            k = [coef[n, x, y : y + 1, :] for n in range(6)]
            k += [coef[6 + 3 * c + m, x, y : y + 1, :] for m in range(3)]
            own = [at[m, x + 1, y + 1] for m in range(3)]
            value = k[0] * at[c, x + 2, y + 1] + k[1] * at[c, x, y + 1]
            value += k[2] * at[c, x + 1, y + 2] + k[3] * at[c, x + 1, y]
            value += pltpu.roll(k[4] * own[c], 127, axis=1) + pltpu.roll(k[5] * own[c], 1, axis=1)
            value += k[6] * own[0] + k[7] * own[1] + k[8] * own[2]
            natural[pl.ds(((c * wide_x + x) * vectors) * wide_y + y, vectors, stride=wide_y), :] = value
            columns.append(value)
        updated = jnp.concatenate(columns, axis=1)
        first = updated.astype(jnp.bfloat16)
        second = (updated - first.astype(jnp.float32)).astype(jnp.bfloat16)
        split[x, 0:vectors, :] = first
        split[x, vectors : 2 * vectors, :] = second

    gram = jnp.zeros((2 * vectors, 2 * vectors), jnp.float32)
    for c in range(3):
        for i in (2, 3):
            halo(c, i).wait_recv()

        def inside(x, carry, c=c):
            plane_of(c, x)
            return carry

        def outside(n, carry, c=c):
            plane_of(c, n * (wide_x - 1))
            return carry

        lax.fori_loop(1, wide_x - 1, inside, 0)
        for i in (0, 1):
            halo(c, i).wait_recv()
        lax.fori_loop(0, 2, outside, 0)
        both = jnp.concatenate([split[x] for x in range(wide_x)], axis=1)
        gram += lax.dot_general(both, both, (((1,), (1,)), ((), ())), preferred_element_type=jnp.float32)
        if c < 2:
            spread(2 + c)
    for n in range(4, tells + 1):
        spread(n)

    gram = gram[:vectors] + gram[vectors:]
    gram = gram[:, :vectors] + gram[:, vectors:]
    slots[me] = jnp.concatenate([gram[8 * i : 8 * i + 8] for i in range(4)], axis=1)

    def give(step):
        there = lax.rem(me + step, devices)
        pltpu.make_async_remote_copy(
            slots.at[me], slots.at[me], gram_send, gram_recv,
            device_id=(there // ny, lax.rem(there, ny)), device_id_type=MESH).start()

    each(1, devices, give)

    def convert(n, carry):
        for part in range(2):
            value = natural[pl.ds(pl.multiple_of((2 * n + part) * vectors * wide_y, 256), vectors * wide_y), :]
            first = value.astype(jnp.bfloat16)
            high[n, :, part * 128 : part * 128 + 128] = first
            low[n, :, part * 128 : part * 128 + 128] = (value - first.astype(jnp.float32)).astype(jnp.bfloat16)
        return carry

    lax.fori_loop(0, high.shape[0], convert, 0)
    others = slots.at[pl.ds(0, devices - 1)]
    gathered = pltpu.make_async_remote_copy(
        others, others, gram_send, gram_recv, device_id=neighbour(nx, ny, 0, 1), device_id_type=MESH)
    gathered.wait_recv()
    if devices <= 64:
        level = [slots[i] for i in range(devices)]
        while len(level) > 1:
            level = [sum(level[i : i + 2][1:], level[i]) for i in range(0, len(level), 2)]
        summed = level[0]
    else:
        summed = lax.fori_loop(1, devices, lambda i, value: value + slots[i], slots[0])
    total[...] = summed / entries
    gathered.wait_send()
    for i in range(8):
        base_copy(i).wait_send()
    for c in range(3):
        for i in range(4):
            halo(c, i).wait_send()


def eliminate(packed):
    shape = packed.shape
    row, lane = lax.broadcasted_iota(jnp.int32, shape, 0), lax.broadcasted_iota(jnp.int32, shape, 1)
    left = [packed] + [pltpu.roll(packed, 128 - 32 * i, axis=1) for i in range(1, 4)]
    right = [[(lane // 8 + 16 * h == row + 8 * i).astype(jnp.float32) for h in range(2)] for i in range(4)]
    pivots = []
    for p in range(4):
        rest = range(p, 4)
        columns = [
            {i: jnp.broadcast_to(left[i][:, k : k + 1], shape) for i in rest} for k in range(8 * p, 8 * p + 8)]
        pivot = jnp.ones(shape, jnp.float32)
        for j in range(8):
            here = columns[j][p][j : j + 1, :]
            pivot = jnp.where(row == j, here, pivot)
            inverse = 1.0 / here
            factor = {i: columns[j][i] * inverse for i in rest}
            factor[p] = jnp.where(row > j, factor[p], 0.0)
            for l in range(j + 1, 8):
                across = columns[l][p][j : j + 1, :]
                for i in rest:
                    columns[l][i] = columns[l][i] - factor[i] * across
            across = left[p][j : j + 1, :]
            for i in rest:
                left[i] = left[i] - factor[i] * across
            for h in range(2 if p >= 2 else 1):
                across = right[p][h][j : j + 1, :]
                for i in rest:
                    right[i][h] = right[i][h] - factor[i] * across
        pivots.append(pivot)
    upper = []
    for i in range(4):
        scale = lax.rsqrt(pivots[i])
        upper.append(jnp.where(lane >= row + 8 * i, left[i] * scale, 0.0)[:, :32])
        right[i] = [part * scale for part in right[i]]
    return upper, right


def factor_kernel(total, high, low, q, upper, weights, result, factor, out_sem, factor_sem):
    pairs = high.shape[0]
    vectors, wide_y = q.shape[0], q.shape[2]
    above, inverse = eliminate(total[...])
    for i in range(4):
        factor[8 * i : 8 * i + 8, :] = above[i]
    store_factor = pltpu.make_async_copy(factor, upper, factor_sem)
    store_factor.start()
    shape = (8, 128)
    row, lane = lax.broadcasted_iota(jnp.int32, shape, 0), lax.broadcasted_iota(jnp.int32, shape, 1)
    same = (lane % 8 == row).astype(jnp.float32)
    for u in range(vectors // 2):
        for h in range(2):
            block = inverse[u // 4][h]
            r = 2 * u % 8
            value = jnp.concatenate([block[r : r + 1, :] * same, block[r + 1 : r + 2, :] * same], axis=0)
            first = value.astype(jnp.bfloat16)
            second = (value - first.astype(jnp.float32)).astype(jnp.bfloat16)
            for place, part in enumerate((first, second, first)):
                weights[16 * u : 16 * u + 16, 256 * place + 128 * h : 256 * place + 128 * h + 128] = part

    def store(n):
        part = pl.ds(2 * n, 2)
        return pltpu.make_async_copy(result.at[:, part], q.at[:, part], out_sem.at[n])

    def pair(n, carry):
        first, second = high[n], low[n]
        value = jnp.dot(
            weights[...], jnp.concatenate([first, first, second], axis=0), preferred_element_type=jnp.float32)
        for part in range(2):
            result[:, 2 * n + part] = value[:, part * 128 : part * 128 + 128].reshape(vectors, wide_y, 128)
        store(n).start()
        return carry

    def done(n, carry):
        store(n).wait()
        return carry

    lax.fori_loop(0, pairs, pair, 0)
    lax.fori_loop(0, pairs, done, 0)
    store_factor.wait()


def on_device(base_state, adjoint_block):
    nx, ny = lax.axis_size("gx"), lax.axis_size("gy")
    vectors, _, wide_x, wide_y, lanes = adjoint_block.shape
    assert (vectors, wide_y, lanes) == (32, 8, 128)
    entries = float(3 * wide_x * wide_y * lanes * nx * ny)
    f32, bf16, dma = jnp.float32, jnp.bfloat16, pltpu.SemaphoreType.DMA
    vmem, anywhere = pl.BlockSpec(memory_space=pltpu.VMEM), pl.BlockSpec(memory_space=pl.ANY)
    planes = 3 * wide_x
    rows = vectors * planes * wide_y
    half = (planes // 2, vectors * wide_y, 256)
    base_state, rows_of, tiles_of = (
        pltpu.with_memory_space_constraint(part, pltpu.HBM)
        for part in (base_state, adjoint_block.reshape(vectors, 3, wide_x, wide_y, 1, 128), adjoint_block.reshape(rows, 128)))
    high, low, total = pl.pallas_call(
        functools.partial(step_kernel, nx, ny, entries),
        out_shape=(pltpu.VMEM(half, bf16), pltpu.VMEM(half, bf16), pltpu.VMEM((8, 128), f32)),
        in_specs=[anywhere, anywhere, anywhere],
        out_specs=(vmem, vmem, vmem),
        scratch_shapes=[
            pltpu.VMEM(base_state.shape, f32),
            pltpu.VMEM((rows, 128), f32),
            dma((2,)),
            pltpu.VMEM((2, wide_x, 3, WIDE, 128), f32),
            pltpu.VMEM((2, 3, WIDE, wide_y, 128), f32),
            pltpu.VMEM((2, wide_x, 3, WIDE, 128), f32),
            pltpu.VMEM((2, 2, WIDE, 3, WIDE, 128), f32),
            pltpu.VMEM((3, wide_x + 4, wide_y + 8, 128), f32),
            pltpu.VMEM((3, wide_x + 2, wide_y + 8, 128), f32),
            pltpu.VMEM((15, wide_x, wide_y, 128), f32),
            pltpu.VMEM((3, wide_x + 2, wide_y + 2, vectors, 128), f32),
            pltpu.VMEM((wide_x, 2 * vectors, wide_y * 128), bf16),
            pltpu.VMEM((rows, 128), f32),
            pltpu.VMEM((nx * ny, 8, 128), f32),
            dma((8,)), dma((8,)), dma((3, 4)), dma((3, 4)),
            pltpu.SemaphoreType.REGULAR((len(rounds(nx, ny)),)), dma, dma,
        ],
        compiler_params=pltpu.CompilerParams(
            collective_id=0, has_side_effects=True, vmem_limit_bytes=40 * 1024 * 1024),
    )(base_state, tiles_of, rows_of)
    high, low, total = (pltpu.with_memory_space_constraint(part, pltpu.VMEM) for part in (high, low, total))
    q_shape = (vectors, planes, wide_y, 128)
    q, upper = pl.pallas_call(
        factor_kernel,
        out_shape=(jax.ShapeDtypeStruct(q_shape, f32), jax.ShapeDtypeStruct((vectors, vectors), f32)),
        in_specs=[vmem, vmem, vmem],
        out_specs=(anywhere, anywhere),
        scratch_shapes=[
            pltpu.VMEM((vectors * wide_y, 768), bf16),
            pltpu.VMEM(q_shape, f32),
            pltpu.VMEM((vectors, vectors), f32),
            dma((planes // 2,)), dma,
        ],
        compiler_params=pltpu.CompilerParams(vmem_limit_bytes=40 * 1024 * 1024),
    )(total, high, low)
    return (q.reshape(adjoint_block.shape), upper)


def solution(mesh):
    in_specs = (P(None, "gx", "gy", None), P(None, None, "gx", "gy", None))
    out_specs = (P(None, None, "gx", "gy", None), P())
    return jax.shard_map(
        on_device, mesh=mesh, in_specs=in_specs, out_specs=out_specs, check_vma=False
    )
```

```python
import functools
import math

import jax
import jax.numpy as jnp
from jax import lax
from jax.experimental import pallas as pl
from jax.experimental.pallas import tpu as pltpu
from jax.sharding import PartitionSpec as P

ADVECT = 0.1
DIFFUSE = 0.08
DRIVE_SCALE = 0.25
WAVENUMBER = 4.0
MESH = pl.DeviceIdType.MESH


WIDE = 2
SIDES = ((-1, 0), (1, 0), (0, -1), (0, 1), (-1, -1), (-1, 1), (1, -1), (1, 1))


def neighbour(nx, ny, dx, dy):
    return (lax.rem(lax.axis_index("gx") + dx + nx, nx), lax.rem(lax.axis_index("gy") + dy + ny, ny))


def facing(nx, ny, role):
    odd = lax.rem(lax.axis_index("gx") if role < 2 else lax.axis_index("gy"), 2)
    up = odd if role % 2 == 0 else 1 - odd
    step = 2 * up - 1
    return (neighbour(nx, ny, step, 0) if role < 2 else neighbour(nx, ny, 0, step)), up


ROLES = (2, 3, 0, 1)


def meet(nx, ny):
    barrier = pltpu.get_barrier_semaphore()
    for role in ROLES:
        pl.semaphore_signal(barrier, inc=1, device_id=facing(nx, ny, role)[0], device_id_type=MESH)
    return barrier, len(ROLES)


@functools.cache
def rounds(nx, ny):
    known = {(0, 0), (1, 0), (nx - 1, 0), (0, 1), (0, ny - 1)}
    steps = []

    def add(dx, dy):
        assert (dx % nx, dy % ny) in known
        steps.append((dx, dy))
        for sign in (-1, 1):
            known.update({((x + sign * dx) % nx, (y + sign * dy) % ny) for x, y in reached})

    for size, unit in ((nx, (1, 0)), (ny, (0, 1))):
        reach = 1
        while 2 * reach < size:
            reached = set(known)
            add(reach * unit[0], reach * unit[1])
            reach *= 2
    while len(known) < nx * ny:
        reached = set(known)
        add(0, 1)
        reached = set(known)
        if len(known) < nx * ny:
            add(1, 0)
    return tuple(steps)


def tell(nx, ny, heard, n):
    dx, dy = rounds(nx, ny)[n]
    for sign in (-1, 1):
        pl.semaphore_signal(
            heard.at[n], inc=1, device_id=neighbour(nx, ny, sign * dx, sign * dy), device_id_type=MESH)


def each(low, high, body):
    if high - low <= 64:
        for i in range(low, high):
            body(i)
        return

    def run(i, carry):
        body(i)
        return carry

    lax.fori_loop(low, high, run, 0)


def advance_rows(bext, forcing, x, wide_y):
    rows = wide_y + 2
    centre = [bext[c, x + 1, 1 : 1 + rows, :] for c in range(3)]
    advanced = []
    for c in range(3):
        east, west = bext[c, x + 2, 1 : 1 + rows, :], bext[c, x, 1 : 1 + rows, :]
        north, south = bext[c, x + 1, 2 : 2 + rows, :], bext[c, x + 1, 0:rows, :]
        up, down = pltpu.roll(centre[c], 127, axis=1), pltpu.roll(centre[c], 1, axis=1)
        laplacian = east + west + north + south + up + down - 6.0 * centre[c]
        advection = centre[0] * (east - west) + centre[1] * (north - south) + centre[2] * (up - down)
        value = centre[c] + DIFFUSE * laplacian - ADVECT * advection
        advanced.append(value + forcing if c == 0 else value)
    return advanced


def step_kernel(
    nx, ny, entries, base_in, a_in, rows_in, high, low, total, base, a2, in_sem, edges, bx, by, bc, bext, adv, coef, at,
    part, inside, outside, natural, slots, base_send, base_recv, halo_send, halo_recv, heard, gram_send, gram_recv,
):
    wide_x, wide_y = base.shape[1], base.shape[2]
    vectors = at.shape[3]
    stride = 3 * wide_x * wide_y
    gx, gy = lax.axis_index("gx"), lax.axis_index("gy")
    devices, me = nx * ny, gx * ny + gy
    base_load = pltpu.make_async_copy(base_in, base, in_sem.at[0])
    load = pltpu.make_async_copy(a_in, a2, in_sem.at[1])
    base_load.start()
    barrier, met = meet(nx, ny)
    load.start()

    def move(c):
        def plane_of(x, carry):
            for y in range(wide_y):
                at[c, x + 1, y + 1] = a2[pl.ds((c * wide_x + x) * wide_y + y, vectors, stride=stride), :]
            return carry
        lax.fori_loop(0, wide_x, plane_of, 0)

    def base_copy(i):
        dx, dy = SIDES[i]
        near_x = pl.ds(0, WIDE) if dx < 0 else pl.ds(wide_x - WIDE, WIDE)
        side = 0 if dy < 0 else 1
        if dy == 0:
            src, dst = base.at[:, near_x], bx.at[(1 - dx) // 2]
        elif dx == 0:
            src, dst = edges.at[side], by.at[1 - side]
        else:
            src, dst = edges.at[side, 0 if dx < 0 else wide_x - 1], bc.at[(1 - dx) // 2, 1 - side]
        return pltpu.make_async_remote_copy(
            src, dst, base_send.at[i], base_recv.at[i],
            device_id=neighbour(nx, ny, dx, dy), device_id_type=MESH)

    inner_x, inner_y = pl.ds(1, wide_x), pl.ds(1, wide_y)

    def halo_start(c, role):
        peer, up = facing(nx, ny, role)
        if role < 2:
            side, near, far = up, up * (wide_x - 1), (1 - up) * (wide_x + 1)
            pairs = [(rows_in.at[:, c, near, y, 0], at.at[c, far, y + 1]) for y in range(wide_y)]
        else:
            side, near, far = 2 + up, up * (wide_y - 1), (1 - up) * (wide_y + 1)
            pairs = [(rows_in.at[:, c, x, near, 0], at.at[c, x + 1, far]) for x in range(wide_x)]
        for src, dst in pairs:
            pltpu.make_async_remote_copy(
                src, dst, halo_send.at[c, side], halo_recv.at[c, side], device_id=peer, device_id_type=MESH).start()

    def halo(c, i):
        dx, dy = SIDES[i]
        if dx:
            whole = at.at[c, wide_x + 1 if dx < 0 else 0, inner_y]
        else:
            whole = at.at[c, inner_x, wide_y + 1 if dy < 0 else 0]
        return pltpu.make_async_remote_copy(
            whole, whole, halo_send.at[c, i], halo_recv.at[c, i],
            device_id=neighbour(nx, ny, dx, dy), device_id_type=MESH)

    tells = len(rounds(nx, ny))

    def spread(n):
        if 0 < n <= tells:
            pl.semaphore_wait(heard.at[n - 1], 2)
        if n < tells:
            tell(nx, ny, heard, n)

    pl.semaphore_wait(barrier, met)
    spread(0)
    halo_start(0, 2)
    halo_start(0, 0)
    base_load.wait()
    for side, start in ((0, 0), (1, wide_y - WIDE)):
        for c in range(3):
            edges[side, :, c] = base[c, :, start : start + WIDE, :]
    for i in range(4):
        base_copy(i).start()
    halo_start(0, 3)
    halo_start(0, 1)
    spread(1)
    for i in range(4, 8):
        base_copy(i).start()
    for c in (1, 2):
        for role in ROLES:
            halo_start(c, role)
    load.wait()
    for c in range(3):
        move(c)
    spread(2)

    for c in range(3):
        bext[c, WIDE : WIDE + wide_x, WIDE : WIDE + wide_y, :] = base[c]
    for i in range(8):
        base_copy(i).wait_recv()
    near, far = WIDE + wide_x, WIDE + wide_y
    for c in range(3):
        for sx, start_x in ((0, 0), (1, near)):
            bext[c, start_x : start_x + WIDE, WIDE:far, :] = bx[sx, c]
            edge_x = WIDE - 1 if sx == 0 else near
            for sy, start_y in ((0, 0), (1, far)):
                bext[c, edge_x, start_y : start_y + WIDE, :] = bc[sx, sy, c]
        for sy, start_y in ((0, 0), (1, far)):
            bext[c, WIDE:near, start_y : start_y + WIDE, :] = by[sy, :, c]

    ny_total = wide_y * ny
    column = lax.broadcasted_iota(jnp.int32, (wide_y + 2, 128), 0) + (gy * wide_y + ny_total - 1)
    phases = 2.0 * math.pi * WAVENUMBER * lax.rem(column, ny_total).astype(jnp.float32) / float(ny_total)
    forcing = DRIVE_SCALE * jnp.sin(phases)
    for x in range(wide_x + 2):
        for c, value in enumerate(advance_rows(bext, forcing, x, wide_y)):
            adv[c, x, 0 : wide_y + 2, :] = value
    for x in range(wide_x):
        inner = [adv[m, x + 1, 1 : 1 + wide_y, :] for m in range(3)]
        coef[0, x] = ADVECT * adv[0, x + 2, 1 : 1 + wide_y, :] + DIFFUSE
        coef[1, x] = DIFFUSE - ADVECT * adv[0, x, 1 : 1 + wide_y, :]
        coef[2, x] = ADVECT * adv[1, x + 1, 2 : 2 + wide_y, :] + DIFFUSE
        coef[3, x] = DIFFUSE - ADVECT * adv[1, x + 1, 0:wide_y, :]
        coef[4, x] = ADVECT * inner[2] + DIFFUSE
        coef[5, x] = DIFFUSE - ADVECT * inner[2]
        for m in range(3):
            slopes = (
                adv[m, x + 2, 1 : 1 + wide_y, :] - adv[m, x, 1 : 1 + wide_y, :],
                adv[m, x + 1, 2 : 2 + wide_y, :] - adv[m, x + 1, 0:wide_y, :],
                pltpu.roll(inner[m], 127, axis=1) - pltpu.roll(inner[m], 1, axis=1),
            )
            for i in range(3):
                own = 1.0 - 6.0 * DIFFUSE if i == m else 0.0
                coef[6 + 3 * i + m, x] = own - ADVECT * slopes[i]

    spread(3)

    def halves(value):
        first = value.astype(jnp.bfloat16)
        return first, (value - first.astype(jnp.float32)).astype(jnp.bfloat16)

    def keep(where, c, place, value):
        lanes = slice(place * 128, place * 128 + 128)
        where[c, 0:vectors, lanes], where[c, vectors : 2 * vectors, lanes] = halves(value)

    def near_terms(c, x, y, west, east, south, north):
        own = [at[m, x + 1, y + 1] for m in range(3)]
        mine = at[c, x + 1, y + 1]
        k = lambda n: coef[n, x, y : y + 1, :]
        value = pltpu.roll(k(4) * mine, 127, axis=1) + pltpu.roll(k(5) * mine, 1, axis=1)
        for m in range(3):
            value += k(6 + 3 * c + m) * own[m]
        if east:
            value += k(0) * at[c, x + 2, y + 1]
        if west:
            value += k(1) * at[c, x, y + 1]
        if north:
            value += k(2) * at[c, x + 1, y + 2]
        if south:
            value += k(3) * at[c, x + 1, y]
        return value

    def row_of(c, x, y):
        return pl.ds((c * wide_x + x) * vectors * wide_y + y, vectors, stride=wide_y)

    def near_part(c, carry):
        for x in range(wide_x):
            for y in range(wide_y):
                value = near_terms(c, x, y, x > 0, x < wide_x - 1, y > 0, y < wide_y - 1)
                if 0 < x < wide_x - 1 and 0 < y < wide_y - 1:
                    natural[row_of(c, x, y), :] = value
                    keep(inside, c, (x - 1) * (wide_y - 2) + y - 1, value)
                else:
                    part[c, x, y] = value
        return carry

    lax.fori_loop(0, 3, near_part, 0)
    spread(4)

    def square(value):
        return lax.dot_general(value, value, (((1,), (1,)), ((), ())), preferred_element_type=jnp.float32)

    gram = square(inside[0]) + square(inside[1]) + square(inside[2])
    border = [(x, y) for x in range(wide_x) for y in range(wide_y)
              if not (0 < x < wide_x - 1 and 0 < y < wide_y - 1)]
    for c in range(3):
        for i in range(4):
            halo(c, i).wait_recv()
        for place, (x, y) in enumerate(border):
            k = lambda n: coef[n, x, y : y + 1, :]
            value = part[c, x, y]
            if x == 0:
                value += k(1) * at[c, 0, y + 1]
            if x == wide_x - 1:
                value += k(0) * at[c, wide_x + 1, y + 1]
            if y == 0:
                value += k(3) * at[c, x + 1, 0]
            if y == wide_y - 1:
                value += k(2) * at[c, x + 1, wide_y + 1]
            part[c, x, y] = value
            keep(outside, c, place, value)
        gram += square(outside[c])
        spread(5 + c)
    for n in range(8, tells + 1):
        spread(n)

    gram = gram[:vectors] + gram[vectors:]
    gram = gram[:, :vectors] + gram[:, vectors:]
    slots[me] = jnp.concatenate([gram[8 * i : 8 * i + 8] for i in range(4)], axis=1)

    def give(step):
        there = lax.rem(me + step, devices)
        pltpu.make_async_remote_copy(
            slots.at[me], slots.at[me], gram_send, gram_recv,
            device_id=(there // ny, lax.rem(there, ny)), device_id_type=MESH).start()

    each(1, devices, give)

    def place_border(c, carry):
        for x, y in border:
            natural[row_of(c, x, y), :] = part[c, x, y]
        return carry

    lax.fori_loop(0, 3, place_border, 0)

    def convert(n, carry):
        for side in range(2):
            value = natural[pl.ds(pl.multiple_of((2 * n + side) * vectors * wide_y, 256), vectors * wide_y), :]
            lanes = slice(side * 128, side * 128 + 128)
            high[n, :, lanes], low[n, :, lanes] = halves(value)
        return carry

    lax.fori_loop(0, high.shape[0], convert, 0)
    others = slots.at[pl.ds(0, devices - 1)]
    gathered = pltpu.make_async_remote_copy(
        others, others, gram_send, gram_recv, device_id=neighbour(nx, ny, 0, 1), device_id_type=MESH)
    gathered.wait_recv()
    if devices <= 64:
        level = [slots[i] for i in range(devices)]
        while len(level) > 1:
            level = [sum(level[i : i + 2][1:], level[i]) for i in range(0, len(level), 2)]
        summed = level[0]
    else:
        summed = lax.fori_loop(1, devices, lambda i, value: value + slots[i], slots[0])
    total[...] = summed / entries
    gathered.wait_send()
    for i in range(8):
        base_copy(i).wait_send()
    for c in range(3):
        for i in range(4):
            halo(c, i).wait_send()


def eliminate(packed):
    shape = packed.shape
    row, lane = lax.broadcasted_iota(jnp.int32, shape, 0), lax.broadcasted_iota(jnp.int32, shape, 1)
    left = [packed] + [pltpu.roll(packed, 128 - 32 * i, axis=1) for i in range(1, 4)]
    right = [[(lane // 8 + 16 * h == row + 8 * i).astype(jnp.float32) for h in range(2)] for i in range(4)]
    pivots = []
    for p in range(4):
        rest = range(p, 4)
        columns = [
            {i: jnp.broadcast_to(left[i][:, k : k + 1], shape) for i in rest} for k in range(8 * p, 8 * p + 8)]
        pivot = jnp.ones(shape, jnp.float32)
        for j in range(8):
            here = columns[j][p][j : j + 1, :]
            pivot = jnp.where(row == j, here, pivot)
            inverse = 1.0 / here
            factor = {i: columns[j][i] * inverse for i in rest}
            factor[p] = jnp.where(row > j, factor[p], 0.0)
            for l in range(j + 1, 8):
                across = columns[l][p][j : j + 1, :]
                for i in rest:
                    columns[l][i] = columns[l][i] - factor[i] * across
            across = left[p][j : j + 1, :]
            for i in rest:
                left[i] = left[i] - factor[i] * across
            for h in range(2 if p >= 2 else 1):
                across = right[p][h][j : j + 1, :]
                for i in rest:
                    right[i][h] = right[i][h] - factor[i] * across
        pivots.append(pivot)
    upper = []
    for i in range(4):
        scale = lax.rsqrt(pivots[i])
        upper.append(jnp.where(lane >= row + 8 * i, left[i] * scale, 0.0)[:, :32])
        right[i] = [part * scale for part in right[i]]
    return upper, right


def factor_kernel(total, high, low, q, upper, weights, result, factor, out_sem, factor_sem):
    pairs = high.shape[0]
    vectors, wide_y = q.shape[0], q.shape[2]
    above, inverse = eliminate(total[...])
    for i in range(4):
        factor[8 * i : 8 * i + 8, :] = above[i]
    store_factor = pltpu.make_async_copy(factor, upper, factor_sem)
    store_factor.start()
    shape = (8, 128)
    row, lane = lax.broadcasted_iota(jnp.int32, shape, 0), lax.broadcasted_iota(jnp.int32, shape, 1)
    same = (lane % 8 == row).astype(jnp.float32)
    for u in range(vectors // 2):
        for h in range(2):
            block = inverse[u // 4][h]
            r = 2 * u % 8
            value = jnp.concatenate([block[r : r + 1, :] * same, block[r + 1 : r + 2, :] * same], axis=0)
            first = value.astype(jnp.bfloat16)
            second = (value - first.astype(jnp.float32)).astype(jnp.bfloat16)
            for place, part in enumerate((first, second, first)):
                weights[16 * u : 16 * u + 16, 256 * place + 128 * h : 256 * place + 128 * h + 128] = part

    def store(n):
        part = pl.ds(2 * n, 2)
        return pltpu.make_async_copy(result.at[:, part], q.at[:, part], out_sem.at[n])

    def pair(n, carry):
        first, second = high[n], low[n]
        value = jnp.dot(
            weights[...], jnp.concatenate([first, first, second], axis=0), preferred_element_type=jnp.float32)
        for part in range(2):
            result[:, 2 * n + part] = value[:, part * 128 : part * 128 + 128].reshape(vectors, wide_y, 128)
        store(n).start()
        return carry

    def done(n, carry):
        store(n).wait()
        return carry

    lax.fori_loop(0, pairs, pair, 0)
    lax.fori_loop(0, pairs, done, 0)
    store_factor.wait()


def on_device(base_state, adjoint_block):
    nx, ny = lax.axis_size("gx"), lax.axis_size("gy")
    vectors, _, wide_x, wide_y, lanes = adjoint_block.shape
    assert (vectors, wide_y, lanes) == (32, 8, 128)
    entries = float(3 * wide_x * wide_y * lanes * nx * ny)
    f32, bf16, dma = jnp.float32, jnp.bfloat16, pltpu.SemaphoreType.DMA
    vmem, anywhere = pl.BlockSpec(memory_space=pltpu.VMEM), pl.BlockSpec(memory_space=pl.ANY)
    planes = 3 * wide_x
    rows = vectors * planes * wide_y
    inner = (wide_x - 2) * (wide_y - 2)
    half = (planes // 2, vectors * wide_y, 256)
    base_state, rows_of, tiles_of = (
        pltpu.with_memory_space_constraint(part, pltpu.HBM)
        for part in (base_state, adjoint_block.reshape(vectors, 3, wide_x, wide_y, 1, 128), adjoint_block.reshape(rows, 128)))
    high, low, total = pl.pallas_call(
        functools.partial(step_kernel, nx, ny, entries),
        out_shape=(pltpu.VMEM(half, bf16), pltpu.VMEM(half, bf16), pltpu.VMEM((8, 128), f32)),
        in_specs=[anywhere, anywhere, anywhere],
        out_specs=(vmem, vmem, vmem),
        scratch_shapes=[
            pltpu.VMEM(base_state.shape, f32),
            pltpu.VMEM((rows, 128), f32),
            dma((2,)),
            pltpu.VMEM((2, wide_x, 3, WIDE, 128), f32),
            pltpu.VMEM((2, 3, WIDE, wide_y, 128), f32),
            pltpu.VMEM((2, wide_x, 3, WIDE, 128), f32),
            pltpu.VMEM((2, 2, 3, WIDE, 128), f32),
            pltpu.VMEM((3, wide_x + 4, wide_y + 8, 128), f32),
            pltpu.VMEM((3, wide_x + 2, wide_y + 8, 128), f32),
            pltpu.VMEM((15, wide_x, wide_y, 128), f32),
            pltpu.VMEM((3, wide_x + 2, wide_y + 2, vectors, 128), f32),
            pltpu.VMEM((3, wide_x, wide_y, vectors, 128), f32),
            pltpu.VMEM((3, 2 * vectors, inner * 128), bf16),
            pltpu.VMEM((3, 2 * vectors, (wide_x * wide_y - inner) * 128), bf16),
            pltpu.VMEM((rows, 128), f32),
            pltpu.VMEM((nx * ny, 8, 128), f32),
            dma((8,)), dma((8,)), dma((3, 4)), dma((3, 4)),
            pltpu.SemaphoreType.REGULAR((len(rounds(nx, ny)),)), dma, dma,
        ],
        compiler_params=pltpu.CompilerParams(
            collective_id=0, has_side_effects=True, vmem_limit_bytes=40 * 1024 * 1024),
    )(base_state, tiles_of, rows_of)
    high, low, total = (pltpu.with_memory_space_constraint(part, pltpu.VMEM) for part in (high, low, total))
    q_shape = (vectors, planes, wide_y, 128)
    q, upper = pl.pallas_call(
        factor_kernel,
        out_shape=(jax.ShapeDtypeStruct(q_shape, f32), jax.ShapeDtypeStruct((vectors, vectors), f32)),
        in_specs=[vmem, vmem, vmem],
        out_specs=(anywhere, anywhere),
        scratch_shapes=[
            pltpu.VMEM((vectors * wide_y, 768), bf16),
            pltpu.VMEM(q_shape, f32),
            pltpu.VMEM((vectors, vectors), f32),
            dma((planes // 2,)), dma,
        ],
        compiler_params=pltpu.CompilerParams(vmem_limit_bytes=40 * 1024 * 1024),
    )(total, high, low)
    return (q.reshape(adjoint_block.shape), upper)


def solution(mesh):
    in_specs = (P(None, "gx", "gy", None), P(None, None, "gx", "gy", None))
    out_specs = (P(None, None, "gx", "gy", None), P())
    return jax.shard_map(
        on_device, mesh=mesh, in_specs=in_specs, out_specs=out_specs, check_vma=False
    )
```

```python
import functools
import math

import jax
import jax.numpy as jnp
from jax import lax
from jax.experimental import pallas as pl
from jax.experimental.pallas import tpu as pltpu
from jax.sharding import PartitionSpec as P

ADVECT = 0.1
DIFFUSE = 0.08
DRIVE_SCALE = 0.25
WAVENUMBER = 4.0
MESH = pl.DeviceIdType.MESH


WIDE = 2
SIDES = ((-1, 0), (1, 0), (0, -1), (0, 1), (-1, -1), (-1, 1), (1, -1), (1, 1))


def neighbour(nx, ny, dx, dy):
    return (lax.rem(lax.axis_index("gx") + dx + nx, nx), lax.rem(lax.axis_index("gy") + dy + ny, ny))


def facing(nx, ny, role):
    odd = lax.rem(lax.axis_index("gx") if role < 2 else lax.axis_index("gy"), 2)
    up = odd if role % 2 == 0 else 1 - odd
    step = 2 * up - 1
    return (neighbour(nx, ny, step, 0) if role < 2 else neighbour(nx, ny, 0, step)), up


ROLES = (2, 3, 0, 1)


def meet(nx, ny):
    barrier = pltpu.get_barrier_semaphore()
    for role in ROLES:
        pl.semaphore_signal(barrier, inc=1, device_id=facing(nx, ny, role)[0], device_id_type=MESH)
    return barrier, len(ROLES)


@functools.cache
def rounds(nx, ny):
    known = {(0, 0), (1, 0), (nx - 1, 0), (0, 1), (0, ny - 1)}
    steps = []

    def add(dx, dy):
        assert (dx % nx, dy % ny) in known
        steps.append((dx, dy))
        for sign in (-1, 1):
            known.update({((x + sign * dx) % nx, (y + sign * dy) % ny) for x, y in reached})

    for size, unit in ((nx, (1, 0)), (ny, (0, 1))):
        reach = 1
        while 2 * reach < size:
            reached = set(known)
            add(reach * unit[0], reach * unit[1])
            reach *= 2
    while len(known) < nx * ny:
        reached = set(known)
        add(0, 1)
        reached = set(known)
        if len(known) < nx * ny:
            add(1, 0)
    return tuple(steps)


def tell(nx, ny, heard, n):
    dx, dy = rounds(nx, ny)[n]
    for sign in (-1, 1):
        pl.semaphore_signal(
            heard.at[n], inc=1, device_id=neighbour(nx, ny, sign * dx, sign * dy), device_id_type=MESH)


def each(low, high, body):
    if high - low <= 64:
        for i in range(low, high):
            body(i)
        return

    def run(i, carry):
        body(i)
        return carry

    lax.fori_loop(low, high, run, 0)


def advance_rows(bext, forcing, x, wide_y):
    rows = wide_y + 2
    centre = [bext[c, x + 1, 1 : 1 + rows, :] for c in range(3)]
    advanced = []
    for c in range(3):
        east, west = bext[c, x + 2, 1 : 1 + rows, :], bext[c, x, 1 : 1 + rows, :]
        north, south = bext[c, x + 1, 2 : 2 + rows, :], bext[c, x + 1, 0:rows, :]
        up, down = pltpu.roll(centre[c], 127, axis=1), pltpu.roll(centre[c], 1, axis=1)
        laplacian = east + west + north + south + up + down - 6.0 * centre[c]
        advection = centre[0] * (east - west) + centre[1] * (north - south) + centre[2] * (up - down)
        value = centre[c] + DIFFUSE * laplacian - ADVECT * advection
        advanced.append(value + forcing if c == 0 else value)
    return advanced


def step_kernel(
    nx, ny, entries, base_in, a_in, rows_in, high, low, total, base, a2, in_sem, edges, bx, by, bc, bext, adv, coef, at,
    part, inside, outside, natural, slots, base_send, base_recv, halo_send, halo_recv, heard, gram_send, gram_recv,
):
    wide_x, wide_y = base.shape[1], base.shape[2]
    vectors = at.shape[3]
    stride = 3 * wide_x * wide_y
    gx, gy = lax.axis_index("gx"), lax.axis_index("gy")
    devices, me = nx * ny, gx * ny + gy
    base_load = pltpu.make_async_copy(base_in, base, in_sem.at[0])
    load = pltpu.make_async_copy(a_in, a2, in_sem.at[1])
    base_load.start()
    barrier, met = meet(nx, ny)
    load.start()

    def move(c):
        def plane_of(x, carry):
            for y in range(wide_y):
                at[c, x + 1, y + 1] = a2[pl.ds((c * wide_x + x) * wide_y + y, vectors, stride=stride), :]
            return carry
        lax.fori_loop(0, wide_x, plane_of, 0)

    def base_copy(i):
        dx, dy = SIDES[i]
        near_x = pl.ds(0, WIDE) if dx < 0 else pl.ds(wide_x - WIDE, WIDE)
        side = 0 if dy < 0 else 1
        if dy == 0:
            src, dst = base.at[:, near_x], bx.at[(1 - dx) // 2]
        elif dx == 0:
            src, dst = edges.at[side], by.at[1 - side]
        else:
            src, dst = edges.at[side, 0 if dx < 0 else wide_x - 1], bc.at[(1 - dx) // 2, 1 - side]
        return pltpu.make_async_remote_copy(
            src, dst, base_send.at[i], base_recv.at[i],
            device_id=neighbour(nx, ny, dx, dy), device_id_type=MESH)

    inner_x, inner_y = pl.ds(1, wide_x), pl.ds(1, wide_y)

    def halo_start(c, role):
        peer, up = facing(nx, ny, role)
        if role < 2:
            side, near, far = up, up * (wide_x - 1), (1 - up) * (wide_x + 1)
            pairs = [(rows_in.at[:, c, near, y, 0], at.at[c, far, y + 1]) for y in range(wide_y)]
        else:
            side, near, far = 2 + up, up * (wide_y - 1), (1 - up) * (wide_y + 1)
            pairs = [(rows_in.at[:, c, x, near, 0], at.at[c, x + 1, far]) for x in range(wide_x)]
        for src, dst in pairs:
            pltpu.make_async_remote_copy(
                src, dst, halo_send.at[c, side], halo_recv.at[c, side], device_id=peer, device_id_type=MESH).start()

    def halo(c, i):
        dx, dy = SIDES[i]
        if dx:
            whole = at.at[c, wide_x + 1 if dx < 0 else 0, inner_y]
        else:
            whole = at.at[c, inner_x, wide_y + 1 if dy < 0 else 0]
        return pltpu.make_async_remote_copy(
            whole, whole, halo_send.at[c, i], halo_recv.at[c, i],
            device_id=neighbour(nx, ny, dx, dy), device_id_type=MESH)

    tells = len(rounds(nx, ny))

    def spread(n):
        if 0 < n <= tells:
            pl.semaphore_wait(heard.at[n - 1], 2)
        if n < tells:
            tell(nx, ny, heard, n)

    pl.semaphore_wait(barrier, met)
    spread(0)
    halo_start(0, 2)
    halo_start(0, 0)
    base_load.wait()
    for side, start in ((0, 0), (1, wide_y - WIDE)):
        for c in range(3):
            edges[side, :, c] = base[c, :, start : start + WIDE, :]
    for i in range(4):
        base_copy(i).start()
    halo_start(0, 3)
    halo_start(0, 1)
    spread(1)
    for i in range(4, 8):
        base_copy(i).start()
    for c in (1, 2):
        for role in ROLES:
            halo_start(c, role)
    load.wait()
    for c in range(3):
        move(c)
    spread(2)

    for c in range(3):
        bext[c, WIDE : WIDE + wide_x, WIDE : WIDE + wide_y, :] = base[c]
    for i in range(8):
        base_copy(i).wait_recv()
    near, far = WIDE + wide_x, WIDE + wide_y
    for c in range(3):
        for sx, start_x in ((0, 0), (1, near)):
            bext[c, start_x : start_x + WIDE, WIDE:far, :] = bx[sx, c]
            edge_x = WIDE - 1 if sx == 0 else near
            for sy, start_y in ((0, 0), (1, far)):
                bext[c, edge_x, start_y : start_y + WIDE, :] = bc[sx, sy, c]
        for sy, start_y in ((0, 0), (1, far)):
            bext[c, WIDE:near, start_y : start_y + WIDE, :] = by[sy, :, c]

    ny_total = wide_y * ny
    column = lax.broadcasted_iota(jnp.int32, (wide_y + 2, 128), 0) + (gy * wide_y + ny_total - 1)
    phases = 2.0 * math.pi * WAVENUMBER * lax.rem(column, ny_total).astype(jnp.float32) / float(ny_total)
    forcing = DRIVE_SCALE * jnp.sin(phases)
    for x in range(wide_x + 2):
        for c, value in enumerate(advance_rows(bext, forcing, x, wide_y)):
            adv[c, x, 0 : wide_y + 2, :] = value
    for x in range(wide_x):
        inner = [adv[m, x + 1, 1 : 1 + wide_y, :] for m in range(3)]
        coef[0, x] = ADVECT * adv[0, x + 2, 1 : 1 + wide_y, :] + DIFFUSE
        coef[1, x] = DIFFUSE - ADVECT * adv[0, x, 1 : 1 + wide_y, :]
        coef[2, x] = ADVECT * adv[1, x + 1, 2 : 2 + wide_y, :] + DIFFUSE
        coef[3, x] = DIFFUSE - ADVECT * adv[1, x + 1, 0:wide_y, :]
        coef[4, x] = ADVECT * inner[2] + DIFFUSE
        coef[5, x] = DIFFUSE - ADVECT * inner[2]
        for m in range(3):
            slopes = (
                adv[m, x + 2, 1 : 1 + wide_y, :] - adv[m, x, 1 : 1 + wide_y, :],
                adv[m, x + 1, 2 : 2 + wide_y, :] - adv[m, x + 1, 0:wide_y, :],
                pltpu.roll(inner[m], 127, axis=1) - pltpu.roll(inner[m], 1, axis=1),
            )
            for i in range(3):
                own = 1.0 - 6.0 * DIFFUSE if i == m else 0.0
                coef[6 + 3 * i + m, x] = own - ADVECT * slopes[i]

    spread(3)

    def halves(value):
        first = value.astype(jnp.bfloat16)
        return first, (value - first.astype(jnp.float32)).astype(jnp.bfloat16)

    def keep(where, c, place, value):
        lanes = slice(place * 128, place * 128 + 128)
        where[c, 0:vectors, lanes], where[c, vectors : 2 * vectors, lanes] = halves(value)

    def near_terms(c, x, y, west, east, south, north):
        own = [at[m, x + 1, y + 1] for m in range(3)]
        mine = at[c, x + 1, y + 1]
        k = lambda n: coef[n, x, y : y + 1, :]
        value = pltpu.roll(k(4) * mine, 127, axis=1) + pltpu.roll(k(5) * mine, 1, axis=1)
        for m in range(3):
            value += k(6 + 3 * c + m) * own[m]
        if east:
            value += k(0) * at[c, x + 2, y + 1]
        if west:
            value += k(1) * at[c, x, y + 1]
        if north:
            value += k(2) * at[c, x + 1, y + 2]
        if south:
            value += k(3) * at[c, x + 1, y]
        return value

    def row_of(c, x, y):
        return pl.ds((c * wide_x + x) * vectors * wide_y + y, vectors, stride=wide_y)

    def near_part(c, carry):
        for x in range(wide_x):
            for y in range(wide_y):
                value = near_terms(c, x, y, x > 0, x < wide_x - 1, y > 0, y < wide_y - 1)
                if 0 < x < wide_x - 1 and 0 < y < wide_y - 1:
                    natural[row_of(c, x, y), :] = value
                    keep(inside, c, (x - 1) * (wide_y - 2) + y - 1, value)
                else:
                    part[c, x, y] = value
        return carry

    lax.fori_loop(0, 3, near_part, 0)
    spread(4)

    def square(value):
        return lax.dot_general(value, value, (((1,), (1,)), ((), ())), preferred_element_type=jnp.float32)

    gram = square(inside[0]) + square(inside[1]) + square(inside[2])
    border = [(x, y) for x in range(wide_x) for y in range(wide_y)
              if not (0 < x < wide_x - 1 and 0 < y < wide_y - 1)]
    for c in range(3):
        for i in range(4):
            halo(c, i).wait_recv()
        for place, (x, y) in enumerate(border):
            k = lambda n: coef[n, x, y : y + 1, :]
            value = part[c, x, y]
            if x == 0:
                value += k(1) * at[c, 0, y + 1]
            if x == wide_x - 1:
                value += k(0) * at[c, wide_x + 1, y + 1]
            if y == 0:
                value += k(3) * at[c, x + 1, 0]
            if y == wide_y - 1:
                value += k(2) * at[c, x + 1, wide_y + 1]
            part[c, x, y] = value
            keep(outside, c, place, value)
        gram += square(outside[c])
        spread(5 + c)
    for n in range(8, tells + 1):
        spread(n)

    gram = gram[:vectors] + gram[vectors:]
    gram = gram[:, :vectors] + gram[:, vectors:]
    slots[me] = jnp.concatenate([gram[8 * i : 8 * i + 8] for i in range(4)], axis=1)

    def give(step):
        there = lax.rem(me + step, devices)
        pltpu.make_async_remote_copy(
            slots.at[me], slots.at[me], gram_send, gram_recv,
            device_id=(there // ny, lax.rem(there, ny)), device_id_type=MESH).start()

    each(1, devices, give)

    def place_border(c, carry):
        for x, y in border:
            natural[row_of(c, x, y), :] = part[c, x, y]
        return carry

    lax.fori_loop(0, 3, place_border, 0)

    def convert(n, carry):
        for side in range(2):
            value = natural[pl.ds(pl.multiple_of((2 * n + side) * vectors * wide_y, 256), vectors * wide_y), :]
            lanes = slice(side * 128, side * 128 + 128)
            high[n, :, lanes], low[n, :, lanes] = halves(value)
        return carry

    lax.fori_loop(0, high.shape[0], convert, 0)
    others = slots.at[pl.ds(0, devices - 1)]
    gathered = pltpu.make_async_remote_copy(
        others, others, gram_send, gram_recv, device_id=neighbour(nx, ny, 0, 1), device_id_type=MESH)
    gathered.wait_recv()
    if devices <= 64:
        level = [slots[i] for i in range(devices)]
        while len(level) > 1:
            level = [sum(level[i : i + 2][1:], level[i]) for i in range(0, len(level), 2)]
        summed = level[0]
    else:
        summed = lax.fori_loop(1, devices, lambda i, value: value + slots[i], slots[0])
    total[...] = summed / entries
    gathered.wait_send()
    for i in range(8):
        base_copy(i).wait_send()
    for c in range(3):
        for i in range(4):
            halo(c, i).wait_send()


def eliminate(packed):
    shape = packed.shape
    row, lane = lax.broadcasted_iota(jnp.int32, shape, 0), lax.broadcasted_iota(jnp.int32, shape, 1)
    left = [packed] + [pltpu.roll(packed, 128 - 32 * i, axis=1) for i in range(1, 4)]
    right = [[(lane // 8 + 16 * h == row + 8 * i).astype(jnp.float32) for h in range(2)] for i in range(4)]
    pivots = []
    for p in range(4):
        rest = range(p, 4)
        columns = [
            {i: jnp.broadcast_to(left[i][:, k : k + 1], shape) for i in rest} for k in range(8 * p, 8 * p + 8)]
        pivot = jnp.ones(shape, jnp.float32)
        for j in range(8):
            here = columns[j][p][j : j + 1, :]
            pivot = jnp.where(row == j, here, pivot)
            inverse = 1.0 / here
            factor = {i: columns[j][i] * inverse for i in rest}
            factor[p] = jnp.where(row > j, factor[p], 0.0)
            for l in range(j + 1, 8):
                across = columns[l][p][j : j + 1, :]
                for i in rest:
                    columns[l][i] = columns[l][i] - factor[i] * across
            across = left[p][j : j + 1, :]
            for i in rest:
                left[i] = left[i] - factor[i] * across
            for h in range(2 if p >= 2 else 1):
                across = right[p][h][j : j + 1, :]
                for i in rest:
                    right[i][h] = right[i][h] - factor[i] * across
        pivots.append(pivot)
    upper = []
    for i in range(4):
        scale = lax.rsqrt(pivots[i])
        upper.append(jnp.where(lane >= row + 8 * i, left[i] * scale, 0.0)[:, :32])
        right[i] = [part * scale for part in right[i]]
    return upper, right


def factor_kernel(total, high, low, q, upper, weights, result, factor, out_sem, factor_sem):
    pairs = high.shape[0]
    vectors, wide_y = q.shape[0], q.shape[2]
    above, inverse = eliminate(total[...])
    for i in range(4):
        factor[8 * i : 8 * i + 8, :] = above[i]
    store_factor = pltpu.make_async_copy(factor, upper, factor_sem)
    store_factor.start()
    shape = (8, 128)
    row, lane = lax.broadcasted_iota(jnp.int32, shape, 0), lax.broadcasted_iota(jnp.int32, shape, 1)
    same = (lane % 8 == row).astype(jnp.float32)
    for u in range(vectors // 2):
        for h in range(2):
            block = inverse[u // 4][h]
            r = 2 * u % 8
            value = jnp.concatenate([block[r : r + 1, :] * same, block[r + 1 : r + 2, :] * same], axis=0)
            first = value.astype(jnp.bfloat16)
            second = (value - first.astype(jnp.float32)).astype(jnp.bfloat16)
            for place, part in enumerate((first, second, first)):
                weights[16 * u : 16 * u + 16, 256 * place + 128 * h : 256 * place + 128 * h + 128] = part

    def store(n):
        part = pl.ds(2 * n, 2)
        return pltpu.make_async_copy(result.at[:, part], q.at[:, part], out_sem.at[n])

    def pair(n, carry):
        first, second = high[n], low[n]
        value = jnp.dot(
            weights[...], jnp.concatenate([first, first, second], axis=0), preferred_element_type=jnp.float32)
        for part in range(2):
            result[:, 2 * n + part] = value[:, part * 128 : part * 128 + 128].reshape(vectors, wide_y, 128)
        store(n).start()
        return carry

    def done(n, carry):
        store(n).wait()
        return carry

    for n in range(pairs):
        pair(n, 0)
    lax.fori_loop(0, pairs, done, 0)
    store_factor.wait()


def on_device(base_state, adjoint_block):
    nx, ny = lax.axis_size("gx"), lax.axis_size("gy")
    vectors, _, wide_x, wide_y, lanes = adjoint_block.shape
    assert (vectors, wide_y, lanes) == (32, 8, 128)
    entries = float(3 * wide_x * wide_y * lanes * nx * ny)
    f32, bf16, dma = jnp.float32, jnp.bfloat16, pltpu.SemaphoreType.DMA
    vmem, anywhere = pl.BlockSpec(memory_space=pltpu.VMEM), pl.BlockSpec(memory_space=pl.ANY)
    planes = 3 * wide_x
    rows = vectors * planes * wide_y
    inner = (wide_x - 2) * (wide_y - 2)
    half = (planes // 2, vectors * wide_y, 256)
    base_state, rows_of, tiles_of = (
        pltpu.with_memory_space_constraint(part, pltpu.HBM)
        for part in (base_state, adjoint_block.reshape(vectors, 3, wide_x, wide_y, 1, 128), adjoint_block.reshape(rows, 128)))
    high, low, total = pl.pallas_call(
        functools.partial(step_kernel, nx, ny, entries),
        out_shape=(pltpu.VMEM(half, bf16), pltpu.VMEM(half, bf16), pltpu.VMEM((8, 128), f32)),
        in_specs=[anywhere, anywhere, anywhere],
        out_specs=(vmem, vmem, vmem),
        scratch_shapes=[
            pltpu.VMEM(base_state.shape, f32),
            pltpu.VMEM((rows, 128), f32),
            dma((2,)),
            pltpu.VMEM((2, wide_x, 3, WIDE, 128), f32),
            pltpu.VMEM((2, 3, WIDE, wide_y, 128), f32),
            pltpu.VMEM((2, wide_x, 3, WIDE, 128), f32),
            pltpu.VMEM((2, 2, 3, WIDE, 128), f32),
            pltpu.VMEM((3, wide_x + 4, wide_y + 8, 128), f32),
            pltpu.VMEM((3, wide_x + 2, wide_y + 8, 128), f32),
            pltpu.VMEM((15, wide_x, wide_y, 128), f32),
            pltpu.VMEM((3, wide_x + 2, wide_y + 2, vectors, 128), f32),
            pltpu.VMEM((3, wide_x, wide_y, vectors, 128), f32),
            pltpu.VMEM((3, 2 * vectors, inner * 128), bf16),
            pltpu.VMEM((3, 2 * vectors, (wide_x * wide_y - inner) * 128), bf16),
            pltpu.VMEM((rows, 128), f32),
            pltpu.VMEM((nx * ny, 8, 128), f32),
            dma((8,)), dma((8,)), dma((3, 4)), dma((3, 4)),
            pltpu.SemaphoreType.REGULAR((len(rounds(nx, ny)),)), dma, dma,
        ],
        compiler_params=pltpu.CompilerParams(
            collective_id=0, has_side_effects=True, vmem_limit_bytes=40 * 1024 * 1024),
    )(base_state, tiles_of, rows_of)
    high, low, total = (pltpu.with_memory_space_constraint(part, pltpu.VMEM) for part in (high, low, total))
    q_shape = (vectors, planes, wide_y, 128)
    q, upper = pl.pallas_call(
        factor_kernel,
        out_shape=(jax.ShapeDtypeStruct(q_shape, f32), jax.ShapeDtypeStruct((vectors, vectors), f32)),
        in_specs=[vmem, vmem, vmem],
        out_specs=(anywhere, anywhere),
        scratch_shapes=[
            pltpu.VMEM((vectors * wide_y, 768), bf16),
            pltpu.VMEM(q_shape, f32),
            pltpu.VMEM((vectors, vectors), f32),
            dma((planes // 2,)), dma,
        ],
        compiler_params=pltpu.CompilerParams(vmem_limit_bytes=40 * 1024 * 1024),
    )(total, high, low)
    return (q.reshape(adjoint_block.shape), upper)


def solution(mesh):
    in_specs = (P(None, "gx", "gy", None), P(None, None, "gx", "gy", None))
    out_specs = (P(None, None, "gx", "gy", None), P())
    return jax.shard_map(
        on_device, mesh=mesh, in_specs=in_specs, out_specs=out_specs, check_vma=False
    )
```

```python
import functools
import math

import jax
import jax.numpy as jnp
from jax import lax
from jax.experimental import pallas as pl
from jax.experimental.pallas import tpu as pltpu
from jax.sharding import PartitionSpec as P

ADVECT = 0.1
DIFFUSE = 0.08
DRIVE_SCALE = 0.25
WAVENUMBER = 4.0
MESH = pl.DeviceIdType.MESH


WIDE = 2
SIDES = ((-1, 0), (1, 0), (0, -1), (0, 1), (-1, -1), (-1, 1), (1, -1), (1, 1))


def neighbour(nx, ny, dx, dy):
    return (lax.rem(lax.axis_index("gx") + dx + nx, nx), lax.rem(lax.axis_index("gy") + dy + ny, ny))


def facing(nx, ny, role):
    odd = lax.rem(lax.axis_index("gx") if role < 2 else lax.axis_index("gy"), 2)
    up = odd if role % 2 == 0 else 1 - odd
    step = 2 * up - 1
    return (neighbour(nx, ny, step, 0) if role < 2 else neighbour(nx, ny, 0, step)), up


ROLES = (2, 3, 0, 1)


def meet(nx, ny):
    barrier = pltpu.get_barrier_semaphore()
    for role in ROLES:
        pl.semaphore_signal(barrier, inc=1, device_id=facing(nx, ny, role)[0], device_id_type=MESH)
    return barrier, len(ROLES)


@functools.cache
def rounds(nx, ny):
    known = {(0, 0), (1, 0), (nx - 1, 0), (0, 1), (0, ny - 1)}
    steps = []

    def add(dx, dy):
        assert (dx % nx, dy % ny) in known
        steps.append((dx, dy))
        for sign in (-1, 1):
            known.update({((x + sign * dx) % nx, (y + sign * dy) % ny) for x, y in reached})

    for size, unit in ((nx, (1, 0)), (ny, (0, 1))):
        reach = 1
        while 2 * reach < size:
            reached = set(known)
            add(reach * unit[0], reach * unit[1])
            reach *= 2
    while len(known) < nx * ny:
        reached = set(known)
        add(0, 1)
        reached = set(known)
        if len(known) < nx * ny:
            add(1, 0)
    return tuple(steps)


def tell(nx, ny, heard, n):
    dx, dy = rounds(nx, ny)[n]
    for sign in (-1, 1):
        pl.semaphore_signal(
            heard.at[n], inc=1, device_id=neighbour(nx, ny, sign * dx, sign * dy), device_id_type=MESH)


def each(low, high, body):
    if high - low <= 64:
        for i in range(low, high):
            body(i)
        return

    def run(i, carry):
        body(i)
        return carry

    lax.fori_loop(low, high, run, 0)


def advance_rows(bext, forcing, x, wide_y):
    rows = wide_y + 2
    centre = [bext[c, x + 1, 1 : 1 + rows, :] for c in range(3)]
    advanced = []
    for c in range(3):
        east, west = bext[c, x + 2, 1 : 1 + rows, :], bext[c, x, 1 : 1 + rows, :]
        north, south = bext[c, x + 1, 2 : 2 + rows, :], bext[c, x + 1, 0:rows, :]
        up, down = pltpu.roll(centre[c], 127, axis=1), pltpu.roll(centre[c], 1, axis=1)
        laplacian = east + west + north + south + up + down - 6.0 * centre[c]
        advection = centre[0] * (east - west) + centre[1] * (north - south) + centre[2] * (up - down)
        value = centre[c] + DIFFUSE * laplacian - ADVECT * advection
        advanced.append(value + forcing if c == 0 else value)
    return advanced


def step_kernel(
    nx, ny, entries, base_in, a_in, rows_in, high, low, total, base, a2, in_sem, edges, tips, bx, by, on_corner, off_corner, bext, adv, coef, at,
    part, inside, outside, natural, slots, base_send, base_recv, halo_send, halo_recv, heard, gram_send, gram_recv,
):
    wide_x, wide_y = base.shape[1], base.shape[2]
    vectors = at.shape[3]
    stride = 3 * wide_x * wide_y
    gx, gy = lax.axis_index("gx"), lax.axis_index("gy")
    devices, me = nx * ny, gx * ny + gy
    base_load = pltpu.make_async_copy(base_in, base, in_sem.at[0])
    load = pltpu.make_async_copy(a_in, a2, in_sem.at[1])
    base_load.start()
    barrier, met = meet(nx, ny)
    load.start()

    def move(c):
        def plane_of(x, carry):
            for y in range(wide_y):
                at[c, x + 1, y + 1] = a2[pl.ds((c * wide_x + x) * wide_y + y, vectors, stride=stride), :]
            return carry
        lax.fori_loop(0, wide_x, plane_of, 0)

    odd = lax.rem(gx, 2)

    def base_copy(i):
        if i < 4:
            dx, dy = SIDES[i]
            near_x = pl.ds(0, WIDE) if dx < 0 else pl.ds(wide_x - WIDE, WIDE)
            side = 0 if dy < 0 else 1
            src, dst = (base.at[:, near_x], bx.at[(1 - dx) // 2]) if dx else (edges.at[side], by.at[1 - side])
            peer = neighbour(nx, ny, dx, dy)
        elif i < 6:
            side = i - 4
            src, dst = tips.at[side, odd], off_corner.at[1 - side]
            peer = neighbour(nx, ny, 2 * odd - 1, 2 * side - 1)
        else:
            side = i - 6
            src, dst = by.at[side, (1 - odd) * (wide_x - 1)], on_corner.at[side]
            peer = neighbour(nx, ny, 1 - 2 * odd, 0)
        return pltpu.make_async_remote_copy(
            src, dst, base_send.at[i], base_recv.at[i], device_id=peer, device_id_type=MESH)

    inner_x, inner_y = pl.ds(1, wide_x), pl.ds(1, wide_y)

    def halo_start(c, role):
        peer, up = facing(nx, ny, role)
        if role < 2:
            side, near, far = up, up * (wide_x - 1), (1 - up) * (wide_x + 1)
            pairs = [(rows_in.at[:, c, near, y, 0], at.at[c, far, y + 1]) for y in range(wide_y)]
        else:
            side, near, far = 2 + up, up * (wide_y - 1), (1 - up) * (wide_y + 1)
            pairs = [(rows_in.at[:, c, x, near, 0], at.at[c, x + 1, far]) for x in range(wide_x)]
        for src, dst in pairs:
            pltpu.make_async_remote_copy(
                src, dst, halo_send.at[c, side], halo_recv.at[c, side], device_id=peer, device_id_type=MESH).start()

    def halo(c, i):
        dx, dy = SIDES[i]
        if dx:
            whole = at.at[c, wide_x + 1 if dx < 0 else 0, inner_y]
        else:
            whole = at.at[c, inner_x, wide_y + 1 if dy < 0 else 0]
        return pltpu.make_async_remote_copy(
            whole, whole, halo_send.at[c, i], halo_recv.at[c, i],
            device_id=neighbour(nx, ny, dx, dy), device_id_type=MESH)

    tells = len(rounds(nx, ny))

    def spread(n):
        if 0 < n <= tells:
            pl.semaphore_wait(heard.at[n - 1], 2)
        if n < tells:
            tell(nx, ny, heard, n)

    pl.semaphore_wait(barrier, met)
    spread(0)
    halo_start(0, 2)
    halo_start(0, 0)
    base_load.wait()
    for side, start in ((0, 0), (1, wide_y - WIDE)):
        for c in range(3):
            edges[side, :, c] = base[c, :, start : start + WIDE, :]
            outer = side * (wide_y - 1)
            for end, x in ((0, 0), (1, wide_x - 1)):
                tips[side, end, c : c + 1] = base[c, x, outer : outer + 1, :]
    for i in range(4):
        base_copy(i).start()
    halo_start(0, 3)
    halo_start(0, 1)
    spread(1)
    for i in (4, 5):
        base_copy(i).start()
    for c in (1, 2):
        for role in ROLES:
            halo_start(c, role)
    load.wait()
    for c in range(3):
        move(c)
    spread(2)

    for c in range(3):
        bext[c, WIDE : WIDE + wide_x, WIDE : WIDE + wide_y, :] = base[c]
    for i in (2, 3):
        base_copy(i).wait_recv()
    for i in (6, 7):
        base_copy(i).start()
    for i in (0, 1, 4, 5):
        base_copy(i).wait_recv()
    near, far = WIDE + wide_x, WIDE + wide_y
    on_x = WIDE - 1 + (1 - odd) * (wide_x + 1)
    off_x = WIDE - 1 + odd * (wide_x + 1)
    for c in range(3):
        for sx, start_x in ((0, 0), (1, near)):
            bext[c, start_x : start_x + WIDE, WIDE:far, :] = bx[sx, c]
        for sy, start_y in ((0, 0), (1, far)):
            bext[c, WIDE:near, start_y : start_y + WIDE, :] = by[sy, :, c]
            close = start_y + (1 - sy) * (WIDE - 1)
            bext[c, off_x, close : close + 1, :] = off_corner[sy, c : c + 1]
    for i in (6, 7):
        base_copy(i).wait_recv()
    for c in range(3):
        for sy, start_y in ((0, 0), (1, far)):
            bext[c, on_x, start_y : start_y + WIDE, :] = on_corner[sy, c]

    ny_total = wide_y * ny
    column = lax.broadcasted_iota(jnp.int32, (wide_y + 2, 128), 0) + (gy * wide_y + ny_total - 1)
    phases = 2.0 * math.pi * WAVENUMBER * lax.rem(column, ny_total).astype(jnp.float32) / float(ny_total)
    forcing = DRIVE_SCALE * jnp.sin(phases)
    for x in range(wide_x + 2):
        for c, value in enumerate(advance_rows(bext, forcing, x, wide_y)):
            adv[c, x, 0 : wide_y + 2, :] = value
    for x in range(wide_x):
        inner = [adv[m, x + 1, 1 : 1 + wide_y, :] for m in range(3)]
        coef[0, x] = ADVECT * adv[0, x + 2, 1 : 1 + wide_y, :] + DIFFUSE
        coef[1, x] = DIFFUSE - ADVECT * adv[0, x, 1 : 1 + wide_y, :]
        coef[2, x] = ADVECT * adv[1, x + 1, 2 : 2 + wide_y, :] + DIFFUSE
        coef[3, x] = DIFFUSE - ADVECT * adv[1, x + 1, 0:wide_y, :]
        coef[4, x] = ADVECT * inner[2] + DIFFUSE
        coef[5, x] = DIFFUSE - ADVECT * inner[2]
        for m in range(3):
            slopes = (
                adv[m, x + 2, 1 : 1 + wide_y, :] - adv[m, x, 1 : 1 + wide_y, :],
                adv[m, x + 1, 2 : 2 + wide_y, :] - adv[m, x + 1, 0:wide_y, :],
                pltpu.roll(inner[m], 127, axis=1) - pltpu.roll(inner[m], 1, axis=1),
            )
            for i in range(3):
                own = 1.0 - 6.0 * DIFFUSE if i == m else 0.0
                coef[6 + 3 * i + m, x] = own - ADVECT * slopes[i]

    spread(3)

    def halves(value):
        first = value.astype(jnp.bfloat16)
        return first, (value - first.astype(jnp.float32)).astype(jnp.bfloat16)

    def keep(where, c, place, value):
        lanes = slice(place * 128, place * 128 + 128)
        where[c, 0:vectors, lanes], where[c, vectors : 2 * vectors, lanes] = halves(value)

    def near_terms(c, x, y, west, east, south, north):
        own = [at[m, x + 1, y + 1] for m in range(3)]
        mine = at[c, x + 1, y + 1]
        k = lambda n: coef[n, x, y : y + 1, :]
        value = pltpu.roll(k(4) * mine, 127, axis=1) + pltpu.roll(k(5) * mine, 1, axis=1)
        for m in range(3):
            value += k(6 + 3 * c + m) * own[m]
        if east:
            value += k(0) * at[c, x + 2, y + 1]
        if west:
            value += k(1) * at[c, x, y + 1]
        if north:
            value += k(2) * at[c, x + 1, y + 2]
        if south:
            value += k(3) * at[c, x + 1, y]
        return value

    def row_of(c, x, y):
        return pl.ds((c * wide_x + x) * vectors * wide_y + y, vectors, stride=wide_y)

    def near_part(c, carry):
        for x in range(wide_x):
            for y in range(wide_y):
                value = near_terms(c, x, y, x > 0, x < wide_x - 1, y > 0, y < wide_y - 1)
                if 0 < x < wide_x - 1 and 0 < y < wide_y - 1:
                    natural[row_of(c, x, y), :] = value
                    keep(inside, c, (x - 1) * (wide_y - 2) + y - 1, value)
                else:
                    part[c, x, y] = value
        return carry

    lax.fori_loop(0, 3, near_part, 0)
    spread(4)

    def square(value):
        return lax.dot_general(value, value, (((1,), (1,)), ((), ())), preferred_element_type=jnp.float32)

    gram = square(inside[0]) + square(inside[1]) + square(inside[2])
    border = [(x, y) for x in range(wide_x) for y in range(wide_y)
              if not (0 < x < wide_x - 1 and 0 < y < wide_y - 1)]
    for c in range(3):
        for i in range(4):
            halo(c, i).wait_recv()
        for place, (x, y) in enumerate(border):
            k = lambda n: coef[n, x, y : y + 1, :]
            value = part[c, x, y]
            if x == 0:
                value += k(1) * at[c, 0, y + 1]
            if x == wide_x - 1:
                value += k(0) * at[c, wide_x + 1, y + 1]
            if y == 0:
                value += k(3) * at[c, x + 1, 0]
            if y == wide_y - 1:
                value += k(2) * at[c, x + 1, wide_y + 1]
            part[c, x, y] = value
            keep(outside, c, place, value)
        gram += square(outside[c])
        spread(5 + c)
    for n in range(8, tells + 1):
        spread(n)

    gram = gram[:vectors] + gram[vectors:]
    gram = gram[:, :vectors] + gram[:, vectors:]
    slots[me] = jnp.concatenate([gram[8 * i : 8 * i + 8] for i in range(4)], axis=1)

    def give(step):
        there = lax.rem(me + step, devices)
        pltpu.make_async_remote_copy(
            slots.at[me], slots.at[me], gram_send, gram_recv,
            device_id=(there // ny, lax.rem(there, ny)), device_id_type=MESH).start()

    each(1, devices, give)

    def place_border(c, carry):
        for x, y in border:
            natural[row_of(c, x, y), :] = part[c, x, y]
        return carry

    lax.fori_loop(0, 3, place_border, 0)

    def convert(n, carry):
        for side in range(2):
            value = natural[pl.ds(pl.multiple_of((2 * n + side) * vectors * wide_y, 256), vectors * wide_y), :]
            lanes = slice(side * 128, side * 128 + 128)
            high[n, :, lanes], low[n, :, lanes] = halves(value)
        return carry

    lax.fori_loop(0, high.shape[0], convert, 0)
    others = slots.at[pl.ds(0, devices - 1)]
    gathered = pltpu.make_async_remote_copy(
        others, others, gram_send, gram_recv, device_id=neighbour(nx, ny, 0, 1), device_id_type=MESH)
    gathered.wait_recv()
    if devices <= 64:
        level = [slots[i] for i in range(devices)]
        while len(level) > 1:
            level = [sum(level[i : i + 2][1:], level[i]) for i in range(0, len(level), 2)]
        summed = level[0]
    else:
        summed = lax.fori_loop(1, devices, lambda i, value: value + slots[i], slots[0])
    total[...] = summed / entries
    gathered.wait_send()
    for i in range(8):
        base_copy(i).wait_send()
    for c in range(3):
        for i in range(4):
            halo(c, i).wait_send()


def eliminate(packed):
    shape = packed.shape
    row, lane = lax.broadcasted_iota(jnp.int32, shape, 0), lax.broadcasted_iota(jnp.int32, shape, 1)
    left = [packed] + [pltpu.roll(packed, 128 - 32 * i, axis=1) for i in range(1, 4)]
    right = [[(lane // 8 + 16 * h == row + 8 * i).astype(jnp.float32) for h in range(2)] for i in range(4)]
    pivots = []
    for p in range(4):
        rest = range(p, 4)
        columns = [
            {i: jnp.broadcast_to(left[i][:, k : k + 1], shape) for i in rest} for k in range(8 * p, 8 * p + 8)]
        pivot = jnp.ones(shape, jnp.float32)
        for j in range(8):
            here = columns[j][p][j : j + 1, :]
            pivot = jnp.where(row == j, here, pivot)
            inverse = 1.0 / here
            factor = {i: columns[j][i] * inverse for i in rest}
            factor[p] = jnp.where(row > j, factor[p], 0.0)
            for l in range(j + 1, 8):
                across = columns[l][p][j : j + 1, :]
                for i in rest:
                    columns[l][i] = columns[l][i] - factor[i] * across
            across = left[p][j : j + 1, :]
            for i in rest:
                left[i] = left[i] - factor[i] * across
            for h in range(2 if p >= 2 else 1):
                across = right[p][h][j : j + 1, :]
                for i in rest:
                    right[i][h] = right[i][h] - factor[i] * across
        pivots.append(pivot)
    upper = []
    for i in range(4):
        scale = lax.rsqrt(pivots[i])
        upper.append(jnp.where(lane >= row + 8 * i, left[i] * scale, 0.0)[:, :32])
        right[i] = [part * scale for part in right[i]]
    return upper, right


def factor_kernel(total, high, low, q, upper, weights, result, factor, out_sem, factor_sem):
    pairs = high.shape[0]
    vectors, wide_y = q.shape[0], q.shape[2]
    above, inverse = eliminate(total[...])
    for i in range(4):
        factor[8 * i : 8 * i + 8, :] = above[i]
    store_factor = pltpu.make_async_copy(factor, upper, factor_sem)
    store_factor.start()
    shape = (8, 128)
    row, lane = lax.broadcasted_iota(jnp.int32, shape, 0), lax.broadcasted_iota(jnp.int32, shape, 1)
    same = (lane % 8 == row).astype(jnp.float32)
    for u in range(vectors // 2):
        for h in range(2):
            block = inverse[u // 4][h]
            r = 2 * u % 8
            value = jnp.concatenate([block[r : r + 1, :] * same, block[r + 1 : r + 2, :] * same], axis=0)
            first = value.astype(jnp.bfloat16)
            second = (value - first.astype(jnp.float32)).astype(jnp.bfloat16)
            for place, part in enumerate((first, second, first)):
                weights[16 * u : 16 * u + 16, 256 * place + 128 * h : 256 * place + 128 * h + 128] = part

    def store(n):
        part = pl.ds(2 * n, 2)
        return pltpu.make_async_copy(result.at[:, part], q.at[:, part], out_sem.at[n])

    def pair(n, carry):
        first, second = high[n], low[n]
        value = jnp.dot(
            weights[...], jnp.concatenate([first, first, second], axis=0), preferred_element_type=jnp.float32)
        for part in range(2):
            result[:, 2 * n + part] = value[:, part * 128 : part * 128 + 128].reshape(vectors, wide_y, 128)
        store(n).start()
        return carry

    def done(n, carry):
        store(n).wait()
        return carry

    for n in range(pairs):
        pair(n, 0)
    lax.fori_loop(0, pairs, done, 0)
    store_factor.wait()


def on_device(base_state, adjoint_block):
    nx, ny = lax.axis_size("gx"), lax.axis_size("gy")
    vectors, _, wide_x, wide_y, lanes = adjoint_block.shape
    assert (vectors, wide_y, lanes) == (32, 8, 128)
    entries = float(3 * wide_x * wide_y * lanes * nx * ny)
    f32, bf16, dma = jnp.float32, jnp.bfloat16, pltpu.SemaphoreType.DMA
    vmem, anywhere = pl.BlockSpec(memory_space=pltpu.VMEM), pl.BlockSpec(memory_space=pl.ANY)
    planes = 3 * wide_x
    rows = vectors * planes * wide_y
    inner = (wide_x - 2) * (wide_y - 2)
    half = (planes // 2, vectors * wide_y, 256)
    base_state, rows_of, tiles_of = (
        pltpu.with_memory_space_constraint(part, pltpu.HBM)
        for part in (base_state, adjoint_block.reshape(vectors, 3, wide_x, wide_y, 1, 128), adjoint_block.reshape(rows, 128)))
    high, low, total = pl.pallas_call(
        functools.partial(step_kernel, nx, ny, entries),
        out_shape=(pltpu.VMEM(half, bf16), pltpu.VMEM(half, bf16), pltpu.VMEM((8, 128), f32)),
        in_specs=[anywhere, anywhere, anywhere],
        out_specs=(vmem, vmem, vmem),
        scratch_shapes=[
            pltpu.VMEM(base_state.shape, f32),
            pltpu.VMEM((rows, 128), f32),
            dma((2,)),
            pltpu.VMEM((2, wide_x, 3, WIDE, 128), f32),
            pltpu.VMEM((2, 2, 3, 128), f32),
            pltpu.VMEM((2, 3, WIDE, wide_y, 128), f32),
            pltpu.VMEM((2, wide_x, 3, WIDE, 128), f32),
            pltpu.VMEM((2, 3, WIDE, 128), f32),
            pltpu.VMEM((2, 3, 128), f32),
            pltpu.VMEM((3, wide_x + 4, wide_y + 8, 128), f32),
            pltpu.VMEM((3, wide_x + 2, wide_y + 8, 128), f32),
            pltpu.VMEM((15, wide_x, wide_y, 128), f32),
            pltpu.VMEM((3, wide_x + 2, wide_y + 2, vectors, 128), f32),
            pltpu.VMEM((3, wide_x, wide_y, vectors, 128), f32),
            pltpu.VMEM((3, 2 * vectors, inner * 128), bf16),
            pltpu.VMEM((3, 2 * vectors, (wide_x * wide_y - inner) * 128), bf16),
            pltpu.VMEM((rows, 128), f32),
            pltpu.VMEM((nx * ny, 8, 128), f32),
            dma((8,)), dma((8,)), dma((3, 4)), dma((3, 4)),
            pltpu.SemaphoreType.REGULAR((len(rounds(nx, ny)),)), dma, dma,
        ],
        compiler_params=pltpu.CompilerParams(
            collective_id=0, has_side_effects=True, vmem_limit_bytes=40 * 1024 * 1024),
    )(base_state, tiles_of, rows_of)
    high, low, total = (pltpu.with_memory_space_constraint(part, pltpu.VMEM) for part in (high, low, total))
    q_shape = (vectors, planes, wide_y, 128)
    q, upper = pl.pallas_call(
        factor_kernel,
        out_shape=(jax.ShapeDtypeStruct(q_shape, f32), jax.ShapeDtypeStruct((vectors, vectors), f32)),
        in_specs=[vmem, vmem, vmem],
        out_specs=(anywhere, anywhere),
        scratch_shapes=[
            pltpu.VMEM((vectors * wide_y, 768), bf16),
            pltpu.VMEM(q_shape, f32),
            pltpu.VMEM((vectors, vectors), f32),
            dma((planes // 2,)), dma,
        ],
        compiler_params=pltpu.CompilerParams(vmem_limit_bytes=40 * 1024 * 1024),
    )(total, high, low)
    return (q.reshape(adjoint_block.shape), upper)


def solution(mesh):
    in_specs = (P(None, "gx", "gy", None), P(None, None, "gx", "gy", None))
    out_specs = (P(None, None, "gx", "gy", None), P())
    return jax.shard_map(
        on_device, mesh=mesh, in_specs=in_specs, out_specs=out_specs, check_vma=False
    )
```

```python
import functools
import math

import jax
import jax.numpy as jnp
from jax import lax
from jax.experimental import pallas as pl
from jax.experimental.pallas import tpu as pltpu
from jax.sharding import PartitionSpec as P

ADVECT = 0.1
DIFFUSE = 0.08
DRIVE_SCALE = 0.25
WAVENUMBER = 4.0
MESH = pl.DeviceIdType.MESH


WIDE = 2
SIDES = ((-1, 0), (1, 0), (0, -1), (0, 1), (-1, -1), (-1, 1), (1, -1), (1, 1))


def neighbour(nx, ny, dx, dy):
    return (lax.rem(lax.axis_index("gx") + dx + nx, nx), lax.rem(lax.axis_index("gy") + dy + ny, ny))


def facing(nx, ny, role):
    odd = lax.rem(lax.axis_index("gx") if role < 2 else lax.axis_index("gy"), 2)
    up = odd if role % 2 == 0 else 1 - odd
    step = 2 * up - 1
    return (neighbour(nx, ny, step, 0) if role < 2 else neighbour(nx, ny, 0, step)), up


ROLES = (2, 3, 0, 1)


def meet(nx, ny):
    barrier = pltpu.get_barrier_semaphore()
    for role in ROLES:
        pl.semaphore_signal(barrier, inc=1, device_id=facing(nx, ny, role)[0], device_id_type=MESH)
    return barrier, len(ROLES)


@functools.cache
def rounds(nx, ny):
    known = {(0, 0), (1, 0), (nx - 1, 0), (0, 1), (0, ny - 1)}
    steps = []

    def add(dx, dy):
        assert (dx % nx, dy % ny) in known
        steps.append((dx, dy))
        for sign in (-1, 1):
            known.update({((x + sign * dx) % nx, (y + sign * dy) % ny) for x, y in reached})

    for size, unit in ((nx, (1, 0)), (ny, (0, 1))):
        reach = 1
        while 2 * reach < size:
            reached = set(known)
            add(reach * unit[0], reach * unit[1])
            reach *= 2
    while len(known) < nx * ny:
        reached = set(known)
        add(0, 1)
        reached = set(known)
        if len(known) < nx * ny:
            add(1, 0)
    return tuple(steps)


def tell(nx, ny, heard, n):
    dx, dy = rounds(nx, ny)[n]
    for sign in (-1, 1):
        pl.semaphore_signal(
            heard.at[n], inc=1, device_id=neighbour(nx, ny, sign * dx, sign * dy), device_id_type=MESH)


def each(low, high, body):
    if high - low <= 64:
        for i in range(low, high):
            body(i)
        return

    def run(i, carry):
        body(i)
        return carry

    lax.fori_loop(low, high, run, 0)


def advance_rows(bext, forcing, x, wide_y):
    rows = wide_y + 2
    centre = [bext[c, x + 1, 1 : 1 + rows, :] for c in range(3)]
    advanced = []
    for c in range(3):
        east, west = bext[c, x + 2, 1 : 1 + rows, :], bext[c, x, 1 : 1 + rows, :]
        north, south = bext[c, x + 1, 2 : 2 + rows, :], bext[c, x + 1, 0:rows, :]
        up, down = pltpu.roll(centre[c], 127, axis=1), pltpu.roll(centre[c], 1, axis=1)
        laplacian = east + west + north + south + up + down - 6.0 * centre[c]
        advection = centre[0] * (east - west) + centre[1] * (north - south) + centre[2] * (up - down)
        value = centre[c] + DIFFUSE * laplacian - ADVECT * advection
        advanced.append(value + forcing if c == 0 else value)
    return advanced


def step_kernel(
    nx, ny, entries, base_in, a_in, rows_in, high, low, total, base, a2, in_sem, edges, tips, bx, by, on_corner, off_corner, bext, adv, coef, at,
    part, inside, outside, natural, slots, base_send, base_recv, halo_send, halo_recv, heard, gram_send, gram_recv,
):
    wide_x, wide_y = base.shape[1], base.shape[2]
    vectors = at.shape[3]
    stride = 3 * wide_x * wide_y
    gx, gy = lax.axis_index("gx"), lax.axis_index("gy")
    devices, me = nx * ny, gx * ny + gy
    base_load = pltpu.make_async_copy(base_in, base, in_sem.at[0])
    load = pltpu.make_async_copy(a_in, a2, in_sem.at[1])
    base_load.start()
    barrier, met = meet(nx, ny)
    load.start()

    def move(c):
        def plane_of(x, carry):
            for y in range(wide_y):
                at[c, x + 1, y + 1] = a2[pl.ds((c * wide_x + x) * wide_y + y, vectors, stride=stride), :]
            return carry
        lax.fori_loop(0, wide_x, plane_of, 0)

    odd = lax.rem(gx, 2)

    def base_copy(i):
        if i < 4:
            dx, dy = SIDES[i]
            near_x = pl.ds(0, WIDE) if dx < 0 else pl.ds(wide_x - WIDE, WIDE)
            side = 0 if dy < 0 else 1
            src, dst = (base.at[:, near_x], bx.at[(1 - dx) // 2]) if dx else (edges.at[side], by.at[1 - side])
            peer = neighbour(nx, ny, dx, dy)
        elif i < 6:
            side = i - 4
            src, dst = tips.at[side, odd], off_corner.at[1 - side]
            peer = neighbour(nx, ny, 2 * odd - 1, 2 * side - 1)
        else:
            side = i - 6
            src, dst = by.at[side, (1 - odd) * (wide_x - 1)], on_corner.at[side]
            peer = neighbour(nx, ny, 1 - 2 * odd, 0)
        return pltpu.make_async_remote_copy(
            src, dst, base_send.at[i], base_recv.at[i], device_id=peer, device_id_type=MESH)

    inner_x, inner_y = pl.ds(1, wide_x), pl.ds(1, wide_y)

    def halo_start(c, role):
        peer, up = facing(nx, ny, role)
        if role < 2:
            side, near, far = up, up * (wide_x - 1), (1 - up) * (wide_x + 1)
            pairs = [(rows_in.at[:, c, near, y, 0], at.at[c, far, y + 1]) for y in range(wide_y)]
        else:
            side, near, far = 2 + up, up * (wide_y - 1), (1 - up) * (wide_y + 1)
            pairs = [(rows_in.at[:, c, x, near, 0], at.at[c, x + 1, far]) for x in range(wide_x)]
        for src, dst in pairs:
            pltpu.make_async_remote_copy(
                src, dst, halo_send.at[c, side], halo_recv.at[c, side], device_id=peer, device_id_type=MESH).start()

    def halo(c, i):
        dx, dy = SIDES[i]
        if dx:
            whole = at.at[c, wide_x + 1 if dx < 0 else 0, inner_y]
        else:
            whole = at.at[c, inner_x, wide_y + 1 if dy < 0 else 0]
        return pltpu.make_async_remote_copy(
            whole, whole, halo_send.at[c, i], halo_recv.at[c, i],
            device_id=neighbour(nx, ny, dx, dy), device_id_type=MESH)

    tells = len(rounds(nx, ny))

    def spread(n):
        if 0 < n <= tells:
            pl.semaphore_wait(heard.at[n - 1], 2)
        if n < tells:
            tell(nx, ny, heard, n)

    pl.semaphore_wait(barrier, met)
    spread(0)
    halo_start(0, 2)
    halo_start(0, 0)
    base_load.wait()
    for side, start in ((0, 0), (1, wide_y - WIDE)):
        for c in range(3):
            edges[side, :, c] = base[c, :, start : start + WIDE, :]
            outer = side * (wide_y - 1)
            for end, x in ((0, 0), (1, wide_x - 1)):
                tips[side, end, c : c + 1] = base[c, x, outer : outer + 1, :]
    for i in range(4):
        base_copy(i).start()
    halo_start(0, 3)
    halo_start(0, 1)
    spread(1)
    for i in (4, 5):
        base_copy(i).start()
    for c in (1, 2):
        for role in ROLES:
            halo_start(c, role)
    load.wait()
    for c in range(3):
        move(c)
    spread(2)

    for c in range(3):
        bext[c, WIDE : WIDE + wide_x, WIDE : WIDE + wide_y, :] = base[c]
    for i in (2, 3):
        base_copy(i).wait_recv()
    for i in (6, 7):
        base_copy(i).start()
    for i in (0, 1, 4, 5):
        base_copy(i).wait_recv()
    near, far = WIDE + wide_x, WIDE + wide_y
    on_x = WIDE - 1 + (1 - odd) * (wide_x + 1)
    off_x = WIDE - 1 + odd * (wide_x + 1)
    for c in range(3):
        for sx, start_x in ((0, 0), (1, near)):
            bext[c, start_x : start_x + WIDE, WIDE:far, :] = bx[sx, c]
        for sy, start_y in ((0, 0), (1, far)):
            bext[c, WIDE:near, start_y : start_y + WIDE, :] = by[sy, :, c]
            close = start_y + (1 - sy) * (WIDE - 1)
            bext[c, off_x, close : close + 1, :] = off_corner[sy, c : c + 1]
    for i in (6, 7):
        base_copy(i).wait_recv()
    for c in range(3):
        for sy, start_y in ((0, 0), (1, far)):
            bext[c, on_x, start_y : start_y + WIDE, :] = on_corner[sy, c]

    ny_total = wide_y * ny
    column = lax.broadcasted_iota(jnp.int32, (wide_y + 2, 128), 0) + (gy * wide_y + ny_total - 1)
    phases = 2.0 * math.pi * WAVENUMBER * lax.rem(column, ny_total).astype(jnp.float32) / float(ny_total)
    forcing = DRIVE_SCALE * jnp.sin(phases)
    for x in range(wide_x + 2):
        for c, value in enumerate(advance_rows(bext, forcing, x, wide_y)):
            adv[c, x, 0 : wide_y + 2, :] = value
    for x in range(wide_x):
        inner = [adv[m, x + 1, 1 : 1 + wide_y, :] for m in range(3)]
        coef[0, x] = ADVECT * adv[0, x + 2, 1 : 1 + wide_y, :] + DIFFUSE
        coef[1, x] = DIFFUSE - ADVECT * adv[0, x, 1 : 1 + wide_y, :]
        coef[2, x] = ADVECT * adv[1, x + 1, 2 : 2 + wide_y, :] + DIFFUSE
        coef[3, x] = DIFFUSE - ADVECT * adv[1, x + 1, 0:wide_y, :]
        coef[4, x] = ADVECT * inner[2] + DIFFUSE
        coef[5, x] = DIFFUSE - ADVECT * inner[2]
        for m in range(3):
            slopes = (
                adv[m, x + 2, 1 : 1 + wide_y, :] - adv[m, x, 1 : 1 + wide_y, :],
                adv[m, x + 1, 2 : 2 + wide_y, :] - adv[m, x + 1, 0:wide_y, :],
                pltpu.roll(inner[m], 127, axis=1) - pltpu.roll(inner[m], 1, axis=1),
            )
            for i in range(3):
                own = 1.0 - 6.0 * DIFFUSE if i == m else 0.0
                coef[6 + 3 * i + m, x] = own - ADVECT * slopes[i]

    spread(3)

    def halves(value):
        first = value.astype(jnp.bfloat16)
        return first, (value - first.astype(jnp.float32)).astype(jnp.bfloat16)

    def keep(where, c, place, value):
        lanes = slice(place * 128, place * 128 + 128)
        where[c, 0:vectors, lanes], where[c, vectors : 2 * vectors, lanes] = halves(value)

    def near_terms(c, x, y, west, east, south, north):
        own = [at[m, x + 1, y + 1] for m in range(3)]
        mine = at[c, x + 1, y + 1]
        k = lambda n: coef[n, x, y : y + 1, :]
        value = pltpu.roll(k(4) * mine, 127, axis=1) + pltpu.roll(k(5) * mine, 1, axis=1)
        for m in range(3):
            value += k(6 + 3 * c + m) * own[m]
        if east:
            value += k(0) * at[c, x + 2, y + 1]
        if west:
            value += k(1) * at[c, x, y + 1]
        if north:
            value += k(2) * at[c, x + 1, y + 2]
        if south:
            value += k(3) * at[c, x + 1, y]
        return value

    def row_of(c, x, y):
        return pl.ds((c * wide_x + x) * vectors * wide_y + y, vectors, stride=wide_y)

    def near_part(c, carry):
        for x in range(wide_x):
            for y in range(wide_y):
                value = near_terms(c, x, y, x > 0, x < wide_x - 1, y > 0, y < wide_y - 1)
                if 0 < x < wide_x - 1 and 0 < y < wide_y - 1:
                    natural[row_of(c, x, y), :] = value
                    keep(inside, c, (x - 1) * (wide_y - 2) + y - 1, value)
                else:
                    part[c, x, y] = value
        return carry

    lax.fori_loop(0, 3, near_part, 0)
    spread(4)

    def square(value):
        return lax.dot_general(value, value, (((1,), (1,)), ((), ())), preferred_element_type=jnp.float32)

    gram = square(inside[0]) + square(inside[1]) + square(inside[2])
    border = [(x, y) for x in range(wide_x) for y in range(wide_y)
              if not (0 < x < wide_x - 1 and 0 < y < wide_y - 1)]
    for c in range(3):
        for i in range(4):
            halo(c, i).wait_recv()
        for place, (x, y) in enumerate(border):
            k = lambda n: coef[n, x, y : y + 1, :]
            value = part[c, x, y]
            if x == 0:
                value += k(1) * at[c, 0, y + 1]
            if x == wide_x - 1:
                value += k(0) * at[c, wide_x + 1, y + 1]
            if y == 0:
                value += k(3) * at[c, x + 1, 0]
            if y == wide_y - 1:
                value += k(2) * at[c, x + 1, wide_y + 1]
            part[c, x, y] = value
            keep(outside, c, place, value)
        gram += square(outside[c])
        spread(5 + c)
    for n in range(8, tells + 1):
        spread(n)

    gram = gram[:vectors] + gram[vectors:]
    gram = gram[:, :vectors] + gram[:, vectors:]
    slots[me] = jnp.concatenate([gram[8 * i : 8 * i + 8] for i in range(4)], axis=1)

    def give(step):
        there = lax.rem(me + step, devices)
        pltpu.make_async_remote_copy(
            slots.at[me], slots.at[me], gram_send, gram_recv,
            device_id=(there // ny, lax.rem(there, ny)), device_id_type=MESH).start()

    each(1, devices, give)

    def place_border(c, carry):
        for x, y in border:
            natural[row_of(c, x, y), :] = part[c, x, y]
        return carry

    lax.fori_loop(0, 3, place_border, 0)

    def convert(n, carry):
        for side in range(2):
            value = natural[pl.ds(pl.multiple_of((2 * n + side) * vectors * wide_y, 256), vectors * wide_y), :]
            lanes = slice(side * 128, side * 128 + 128)
            high[n, :, lanes], low[n, :, lanes] = halves(value)
        return carry

    lax.fori_loop(0, high.shape[0], convert, 0)
    others = slots.at[pl.ds(0, devices - 1)]
    gathered = pltpu.make_async_remote_copy(
        others, others, gram_send, gram_recv, device_id=neighbour(nx, ny, 0, 1), device_id_type=MESH)
    gathered.wait_recv()
    if devices <= 64:
        level = [slots[i] for i in range(devices)]
        while len(level) > 1:
            level = [sum(level[i : i + 2][1:], level[i]) for i in range(0, len(level), 2)]
        summed = level[0]
    else:
        summed = lax.fori_loop(1, devices, lambda i, value: value + slots[i], slots[0])
    total[...] = summed / entries
    gathered.wait_send()
    for i in range(8):
        base_copy(i).wait_send()
    for c in range(3):
        for i in range(4):
            halo(c, i).wait_send()


def eliminate(packed):
    shape = packed.shape
    row, lane = lax.broadcasted_iota(jnp.int32, shape, 0), lax.broadcasted_iota(jnp.int32, shape, 1)
    left = [packed] + [pltpu.roll(packed, 128 - 32 * i, axis=1) for i in range(1, 4)]
    right = [[(lane // 8 + 16 * h == row + 8 * i).astype(jnp.float32) for h in range(2)] for i in range(4)]
    pivots = []
    for p in range(4):
        rest = range(p, 4)
        columns = [
            {i: jnp.broadcast_to(left[i][:, k : k + 1], shape) for i in rest} for k in range(8 * p, 8 * p + 8)]
        pivot = jnp.ones(shape, jnp.float32)
        for j in range(8):
            here = columns[j][p][j : j + 1, :]
            pivot = jnp.where(row == j, here, pivot)
            inverse = 1.0 / here
            columns[j][p] = jnp.where(row > j, columns[j][p], 0.0)
            factor = {i: columns[j][i] * inverse for i in rest}
            for l in range(j + 1, 8):
                across = columns[l][p][j : j + 1, :]
                for i in rest:
                    columns[l][i] = columns[l][i] - factor[i] * across
            across = left[p][j : j + 1, :]
            for i in rest:
                left[i] = left[i] - factor[i] * across
            for h in range(2 if p >= 2 else 1):
                across = right[p][h][j : j + 1, :]
                for i in rest:
                    right[i][h] = right[i][h] - factor[i] * across
        pivots.append(pivot)
    upper = []
    for i in range(4):
        scale = lax.rsqrt(pivots[i])
        upper.append(jnp.where(lane >= row + 8 * i, left[i] * scale, 0.0)[:, :32])
        right[i] = [part * scale for part in right[i]]
    return upper, right


def factor_kernel(total, high, low, q, upper, upon, under, result, factor, out_sem, factor_sem):
    pairs = high.shape[0]
    vectors, wide_y = q.shape[0], q.shape[2]
    above, inverse = eliminate(total[...])
    for i in range(4):
        factor[8 * i : 8 * i + 8, :] = above[i]
    store_factor = pltpu.make_async_copy(factor, upper, factor_sem)
    store_factor.start()
    shape = (8, 128)
    row, lane = lax.broadcasted_iota(jnp.int32, shape, 0), lax.broadcasted_iota(jnp.int32, shape, 1)
    same = (lane % 8 == row).astype(jnp.float32)
    for u in range(vectors // 2):
        below = u >= vectors // 4
        for h in range(2 if below else 1):
            block = inverse[u // 4][h]
            r = 2 * u % 8
            value = jnp.concatenate([block[r : r + 1, :] * same, block[r + 1 : r + 2, :] * same], axis=0)
            first = value.astype(jnp.bfloat16)
            second = (value - first.astype(jnp.float32)).astype(jnp.bfloat16)
            for place, part in enumerate((first, second, first)):
                if below:
                    under[16 * u - 128 : 16 * u - 112, 256 * place + 128 * h : 256 * place + 128 * h + 128] = part
                else:
                    upon[16 * u : 16 * u + 16, 128 * place : 128 * place + 128] = part

    def store(n, side):
        part, some = pl.ds(2 * n, 2), pl.ds(side * (vectors // 2), vectors // 2)
        return pltpu.make_async_copy(result.at[some, part], q.at[some, part], out_sem.at[n, side])

    def pair(n, carry):
        first, second = high[n], low[n]
        for side in range(2):
            if side:
                value = jnp.dot(
                    under[...], jnp.concatenate([first, first, second], axis=0), preferred_element_type=jnp.float32)
            else:
                value = jnp.dot(
                    upon[...], jnp.concatenate([first[:128], first[:128], second[:128]], axis=0),
                    preferred_element_type=jnp.float32)
            for part in range(2):
                result[side * 16 : side * 16 + 16, 2 * n + part] = (
                    value[:, part * 128 : part * 128 + 128].reshape(vectors // 2, wide_y, 128))
            store(n, side).start()
        return carry

    def done(n, carry):
        store(n, 0).wait()
        store(n, 1).wait()
        return carry

    for n in range(pairs):
        pair(n, 0)
    lax.fori_loop(0, pairs, done, 0)
    store_factor.wait()


def on_device(base_state, adjoint_block):
    nx, ny = lax.axis_size("gx"), lax.axis_size("gy")
    vectors, _, wide_x, wide_y, lanes = adjoint_block.shape
    assert (vectors, wide_y, lanes) == (32, 8, 128)
    entries = float(3 * wide_x * wide_y * lanes * nx * ny)
    f32, bf16, dma = jnp.float32, jnp.bfloat16, pltpu.SemaphoreType.DMA
    vmem, anywhere = pl.BlockSpec(memory_space=pltpu.VMEM), pl.BlockSpec(memory_space=pl.ANY)
    planes = 3 * wide_x
    rows = vectors * planes * wide_y
    inner = (wide_x - 2) * (wide_y - 2)
    half = (planes // 2, vectors * wide_y, 256)
    base_state, rows_of, tiles_of = (
        pltpu.with_memory_space_constraint(part, pltpu.HBM)
        for part in (base_state, adjoint_block.reshape(vectors, 3, wide_x, wide_y, 1, 128), adjoint_block.reshape(rows, 128)))
    high, low, total = pl.pallas_call(
        functools.partial(step_kernel, nx, ny, entries),
        out_shape=(pltpu.VMEM(half, bf16), pltpu.VMEM(half, bf16), pltpu.VMEM((8, 128), f32)),
        in_specs=[anywhere, anywhere, anywhere],
        out_specs=(vmem, vmem, vmem),
        scratch_shapes=[
            pltpu.VMEM(base_state.shape, f32),
            pltpu.VMEM((rows, 128), f32),
            dma((2,)),
            pltpu.VMEM((2, wide_x, 3, WIDE, 128), f32),
            pltpu.VMEM((2, 2, 3, 128), f32),
            pltpu.VMEM((2, 3, WIDE, wide_y, 128), f32),
            pltpu.VMEM((2, wide_x, 3, WIDE, 128), f32),
            pltpu.VMEM((2, 3, WIDE, 128), f32),
            pltpu.VMEM((2, 3, 128), f32),
            pltpu.VMEM((3, wide_x + 4, wide_y + 8, 128), f32),
            pltpu.VMEM((3, wide_x + 2, wide_y + 8, 128), f32),
            pltpu.VMEM((15, wide_x, wide_y, 128), f32),
            pltpu.VMEM((3, wide_x + 2, wide_y + 2, vectors, 128), f32),
            pltpu.VMEM((3, wide_x, wide_y, vectors, 128), f32),
            pltpu.VMEM((3, 2 * vectors, inner * 128), bf16),
            pltpu.VMEM((3, 2 * vectors, (wide_x * wide_y - inner) * 128), bf16),
            pltpu.VMEM((rows, 128), f32),
            pltpu.VMEM((nx * ny, 8, 128), f32),
            dma((8,)), dma((8,)), dma((3, 4)), dma((3, 4)),
            pltpu.SemaphoreType.REGULAR((len(rounds(nx, ny)),)), dma, dma,
        ],
        compiler_params=pltpu.CompilerParams(
            collective_id=0, has_side_effects=True, vmem_limit_bytes=40 * 1024 * 1024),
    )(base_state, tiles_of, rows_of)
    high, low, total = (pltpu.with_memory_space_constraint(part, pltpu.VMEM) for part in (high, low, total))
    q_shape = (vectors, planes, wide_y, 128)
    q, upper = pl.pallas_call(
        factor_kernel,
        out_shape=(jax.ShapeDtypeStruct(q_shape, f32), jax.ShapeDtypeStruct((vectors, vectors), f32)),
        in_specs=[vmem, vmem, vmem],
        out_specs=(anywhere, anywhere),
        scratch_shapes=[
            pltpu.VMEM((vectors * wide_y // 2, 384), bf16),
            pltpu.VMEM((vectors * wide_y // 2, 768), bf16),
            pltpu.VMEM(q_shape, f32),
            pltpu.VMEM((vectors, vectors), f32),
            dma((planes // 2, 2)), dma,
        ],
        compiler_params=pltpu.CompilerParams(vmem_limit_bytes=40 * 1024 * 1024),
    )(total, high, low)
    return (q.reshape(adjoint_block.shape), upper)


def solution(mesh):
    in_specs = (P(None, "gx", "gy", None), P(None, None, "gx", "gy", None))
    out_specs = (P(None, None, "gx", "gy", None), P())
    return jax.shard_map(
        on_device, mesh=mesh, in_specs=in_specs, out_specs=out_specs, check_vma=False
    )
```

```python
import functools
import math

import jax
import jax.numpy as jnp
from jax import lax
from jax.experimental import pallas as pl
from jax.experimental.pallas import tpu as pltpu
from jax.sharding import PartitionSpec as P

ADVECT = 0.1
DIFFUSE = 0.08
DRIVE_SCALE = 0.25
WAVENUMBER = 4.0
MESH = pl.DeviceIdType.MESH


WIDE = 2
SIDES = ((-1, 0), (1, 0), (0, -1), (0, 1), (-1, -1), (-1, 1), (1, -1), (1, 1))


def neighbour(nx, ny, dx, dy):
    return (lax.rem(lax.axis_index("gx") + dx + nx, nx), lax.rem(lax.axis_index("gy") + dy + ny, ny))


def facing(nx, ny, role):
    odd = lax.rem(lax.axis_index("gx") if role < 2 else lax.axis_index("gy"), 2)
    up = odd if role % 2 == 0 else 1 - odd
    step = 2 * up - 1
    return (neighbour(nx, ny, step, 0) if role < 2 else neighbour(nx, ny, 0, step)), up


ROLES = (2, 3, 0, 1)


def meet(nx, ny):
    barrier = pltpu.get_barrier_semaphore()
    for role in ROLES:
        pl.semaphore_signal(barrier, inc=1, device_id=facing(nx, ny, role)[0], device_id_type=MESH)
    return barrier, len(ROLES)


@functools.cache
def rounds(nx, ny):
    known = {(0, 0), (1, 0), (nx - 1, 0), (0, 1), (0, ny - 1)}
    steps = []

    def add(dx, dy):
        assert (dx % nx, dy % ny) in known
        steps.append((dx, dy))
        for sign in (-1, 1):
            known.update({((x + sign * dx) % nx, (y + sign * dy) % ny) for x, y in reached})

    for size, unit in ((nx, (1, 0)), (ny, (0, 1))):
        reach = 1
        while 2 * reach < size:
            reached = set(known)
            add(reach * unit[0], reach * unit[1])
            reach *= 2
    while len(known) < nx * ny:
        reached = set(known)
        add(0, 1)
        reached = set(known)
        if len(known) < nx * ny:
            add(1, 0)
    return tuple(steps)


def tell(nx, ny, heard, n):
    dx, dy = rounds(nx, ny)[n]
    for sign in (-1, 1):
        pl.semaphore_signal(
            heard.at[n], inc=1, device_id=neighbour(nx, ny, sign * dx, sign * dy), device_id_type=MESH)


def each(low, high, body):
    if high - low <= 64:
        for i in range(low, high):
            body(i)
        return

    def run(i, carry):
        body(i)
        return carry

    lax.fori_loop(low, high, run, 0)


def advance_rows(bext, forcing, x, wide_y):
    rows = wide_y + 2
    centre = [bext[c, x + 1, 1 : 1 + rows, :] for c in range(3)]
    advanced = []
    for c in range(3):
        east, west = bext[c, x + 2, 1 : 1 + rows, :], bext[c, x, 1 : 1 + rows, :]
        north, south = bext[c, x + 1, 2 : 2 + rows, :], bext[c, x + 1, 0:rows, :]
        up, down = pltpu.roll(centre[c], 127, axis=1), pltpu.roll(centre[c], 1, axis=1)
        laplacian = east + west + north + south + up + down - 6.0 * centre[c]
        advection = centre[0] * (east - west) + centre[1] * (north - south) + centre[2] * (up - down)
        value = centre[c] + DIFFUSE * laplacian - ADVECT * advection
        advanced.append(value + forcing if c == 0 else value)
    return advanced


def step_kernel(
    nx, ny, entries, base_in, a_in, rows_in, high, low, total, base, a2, in_sem, edges, tips, bx, by, on_corner, off_corner, bext, adv, coef, at,
    part, inside, outside, natural, slots, base_send, base_recv, halo_send, halo_recv, heard, gram_send, gram_recv,
):
    wide_x, wide_y = base.shape[1], base.shape[2]
    vectors = at.shape[3]
    stride = 3 * wide_x * wide_y
    gx, gy = lax.axis_index("gx"), lax.axis_index("gy")
    devices, me = nx * ny, gx * ny + gy
    base_load = pltpu.make_async_copy(base_in, base, in_sem.at[0])
    load = pltpu.make_async_copy(a_in, a2, in_sem.at[1])
    base_load.start()
    barrier, met = meet(nx, ny)
    load.start()

    def move(c):
        def plane_of(x, carry):
            for y in range(wide_y):
                at[c, x + 1, y + 1] = a2[pl.ds((c * wide_x + x) * wide_y + y, vectors, stride=stride), :]
            return carry
        lax.fori_loop(0, wide_x, plane_of, 0)

    odd = lax.rem(gx, 2)

    def base_copy(i):
        if i < 4:
            dx, dy = SIDES[i]
            near_x = pl.ds(0, WIDE) if dx < 0 else pl.ds(wide_x - WIDE, WIDE)
            side = 0 if dy < 0 else 1
            src, dst = (base.at[:, near_x], bx.at[(1 - dx) // 2]) if dx else (edges.at[side], by.at[1 - side])
            peer = neighbour(nx, ny, dx, dy)
        elif i < 6:
            side = i - 4
            src, dst = tips.at[side, odd], off_corner.at[1 - side]
            peer = neighbour(nx, ny, 2 * odd - 1, 2 * side - 1)
        else:
            side = i - 6
            src, dst = by.at[side, (1 - odd) * (wide_x - 1)], on_corner.at[side]
            peer = neighbour(nx, ny, 1 - 2 * odd, 0)
        return pltpu.make_async_remote_copy(
            src, dst, base_send.at[i], base_recv.at[i], device_id=peer, device_id_type=MESH)

    inner_x, inner_y = pl.ds(1, wide_x), pl.ds(1, wide_y)

    def halo_start(c, role):
        peer, up = facing(nx, ny, role)
        if role < 2:
            side, near, far = up, up * (wide_x - 1), (1 - up) * (wide_x + 1)
            pairs = [(rows_in.at[:, c, near, y, 0], at.at[c, far, y + 1]) for y in range(wide_y)]
        else:
            side, near, far = 2 + up, up * (wide_y - 1), (1 - up) * (wide_y + 1)
            pairs = [(rows_in.at[:, c, x, near, 0], at.at[c, x + 1, far]) for x in range(wide_x)]
        for src, dst in pairs:
            pltpu.make_async_remote_copy(
                src, dst, halo_send.at[c, side], halo_recv.at[c, side], device_id=peer, device_id_type=MESH).start()

    def halo(c, i):
        dx, dy = SIDES[i]
        if dx:
            whole = at.at[c, wide_x + 1 if dx < 0 else 0, inner_y]
        else:
            whole = at.at[c, inner_x, wide_y + 1 if dy < 0 else 0]
        return pltpu.make_async_remote_copy(
            whole, whole, halo_send.at[c, i], halo_recv.at[c, i],
            device_id=neighbour(nx, ny, dx, dy), device_id_type=MESH)

    tells = len(rounds(nx, ny))

    def spread(n):
        if 0 < n <= tells:
            pl.semaphore_wait(heard.at[n - 1], 2)
        if n < tells:
            tell(nx, ny, heard, n)

    pl.semaphore_wait(barrier, met)
    spread(0)
    halo_start(0, 2)
    halo_start(0, 0)
    base_load.wait()
    for side, start in ((0, 0), (1, wide_y - WIDE)):
        for c in range(3):
            edges[side, :, c] = base[c, :, start : start + WIDE, :]
            outer = side * (wide_y - 1)
            for end, x in ((0, 0), (1, wide_x - 1)):
                tips[side, end, c : c + 1] = base[c, x, outer : outer + 1, :]
    for i in range(4):
        base_copy(i).start()
    halo_start(0, 3)
    halo_start(0, 1)
    spread(1)
    for i in (4, 5):
        base_copy(i).start()
    for c in (1, 2):
        for role in ROLES:
            halo_start(c, role)
    load.wait()
    for c in range(3):
        move(c)
    spread(2)

    for c in range(3):
        bext[c, WIDE : WIDE + wide_x, WIDE : WIDE + wide_y, :] = base[c]
    for i in (2, 3):
        base_copy(i).wait_recv()
    for i in (6, 7):
        base_copy(i).start()
    for i in (0, 1, 4, 5):
        base_copy(i).wait_recv()
    near, far = WIDE + wide_x, WIDE + wide_y
    on_x = WIDE - 1 + (1 - odd) * (wide_x + 1)
    off_x = WIDE - 1 + odd * (wide_x + 1)
    for c in range(3):
        for sx, start_x in ((0, 0), (1, near)):
            bext[c, start_x : start_x + WIDE, WIDE:far, :] = bx[sx, c]
        for sy, start_y in ((0, 0), (1, far)):
            bext[c, WIDE:near, start_y : start_y + WIDE, :] = by[sy, :, c]
            close = start_y + (1 - sy) * (WIDE - 1)
            bext[c, off_x, close : close + 1, :] = off_corner[sy, c : c + 1]
    for i in (6, 7):
        base_copy(i).wait_recv()
    for c in range(3):
        for sy, start_y in ((0, 0), (1, far)):
            bext[c, on_x, start_y : start_y + WIDE, :] = on_corner[sy, c]

    ny_total = wide_y * ny
    column = lax.broadcasted_iota(jnp.int32, (wide_y + 2, 128), 0) + (gy * wide_y + ny_total - 1)
    phases = 2.0 * math.pi * WAVENUMBER * lax.rem(column, ny_total).astype(jnp.float32) / float(ny_total)
    forcing = DRIVE_SCALE * jnp.sin(phases)
    for x in range(wide_x + 2):
        for c, value in enumerate(advance_rows(bext, forcing, x, wide_y)):
            adv[c, x, 0 : wide_y + 2, :] = value
    for x in range(wide_x):
        inner = [adv[m, x + 1, 1 : 1 + wide_y, :] for m in range(3)]
        coef[0, x] = ADVECT * adv[0, x + 2, 1 : 1 + wide_y, :] + DIFFUSE
        coef[1, x] = DIFFUSE - ADVECT * adv[0, x, 1 : 1 + wide_y, :]
        coef[2, x] = ADVECT * adv[1, x + 1, 2 : 2 + wide_y, :] + DIFFUSE
        coef[3, x] = DIFFUSE - ADVECT * adv[1, x + 1, 0:wide_y, :]
        coef[4, x] = ADVECT * inner[2] + DIFFUSE
        coef[5, x] = DIFFUSE - ADVECT * inner[2]
        for m in range(3):
            slopes = (
                adv[m, x + 2, 1 : 1 + wide_y, :] - adv[m, x, 1 : 1 + wide_y, :],
                adv[m, x + 1, 2 : 2 + wide_y, :] - adv[m, x + 1, 0:wide_y, :],
                pltpu.roll(inner[m], 127, axis=1) - pltpu.roll(inner[m], 1, axis=1),
            )
            for i in range(3):
                own = 1.0 - 6.0 * DIFFUSE if i == m else 0.0
                coef[6 + 3 * i + m, x] = own - ADVECT * slopes[i]

    spread(3)

    def halves(value):
        first = value.astype(jnp.bfloat16)
        return first, (value - first.astype(jnp.float32)).astype(jnp.bfloat16)

    def keep(where, c, place, value):
        lanes = slice(place * 128, place * 128 + 128)
        where[c, 0:vectors, lanes], where[c, vectors : 2 * vectors, lanes] = halves(value)

    def near_terms(c, x, y, west, east, south, north):
        own = [at[m, x + 1, y + 1] for m in range(3)]
        mine = at[c, x + 1, y + 1]
        k = lambda n: coef[n, x, y : y + 1, :]
        value = pltpu.roll(k(4) * mine, 127, axis=1) + pltpu.roll(k(5) * mine, 1, axis=1)
        for m in range(3):
            value += k(6 + 3 * c + m) * own[m]
        if east:
            value += k(0) * at[c, x + 2, y + 1]
        if west:
            value += k(1) * at[c, x, y + 1]
        if north:
            value += k(2) * at[c, x + 1, y + 2]
        if south:
            value += k(3) * at[c, x + 1, y]
        return value

    def row_of(c, x, y):
        return pl.ds((c * wide_x + x) * vectors * wide_y + y, vectors, stride=wide_y)

    def near_part(c, carry):
        for x in range(wide_x):
            for y in range(wide_y):
                value = near_terms(c, x, y, x > 0, x < wide_x - 1, y > 0, y < wide_y - 1)
                if 0 < x < wide_x - 1 and 0 < y < wide_y - 1:
                    natural[row_of(c, x, y), :] = value
                    keep(inside, c, (x - 1) * (wide_y - 2) + y - 1, value)
                else:
                    part[c, x, y] = value
        return carry

    lax.fori_loop(0, 3, near_part, 0)
    spread(4)

    def square(value):
        return lax.dot_general(value, value, (((1,), (1,)), ((), ())), preferred_element_type=jnp.float32)

    gram = square(inside[0]) + square(inside[1]) + square(inside[2])
    border = [(x, y) for x in range(wide_x) for y in range(wide_y)
              if not (0 < x < wide_x - 1 and 0 < y < wide_y - 1)]
    for c in range(3):
        for i in range(4):
            halo(c, i).wait_recv()
        for place, (x, y) in enumerate(border):
            k = lambda n: coef[n, x, y : y + 1, :]
            value = part[c, x, y]
            if x == 0:
                value += k(1) * at[c, 0, y + 1]
            if x == wide_x - 1:
                value += k(0) * at[c, wide_x + 1, y + 1]
            if y == 0:
                value += k(3) * at[c, x + 1, 0]
            if y == wide_y - 1:
                value += k(2) * at[c, x + 1, wide_y + 1]
            part[c, x, y] = value
            keep(outside, c, place, value)
        gram += square(outside[c])
        spread(5 + c)
    for n in range(8, tells + 1):
        spread(n)

    gram = gram[:vectors] + gram[vectors:]
    gram = gram[:, :vectors] + gram[:, vectors:]
    slots[me] = jnp.concatenate([gram[8 * i : 8 * i + 8] for i in range(4)], axis=1)

    def give(step):
        there = lax.rem(me + step, devices)
        pltpu.make_async_remote_copy(
            slots.at[me], slots.at[me], gram_send, gram_recv,
            device_id=(there // ny, lax.rem(there, ny)), device_id_type=MESH).start()

    each(1, devices, give)

    def place_border(c, carry):
        for x, y in border:
            natural[row_of(c, x, y), :] = part[c, x, y]
        return carry

    lax.fori_loop(0, 3, place_border, 0)

    def convert(n, carry):
        for side in range(2):
            value = natural[pl.ds(pl.multiple_of((2 * n + side) * vectors * wide_y, 256), vectors * wide_y), :]
            lanes = slice(side * 128, side * 128 + 128)
            high[n, :, lanes], low[n, :, lanes] = halves(value)
        return carry

    lax.fori_loop(0, high.shape[0], convert, 0)
    others = slots.at[pl.ds(0, devices - 1)]
    gathered = pltpu.make_async_remote_copy(
        others, others, gram_send, gram_recv, device_id=neighbour(nx, ny, 0, 1), device_id_type=MESH)
    gathered.wait_recv()
    if devices <= 64:
        level = [slots[i] for i in range(devices)]
        while len(level) > 1:
            level = [sum(level[i : i + 2][1:], level[i]) for i in range(0, len(level), 2)]
        summed = level[0]
    else:
        summed = lax.fori_loop(1, devices, lambda i, value: value + slots[i], slots[0])
    total[...] = summed / entries
    gathered.wait_send()
    for i in range(8):
        base_copy(i).wait_send()
    for c in range(3):
        for i in range(4):
            halo(c, i).wait_send()


def eliminate(packed):
    shape = packed.shape
    row, lane = lax.broadcasted_iota(jnp.int32, shape, 0), lax.broadcasted_iota(jnp.int32, shape, 1)
    left = [packed] + [pltpu.roll(packed, 128 - 32 * i, axis=1) for i in range(1, 4)]
    right = [[(lane // 8 + 16 * h == row + 8 * i).astype(jnp.float32) for h in range(2)] for i in range(4)]
    pivots = []
    for p in range(4):
        rest = range(p, 4)
        columns = [
            {i: jnp.broadcast_to(left[i][:, k : k + 1], shape) for i in rest} for k in range(8 * p, 8 * p + 8)]
        pivot = jnp.ones(shape, jnp.float32)
        for j in range(8):
            here = columns[j][p][j : j + 1, :]
            pivot = jnp.where(row == j, here, pivot)
            inverse = 1.0 / here
            columns[j][p] = jnp.where(row > j, columns[j][p], 0.0)
            factor = {i: columns[j][i] * inverse for i in rest}
            for l in range(j + 1, 8):
                across = columns[l][p][j : j + 1, :]
                for i in rest:
                    columns[l][i] = columns[l][i] - factor[i] * across
            across = left[p][j : j + 1, :]
            for i in rest:
                left[i] = left[i] - factor[i] * across
            for h in range(2 if p >= 2 else 1):
                across = right[p][h][j : j + 1, :]
                for i in rest:
                    right[i][h] = right[i][h] - factor[i] * across
        pivots.append(pivot)
    upper = []
    for i in range(4):
        scale = lax.rsqrt(pivots[i])
        upper.append(jnp.where(lane >= row + 8 * i, left[i] * scale, 0.0)[:, :32])
        right[i] = [part * scale for part in right[i]]
    return upper, right


def factor_kernel(total, high, low, q, upper, upon, under, result, factor, out_sem, factor_sem):
    pairs = high.shape[0]
    vectors, wide_y = q.shape[0], q.shape[2]
    above, inverse = eliminate(total[...])
    for i in range(4):
        factor[8 * i : 8 * i + 8, :] = above[i]
    store_factor = pltpu.make_async_copy(factor, upper, factor_sem)
    store_factor.start()
    shape = (8, 128)
    row, lane = lax.broadcasted_iota(jnp.int32, shape, 0), lax.broadcasted_iota(jnp.int32, shape, 1)
    same = (lane % 8 == row).astype(jnp.float32)
    for u in range(vectors // 2):
        below = u >= vectors // 4
        for h in range(2 if below else 1):
            block = inverse[u // 4][h]
            r = 2 * u % 8
            value = jnp.concatenate([block[r : r + 1, :] * same, block[r + 1 : r + 2, :] * same], axis=0)
            first = value.astype(jnp.bfloat16)
            second = (value - first.astype(jnp.float32)).astype(jnp.bfloat16)
            for place, part in enumerate((first, second, first)):
                if below:
                    under[16 * u - 128 : 16 * u - 112, 256 * place + 128 * h : 256 * place + 128 * h + 128] = part
                else:
                    upon[16 * u : 16 * u + 16, 128 * place : 128 * place + 128] = part

    def store(n, side):
        part, some = pl.ds(2 * n, 2), pl.ds(side * (vectors // 2), vectors // 2)
        return pltpu.make_async_copy(result.at[some, part], q.at[some, part], out_sem.at[n, side])

    def pair(n, side):
        first, second = high[n], low[n]
        if side:
            value = jnp.dot(
                under[...], jnp.concatenate([first, first, second], axis=0), preferred_element_type=jnp.float32)
        else:
            value = jnp.dot(
                upon[...], jnp.concatenate([first[:128], first[:128], second[:128]], axis=0),
                preferred_element_type=jnp.float32)
        for part in range(2):
            result[side * 16 : side * 16 + 16, 2 * n + part] = (
                value[:, part * 128 : part * 128 + 128].reshape(vectors // 2, wide_y, 128))
        store(n, side).start()

    def done(n, carry):
        store(n, 0).wait()
        store(n, 1).wait()
        return carry

    for side in range(2):
        for n in range(pairs):
            pair(n, side)
    lax.fori_loop(0, pairs, done, 0)
    store_factor.wait()


def on_device(base_state, adjoint_block):
    nx, ny = lax.axis_size("gx"), lax.axis_size("gy")
    vectors, _, wide_x, wide_y, lanes = adjoint_block.shape
    assert (vectors, wide_y, lanes) == (32, 8, 128)
    entries = float(3 * wide_x * wide_y * lanes * nx * ny)
    f32, bf16, dma = jnp.float32, jnp.bfloat16, pltpu.SemaphoreType.DMA
    vmem, anywhere = pl.BlockSpec(memory_space=pltpu.VMEM), pl.BlockSpec(memory_space=pl.ANY)
    planes = 3 * wide_x
    rows = vectors * planes * wide_y
    inner = (wide_x - 2) * (wide_y - 2)
    half = (planes // 2, vectors * wide_y, 256)
    base_state, rows_of, tiles_of = (
        pltpu.with_memory_space_constraint(part, pltpu.HBM)
        for part in (base_state, adjoint_block.reshape(vectors, 3, wide_x, wide_y, 1, 128), adjoint_block.reshape(rows, 128)))
    high, low, total = pl.pallas_call(
        functools.partial(step_kernel, nx, ny, entries),
        out_shape=(pltpu.VMEM(half, bf16), pltpu.VMEM(half, bf16), pltpu.VMEM((8, 128), f32)),
        in_specs=[anywhere, anywhere, anywhere],
        out_specs=(vmem, vmem, vmem),
        scratch_shapes=[
            pltpu.VMEM(base_state.shape, f32),
            pltpu.VMEM((rows, 128), f32),
            dma((2,)),
            pltpu.VMEM((2, wide_x, 3, WIDE, 128), f32),
            pltpu.VMEM((2, 2, 3, 128), f32),
            pltpu.VMEM((2, 3, WIDE, wide_y, 128), f32),
            pltpu.VMEM((2, wide_x, 3, WIDE, 128), f32),
            pltpu.VMEM((2, 3, WIDE, 128), f32),
            pltpu.VMEM((2, 3, 128), f32),
            pltpu.VMEM((3, wide_x + 4, wide_y + 8, 128), f32),
            pltpu.VMEM((3, wide_x + 2, wide_y + 8, 128), f32),
            pltpu.VMEM((15, wide_x, wide_y, 128), f32),
            pltpu.VMEM((3, wide_x + 2, wide_y + 2, vectors, 128), f32),
            pltpu.VMEM((3, wide_x, wide_y, vectors, 128), f32),
            pltpu.VMEM((3, 2 * vectors, inner * 128), bf16),
            pltpu.VMEM((3, 2 * vectors, (wide_x * wide_y - inner) * 128), bf16),
            pltpu.VMEM((rows, 128), f32),
            pltpu.VMEM((nx * ny, 8, 128), f32),
            dma((8,)), dma((8,)), dma((3, 4)), dma((3, 4)),
            pltpu.SemaphoreType.REGULAR((len(rounds(nx, ny)),)), dma, dma,
        ],
        compiler_params=pltpu.CompilerParams(
            collective_id=0, has_side_effects=True, vmem_limit_bytes=40 * 1024 * 1024),
    )(base_state, tiles_of, rows_of)
    high, low, total = (pltpu.with_memory_space_constraint(part, pltpu.VMEM) for part in (high, low, total))
    q_shape = (vectors, planes, wide_y, 128)
    q, upper = pl.pallas_call(
        factor_kernel,
        out_shape=(jax.ShapeDtypeStruct(q_shape, f32), jax.ShapeDtypeStruct((vectors, vectors), f32)),
        in_specs=[vmem, vmem, vmem],
        out_specs=(anywhere, anywhere),
        scratch_shapes=[
            pltpu.VMEM((vectors * wide_y // 2, 384), bf16),
            pltpu.VMEM((vectors * wide_y // 2, 768), bf16),
            pltpu.VMEM(q_shape, f32),
            pltpu.VMEM((vectors, vectors), f32),
            dma((planes // 2, 2)), dma,
        ],
        compiler_params=pltpu.CompilerParams(vmem_limit_bytes=40 * 1024 * 1024),
    )(total, high, low)
    return (q.reshape(adjoint_block.shape), upper)


def solution(mesh):
    in_specs = (P(None, "gx", "gy", None), P(None, None, "gx", "gy", None))
    out_specs = (P(None, None, "gx", "gy", None), P())
    return jax.shard_map(
        on_device, mesh=mesh, in_specs=in_specs, out_specs=out_specs, check_vma=False
    )
```

```python
import functools
import math

import jax
import jax.numpy as jnp
from jax import lax
from jax.experimental import pallas as pl
from jax.experimental.pallas import tpu as pltpu
from jax.sharding import PartitionSpec as P

ADVECT = 0.1
DIFFUSE = 0.08
DRIVE_SCALE = 0.25
WAVENUMBER = 4.0
MESH = pl.DeviceIdType.MESH


WIDE = 2
SIDES = ((-1, 0), (1, 0), (0, -1), (0, 1), (-1, -1), (-1, 1), (1, -1), (1, 1))


def neighbour(nx, ny, dx, dy):
    return (lax.rem(lax.axis_index("gx") + dx + nx, nx), lax.rem(lax.axis_index("gy") + dy + ny, ny))


def facing(nx, ny, role):
    odd = lax.rem(lax.axis_index("gx") if role < 2 else lax.axis_index("gy"), 2)
    up = odd if role % 2 == 0 else 1 - odd
    step = 2 * up - 1
    return (neighbour(nx, ny, step, 0) if role < 2 else neighbour(nx, ny, 0, step)), up


ROLES = (2, 3, 0, 1)


def meet(nx, ny):
    barrier = pltpu.get_barrier_semaphore()
    for role in ROLES:
        pl.semaphore_signal(barrier, inc=1, device_id=facing(nx, ny, role)[0], device_id_type=MESH)
    return barrier, len(ROLES)


@functools.cache
def rounds(nx, ny):
    known = {(0, 0), (1, 0), (nx - 1, 0), (0, 1), (0, ny - 1)}
    steps = []

    def add(dx, dy):
        assert (dx % nx, dy % ny) in known
        steps.append((dx, dy))
        for sign in (-1, 1):
            known.update({((x + sign * dx) % nx, (y + sign * dy) % ny) for x, y in reached})

    for size, unit in ((nx, (1, 0)), (ny, (0, 1))):
        reach = 1
        while 2 * reach < size:
            reached = set(known)
            add(reach * unit[0], reach * unit[1])
            reach *= 2
    while len(known) < nx * ny:
        reached = set(known)
        add(0, 1)
        reached = set(known)
        if len(known) < nx * ny:
            add(1, 0)
    return tuple(steps)


def tell(nx, ny, heard, n):
    dx, dy = rounds(nx, ny)[n]
    for sign in (-1, 1):
        pl.semaphore_signal(
            heard.at[n], inc=1, device_id=neighbour(nx, ny, sign * dx, sign * dy), device_id_type=MESH)


def each(low, high, body):
    if high - low <= 64:
        for i in range(low, high):
            body(i)
        return

    def run(i, carry):
        body(i)
        return carry

    lax.fori_loop(low, high, run, 0)


def advance_rows(bext, forcing, x, wide_y):
    rows = wide_y + 2
    centre = [bext[c, x + 1, 1 : 1 + rows, :] for c in range(3)]
    advanced = []
    for c in range(3):
        east, west = bext[c, x + 2, 1 : 1 + rows, :], bext[c, x, 1 : 1 + rows, :]
        north, south = bext[c, x + 1, 2 : 2 + rows, :], bext[c, x + 1, 0:rows, :]
        up, down = pltpu.roll(centre[c], 127, axis=1), pltpu.roll(centre[c], 1, axis=1)
        laplacian = east + west + north + south + up + down - 6.0 * centre[c]
        advection = centre[0] * (east - west) + centre[1] * (north - south) + centre[2] * (up - down)
        value = centre[c] + DIFFUSE * laplacian - ADVECT * advection
        advanced.append(value + forcing if c == 0 else value)
    return advanced


def step_kernel(
    nx, ny, entries, base_in, a_in, rows_in, high, low, total, base, a2, in_sem, edges, tips, bx, by, on_corner, off_corner, bext, adv, coef, at,
    part, inside, outside, natural, slots, base_send, base_recv, halo_send, halo_recv, heard, gram_send, gram_recv,
):
    wide_x, wide_y = base.shape[1], base.shape[2]
    vectors = at.shape[3]
    stride = 3 * wide_x * wide_y
    gx, gy = lax.axis_index("gx"), lax.axis_index("gy")
    devices, me = nx * ny, gx * ny + gy
    base_load = pltpu.make_async_copy(base_in, base, in_sem.at[0])
    load = pltpu.make_async_copy(a_in, a2, in_sem.at[1])
    base_load.start()
    barrier, met = meet(nx, ny)
    load.start()

    def move(c):
        def plane_of(x, carry):
            for y in range(wide_y):
                at[c, x + 1, y + 1] = a2[pl.ds((c * wide_x + x) * wide_y + y, vectors, stride=stride), :]
            return carry
        lax.fori_loop(0, wide_x, plane_of, 0)

    odd = lax.rem(gx, 2)

    def base_copy(i):
        if i < 4:
            dx, dy = SIDES[i]
            near_x = pl.ds(0, WIDE) if dx < 0 else pl.ds(wide_x - WIDE, WIDE)
            side = 0 if dy < 0 else 1
            src, dst = (base.at[:, near_x], bx.at[(1 - dx) // 2]) if dx else (edges.at[side], by.at[1 - side])
            peer = neighbour(nx, ny, dx, dy)
        elif i < 6:
            side = i - 4
            src, dst = tips.at[side, odd], off_corner.at[1 - side]
            peer = neighbour(nx, ny, 2 * odd - 1, 2 * side - 1)
        else:
            side = i - 6
            src, dst = by.at[side, (1 - odd) * (wide_x - 1)], on_corner.at[side]
            peer = neighbour(nx, ny, 1 - 2 * odd, 0)
        return pltpu.make_async_remote_copy(
            src, dst, base_send.at[i], base_recv.at[i], device_id=peer, device_id_type=MESH)

    inner_x, inner_y = pl.ds(1, wide_x), pl.ds(1, wide_y)

    def halo_start(c, role):
        peer, up = facing(nx, ny, role)
        if role < 2:
            side, near, far = up, up * (wide_x - 1), (1 - up) * (wide_x + 1)
            pairs = [(rows_in.at[:, c, near, y, 0], at.at[c, far, y + 1]) for y in range(wide_y)]
        else:
            side, near, far = 2 + up, up * (wide_y - 1), (1 - up) * (wide_y + 1)
            pairs = [(rows_in.at[:, c, x, near, 0], at.at[c, x + 1, far]) for x in range(wide_x)]
        for src, dst in pairs:
            pltpu.make_async_remote_copy(
                src, dst, halo_send.at[c, side], halo_recv.at[c, side], device_id=peer, device_id_type=MESH).start()

    def halo(c, i):
        dx, dy = SIDES[i]
        if dx:
            whole = at.at[c, wide_x + 1 if dx < 0 else 0, inner_y]
        else:
            whole = at.at[c, inner_x, wide_y + 1 if dy < 0 else 0]
        return pltpu.make_async_remote_copy(
            whole, whole, halo_send.at[c, i], halo_recv.at[c, i],
            device_id=neighbour(nx, ny, dx, dy), device_id_type=MESH)

    tells = len(rounds(nx, ny))

    def spread(n):
        if 0 < n <= tells:
            pl.semaphore_wait(heard.at[n - 1], 2)
        if n < tells:
            tell(nx, ny, heard, n)

    pl.semaphore_wait(barrier, met)
    spread(0)
    halo_start(0, 2)
    halo_start(0, 0)
    base_load.wait()
    for side, start in ((0, 0), (1, wide_y - WIDE)):
        for c in range(3):
            edges[side, :, c] = base[c, :, start : start + WIDE, :]
            outer = side * (wide_y - 1)
            for end, x in ((0, 0), (1, wide_x - 1)):
                tips[side, end, c : c + 1] = base[c, x, outer : outer + 1, :]
    for i in range(4):
        base_copy(i).start()
    halo_start(0, 3)
    halo_start(0, 1)
    spread(1)
    for i in (4, 5):
        base_copy(i).start()
    for c in (1, 2):
        for role in ROLES:
            halo_start(c, role)
    load.wait()
    for c in range(3):
        move(c)
    spread(2)

    for c in range(3):
        bext[c, WIDE : WIDE + wide_x, WIDE : WIDE + wide_y, :] = base[c]
    for i in (2, 3):
        base_copy(i).wait_recv()
    for i in (6, 7):
        base_copy(i).start()
    for i in (0, 1, 4, 5):
        base_copy(i).wait_recv()
    near, far = WIDE + wide_x, WIDE + wide_y
    on_x = WIDE - 1 + (1 - odd) * (wide_x + 1)
    off_x = WIDE - 1 + odd * (wide_x + 1)
    for c in range(3):
        for sx, start_x in ((0, 0), (1, near)):
            bext[c, start_x : start_x + WIDE, WIDE:far, :] = bx[sx, c]
        for sy, start_y in ((0, 0), (1, far)):
            bext[c, WIDE:near, start_y : start_y + WIDE, :] = by[sy, :, c]
            close = start_y + (1 - sy) * (WIDE - 1)
            bext[c, off_x, close : close + 1, :] = off_corner[sy, c : c + 1]
    for i in (6, 7):
        base_copy(i).wait_recv()
    for c in range(3):
        for sy, start_y in ((0, 0), (1, far)):
            bext[c, on_x, start_y : start_y + WIDE, :] = on_corner[sy, c]

    ny_total = wide_y * ny
    column = lax.broadcasted_iota(jnp.int32, (wide_y + 2, 128), 0) + (gy * wide_y + ny_total - 1)
    phases = 2.0 * math.pi * WAVENUMBER * lax.rem(column, ny_total).astype(jnp.float32) / float(ny_total)
    forcing = DRIVE_SCALE * jnp.sin(phases)
    for x in range(wide_x + 2):
        for c, value in enumerate(advance_rows(bext, forcing, x, wide_y)):
            adv[c, x, 0 : wide_y + 2, :] = value
    for x in range(wide_x):
        inner = [adv[m, x + 1, 1 : 1 + wide_y, :] for m in range(3)]
        coef[0, x] = ADVECT * adv[0, x + 2, 1 : 1 + wide_y, :] + DIFFUSE
        coef[1, x] = DIFFUSE - ADVECT * adv[0, x, 1 : 1 + wide_y, :]
        coef[2, x] = ADVECT * adv[1, x + 1, 2 : 2 + wide_y, :] + DIFFUSE
        coef[3, x] = DIFFUSE - ADVECT * adv[1, x + 1, 0:wide_y, :]
        coef[4, x] = ADVECT * inner[2] + DIFFUSE
        coef[5, x] = DIFFUSE - ADVECT * inner[2]
        for m in range(3):
            slopes = (
                adv[m, x + 2, 1 : 1 + wide_y, :] - adv[m, x, 1 : 1 + wide_y, :],
                adv[m, x + 1, 2 : 2 + wide_y, :] - adv[m, x + 1, 0:wide_y, :],
                pltpu.roll(inner[m], 127, axis=1) - pltpu.roll(inner[m], 1, axis=1),
            )
            for i in range(3):
                own = 1.0 - 6.0 * DIFFUSE if i == m else 0.0
                coef[6 + 3 * i + m, x] = own - ADVECT * slopes[i]

    spread(3)

    def halves(value):
        first = value.astype(jnp.bfloat16)
        return first, (value - first.astype(jnp.float32)).astype(jnp.bfloat16)

    def keep(where, c, place, value):
        lanes = slice(place * 128, place * 128 + 128)
        where[c, 0:vectors, lanes], where[c, vectors : 2 * vectors, lanes] = halves(value)

    def near_terms(c, x, y, west, east, south, north):
        own = [at[m, x + 1, y + 1] for m in range(3)]
        mine = at[c, x + 1, y + 1]
        k = lambda n: coef[n, x, y : y + 1, :]
        value = pltpu.roll(k(4) * mine, 127, axis=1) + pltpu.roll(k(5) * mine, 1, axis=1)
        for m in range(3):
            value += k(6 + 3 * c + m) * own[m]
        if east:
            value += k(0) * at[c, x + 2, y + 1]
        if west:
            value += k(1) * at[c, x, y + 1]
        if north:
            value += k(2) * at[c, x + 1, y + 2]
        if south:
            value += k(3) * at[c, x + 1, y]
        return value

    def row_of(c, x, y):
        return pl.ds((c * wide_x + x) * vectors * wide_y + y, vectors, stride=wide_y)

    def near_part(c, carry):
        for x in range(wide_x):
            for y in range(wide_y):
                value = near_terms(c, x, y, x > 0, x < wide_x - 1, y > 0, y < wide_y - 1)
                if 0 < x < wide_x - 1 and 0 < y < wide_y - 1:
                    natural[row_of(c, x, y), :] = value
                    keep(inside, c, (x - 1) * (wide_y - 2) + y - 1, value)
                else:
                    part[c, x, y] = value
        return carry

    lax.fori_loop(0, 3, near_part, 0)
    spread(4)

    def square(value):
        return lax.dot_general(value, value, (((1,), (1,)), ((), ())), preferred_element_type=jnp.float32)

    gram = square(inside[0]) + square(inside[1]) + square(inside[2])
    border = [(x, y) for x in range(wide_x) for y in range(wide_y)
              if not (0 < x < wide_x - 1 and 0 < y < wide_y - 1)]
    for c in range(3):
        for i in range(4):
            halo(c, i).wait_recv()
        for place, (x, y) in enumerate(border):
            k = lambda n: coef[n, x, y : y + 1, :]
            value = part[c, x, y]
            if x == 0:
                value += k(1) * at[c, 0, y + 1]
            if x == wide_x - 1:
                value += k(0) * at[c, wide_x + 1, y + 1]
            if y == 0:
                value += k(3) * at[c, x + 1, 0]
            if y == wide_y - 1:
                value += k(2) * at[c, x + 1, wide_y + 1]
            part[c, x, y] = value
            keep(outside, c, place, value)
        gram += square(outside[c])
        spread(5 + c)
    for n in range(8, tells + 1):
        spread(n)

    gram = gram[:vectors] + gram[vectors:]
    gram = gram[:, :vectors] + gram[:, vectors:]
    slots[me] = jnp.concatenate([gram[8 * i : 8 * i + 8] for i in range(4)], axis=1)

    def give(step):
        there = lax.rem(me + step, devices)
        pltpu.make_async_remote_copy(
            slots.at[me], slots.at[me], gram_send, gram_recv,
            device_id=(there // ny, lax.rem(there, ny)), device_id_type=MESH).start()

    each(1, devices, give)

    def place_border(c, carry):
        for x, y in border:
            natural[row_of(c, x, y), :] = part[c, x, y]
        return carry

    lax.fori_loop(0, 3, place_border, 0)

    def convert(n, carry):
        for side in range(2):
            value = natural[pl.ds(pl.multiple_of((2 * n + side) * vectors * wide_y, 256), vectors * wide_y), :]
            lanes = slice(side * 128, side * 128 + 128)
            high[n, :, lanes], low[n, :, lanes] = halves(value)
        return carry

    lax.fori_loop(0, high.shape[0], convert, 0)
    others = slots.at[pl.ds(0, devices - 1)]
    gathered = pltpu.make_async_remote_copy(
        others, others, gram_send, gram_recv, device_id=neighbour(nx, ny, 0, 1), device_id_type=MESH)
    gathered.wait_recv()
    if devices <= 64:
        level = [slots[i] for i in range(devices)]
        while len(level) > 1:
            level = [sum(level[i : i + 2][1:], level[i]) for i in range(0, len(level), 2)]
        summed = level[0]
    else:
        summed = lax.fori_loop(1, devices, lambda i, value: value + slots[i], slots[0])
    total[...] = summed / entries
    gathered.wait_send()
    for i in range(8):
        base_copy(i).wait_send()
    for c in range(3):
        for i in range(4):
            halo(c, i).wait_send()


def eliminate(packed, halfway):
    shape = packed.shape
    row, lane = lax.broadcasted_iota(jnp.int32, shape, 0), lax.broadcasted_iota(jnp.int32, shape, 1)
    left = [packed] + [pltpu.roll(packed, 128 - 32 * i, axis=1) for i in range(1, 4)]
    right = [[(lane // 8 + 16 * h == row + 8 * i).astype(jnp.float32) for h in range(2)] for i in range(4)]
    pivots = []
    for p in range(4):
        rest = range(p, 4)
        columns = [
            {i: jnp.broadcast_to(left[i][:, k : k + 1], shape) for i in rest} for k in range(8 * p, 8 * p + 8)]
        pivot = jnp.ones(shape, jnp.float32)
        for j in range(8):
            here = columns[j][p][j : j + 1, :]
            pivot = jnp.where(row == j, here, pivot)
            inverse = 1.0 / here
            columns[j][p] = jnp.where(row > j, columns[j][p], 0.0)
            factor = {i: columns[j][i] * inverse for i in rest}
            for l in range(j + 1, 8):
                across = columns[l][p][j : j + 1, :]
                for i in rest:
                    columns[l][i] = columns[l][i] - factor[i] * across
            across = left[p][j : j + 1, :]
            for i in rest:
                left[i] = left[i] - factor[i] * across
            for h in range(2 if p >= 2 else 1):
                across = right[p][h][j : j + 1, :]
                for i in rest:
                    right[i][h] = right[i][h] - factor[i] * across
        pivots.append(pivot)
        if p == 1:
            halfway([[part * lax.rsqrt(pivots[i]) for part in right[i]] for i in range(2)])
    upper = []
    for i in range(4):
        scale = lax.rsqrt(pivots[i])
        upper.append(jnp.where(lane >= row + 8 * i, left[i] * scale, 0.0)[:, :32])
        right[i] = [part * scale for part in right[i]]
    return upper, right


def factor_kernel(total, high, low, q, upper, upon, under, result, factor, out_sem, factor_sem):
    pairs = high.shape[0]
    vectors, wide_y = q.shape[0], q.shape[2]
    shape = (8, 128)
    row, lane = lax.broadcasted_iota(jnp.int32, shape, 0), lax.broadcasted_iota(jnp.int32, shape, 1)
    same = (lane % 8 == row).astype(jnp.float32)

    def build(u, inverse):
        below = u >= vectors // 4
        for h in range(2 if below else 1):
            block = inverse[u // 4][h]
            r = 2 * u % 8
            value = jnp.concatenate([block[r : r + 1, :] * same, block[r + 1 : r + 2, :] * same], axis=0)
            first = value.astype(jnp.bfloat16)
            second = (value - first.astype(jnp.float32)).astype(jnp.bfloat16)
            for place, part in enumerate((first, second, first)):
                if below:
                    under[16 * u - 128 : 16 * u - 112, 256 * place + 128 * h : 256 * place + 128 * h + 128] = part
                else:
                    upon[16 * u : 16 * u + 16, 128 * place : 128 * place + 128] = part

    def store(n, side):
        part, some = pl.ds(2 * n, 2), pl.ds(side * (vectors // 2), vectors // 2)
        return pltpu.make_async_copy(result.at[some, part], q.at[some, part], out_sem.at[n, side])

    def pair(n, side):
        first, second = high[n], low[n]
        if side:
            value = jnp.dot(
                under[...], jnp.concatenate([first, first, second], axis=0), preferred_element_type=jnp.float32)
        else:
            value = jnp.dot(
                upon[...], jnp.concatenate([first[:128], first[:128], second[:128]], axis=0),
                preferred_element_type=jnp.float32)
        for part in range(2):
            result[side * 16 : side * 16 + 16, 2 * n + part] = (
                value[:, part * 128 : part * 128 + 128].reshape(vectors // 2, wide_y, 128))

    def halfway(inverse):
        for u in range(vectors // 4):
            build(u, inverse)
        for n in range(pairs):
            pair(n, 0)

    above, inverse = eliminate(total[...], halfway)
    for i in range(4):
        factor[8 * i : 8 * i + 8, :] = above[i]
    store_factor = pltpu.make_async_copy(factor, upper, factor_sem)
    store_factor.start()

    def done(n, carry):
        store(n, 0).wait()
        store(n, 1).wait()
        return carry

    for n in range(pairs):
        store(n, 0).start()
    for u in range(vectors // 4, vectors // 2):
        build(u, inverse)
    for n in range(pairs):
        pair(n, 1)
        store(n, 1).start()
    lax.fori_loop(0, pairs, done, 0)
    store_factor.wait()


def on_device(base_state, adjoint_block):
    nx, ny = lax.axis_size("gx"), lax.axis_size("gy")
    vectors, _, wide_x, wide_y, lanes = adjoint_block.shape
    assert (vectors, wide_y, lanes) == (32, 8, 128)
    entries = float(3 * wide_x * wide_y * lanes * nx * ny)
    f32, bf16, dma = jnp.float32, jnp.bfloat16, pltpu.SemaphoreType.DMA
    vmem, anywhere = pl.BlockSpec(memory_space=pltpu.VMEM), pl.BlockSpec(memory_space=pl.ANY)
    planes = 3 * wide_x
    rows = vectors * planes * wide_y
    inner = (wide_x - 2) * (wide_y - 2)
    half = (planes // 2, vectors * wide_y, 256)
    base_state, rows_of, tiles_of = (
        pltpu.with_memory_space_constraint(part, pltpu.HBM)
        for part in (base_state, adjoint_block.reshape(vectors, 3, wide_x, wide_y, 1, 128), adjoint_block.reshape(rows, 128)))
    high, low, total = pl.pallas_call(
        functools.partial(step_kernel, nx, ny, entries),
        out_shape=(pltpu.VMEM(half, bf16), pltpu.VMEM(half, bf16), pltpu.VMEM((8, 128), f32)),
        in_specs=[anywhere, anywhere, anywhere],
        out_specs=(vmem, vmem, vmem),
        scratch_shapes=[
            pltpu.VMEM(base_state.shape, f32),
            pltpu.VMEM((rows, 128), f32),
            dma((2,)),
            pltpu.VMEM((2, wide_x, 3, WIDE, 128), f32),
            pltpu.VMEM((2, 2, 3, 128), f32),
            pltpu.VMEM((2, 3, WIDE, wide_y, 128), f32),
            pltpu.VMEM((2, wide_x, 3, WIDE, 128), f32),
            pltpu.VMEM((2, 3, WIDE, 128), f32),
            pltpu.VMEM((2, 3, 128), f32),
            pltpu.VMEM((3, wide_x + 4, wide_y + 8, 128), f32),
            pltpu.VMEM((3, wide_x + 2, wide_y + 8, 128), f32),
            pltpu.VMEM((15, wide_x, wide_y, 128), f32),
            pltpu.VMEM((3, wide_x + 2, wide_y + 2, vectors, 128), f32),
            pltpu.VMEM((3, wide_x, wide_y, vectors, 128), f32),
            pltpu.VMEM((3, 2 * vectors, inner * 128), bf16),
            pltpu.VMEM((3, 2 * vectors, (wide_x * wide_y - inner) * 128), bf16),
            pltpu.VMEM((rows, 128), f32),
            pltpu.VMEM((nx * ny, 8, 128), f32),
            dma((8,)), dma((8,)), dma((3, 4)), dma((3, 4)),
            pltpu.SemaphoreType.REGULAR((len(rounds(nx, ny)),)), dma, dma,
        ],
        compiler_params=pltpu.CompilerParams(
            collective_id=0, has_side_effects=True, vmem_limit_bytes=40 * 1024 * 1024),
    )(base_state, tiles_of, rows_of)
    high, low, total = (pltpu.with_memory_space_constraint(part, pltpu.VMEM) for part in (high, low, total))
    q_shape = (vectors, planes, wide_y, 128)
    q, upper = pl.pallas_call(
        factor_kernel,
        out_shape=(jax.ShapeDtypeStruct(q_shape, f32), jax.ShapeDtypeStruct((vectors, vectors), f32)),
        in_specs=[vmem, vmem, vmem],
        out_specs=(anywhere, anywhere),
        scratch_shapes=[
            pltpu.VMEM((vectors * wide_y // 2, 384), bf16),
            pltpu.VMEM((vectors * wide_y // 2, 768), bf16),
            pltpu.VMEM(q_shape, f32),
            pltpu.VMEM((vectors, vectors), f32),
            dma((planes // 2, 2)), dma,
        ],
        compiler_params=pltpu.CompilerParams(vmem_limit_bytes=40 * 1024 * 1024),
    )(total, high, low)
    return (q.reshape(adjoint_block.shape), upper)


def solution(mesh):
    in_specs = (P(None, "gx", "gy", None), P(None, None, "gx", "gy", None))
    out_specs = (P(None, None, "gx", "gy", None), P())
    return jax.shard_map(
        on_device, mesh=mesh, in_specs=in_specs, out_specs=out_specs, check_vma=False
    )
```

```python
import functools
import math

import jax
import jax.numpy as jnp
from jax import lax
from jax.experimental import pallas as pl
from jax.experimental.pallas import tpu as pltpu
from jax.sharding import PartitionSpec as P

ADVECT = 0.1
DIFFUSE = 0.08
DRIVE_SCALE = 0.25
WAVENUMBER = 4.0
MESH = pl.DeviceIdType.MESH


WIDE = 2
SIDES = ((-1, 0), (1, 0), (0, -1), (0, 1), (-1, -1), (-1, 1), (1, -1), (1, 1))


def neighbour(nx, ny, dx, dy):
    return (lax.rem(lax.axis_index("gx") + dx + nx, nx), lax.rem(lax.axis_index("gy") + dy + ny, ny))


def facing(nx, ny, role):
    odd = lax.rem(lax.axis_index("gx") if role < 2 else lax.axis_index("gy"), 2)
    up = odd if role % 2 == 0 else 1 - odd
    step = 2 * up - 1
    return (neighbour(nx, ny, step, 0) if role < 2 else neighbour(nx, ny, 0, step)), up


ROLES = (2, 3, 0, 1)


def meet(nx, ny):
    barrier = pltpu.get_barrier_semaphore()
    for role in (0, 2, 3, 1):
        pl.semaphore_signal(barrier, inc=1, device_id=facing(nx, ny, role)[0], device_id_type=MESH)
    return barrier, len(ROLES)


@functools.cache
def rounds(nx, ny):
    known = {(0, 0), (1, 0), (nx - 1, 0), (0, 1), (0, ny - 1)}
    steps = []

    def add(dx, dy):
        assert (dx % nx, dy % ny) in known
        steps.append((dx, dy))
        for sign in (-1, 1):
            known.update({((x + sign * dx) % nx, (y + sign * dy) % ny) for x, y in reached})

    for size, unit in ((nx, (1, 0)), (ny, (0, 1))):
        reach = 1
        while 2 * reach < size:
            reached = set(known)
            add(reach * unit[0], reach * unit[1])
            reach *= 2
    while len(known) < nx * ny:
        reached = set(known)
        add(0, 1)
        reached = set(known)
        if len(known) < nx * ny:
            add(1, 0)
    return tuple(steps)


def tell(nx, ny, heard, n):
    dx, dy = rounds(nx, ny)[n]
    for sign in (-1, 1):
        pl.semaphore_signal(
            heard.at[n], inc=1, device_id=neighbour(nx, ny, sign * dx, sign * dy), device_id_type=MESH)


def each(low, high, body):
    if high - low <= 64:
        for i in range(low, high):
            body(i)
        return

    def run(i, carry):
        body(i)
        return carry

    lax.fori_loop(low, high, run, 0)


def advance_rows(bext, forcing, x, wide_y):
    rows = wide_y + 2
    centre = [bext[c, x + 1, 1 : 1 + rows, :] for c in range(3)]
    advanced = []
    for c in range(3):
        east, west = bext[c, x + 2, 1 : 1 + rows, :], bext[c, x, 1 : 1 + rows, :]
        north, south = bext[c, x + 1, 2 : 2 + rows, :], bext[c, x + 1, 0:rows, :]
        up, down = pltpu.roll(centre[c], 127, axis=1), pltpu.roll(centre[c], 1, axis=1)
        laplacian = east + west + north + south + up + down - 6.0 * centre[c]
        advection = centre[0] * (east - west) + centre[1] * (north - south) + centre[2] * (up - down)
        value = centre[c] + DIFFUSE * laplacian - ADVECT * advection
        advanced.append(value + forcing if c == 0 else value)
    return advanced


def step_kernel(
    nx, ny, entries, base_in, a_in, rows_in, high, low, total, base, a2, in_sem, edges, tips, bx, by, on_corner, off_corner, bext, adv, coef, at,
    part, inside, outside, natural, slots, base_send, base_recv, halo_send, halo_recv, heard, gram_send, gram_recv,
):
    wide_x, wide_y = base.shape[1], base.shape[2]
    vectors = at.shape[3]
    stride = 3 * wide_x * wide_y
    gx, gy = lax.axis_index("gx"), lax.axis_index("gy")
    devices, me = nx * ny, gx * ny + gy
    base_load = pltpu.make_async_copy(base_in, base, in_sem.at[0])
    load = pltpu.make_async_copy(a_in, a2, in_sem.at[1])
    base_load.start()
    barrier, met = meet(nx, ny)
    load.start()

    def move(c):
        def plane_of(x, carry):
            for y in range(wide_y):
                at[c, x + 1, y + 1] = a2[pl.ds((c * wide_x + x) * wide_y + y, vectors, stride=stride), :]
            return carry
        lax.fori_loop(0, wide_x, plane_of, 0)

    odd = lax.rem(gx, 2)

    def base_copy(i):
        if i < 4:
            dx, dy = SIDES[i]
            near_x = pl.ds(0, WIDE) if dx < 0 else pl.ds(wide_x - WIDE, WIDE)
            side = 0 if dy < 0 else 1
            src, dst = (base.at[:, near_x], bx.at[(1 - dx) // 2]) if dx else (edges.at[side], by.at[1 - side])
            peer = neighbour(nx, ny, dx, dy)
        elif i < 6:
            side = i - 4
            src, dst = tips.at[side, odd], off_corner.at[1 - side]
            peer = neighbour(nx, ny, 2 * odd - 1, 2 * side - 1)
        else:
            side = i - 6
            src, dst = by.at[side, (1 - odd) * (wide_x - 1)], on_corner.at[side]
            peer = neighbour(nx, ny, 1 - 2 * odd, 0)
        return pltpu.make_async_remote_copy(
            src, dst, base_send.at[i], base_recv.at[i], device_id=peer, device_id_type=MESH)

    inner_x, inner_y = pl.ds(1, wide_x), pl.ds(1, wide_y)

    def halo_start(c, role):
        peer, up = facing(nx, ny, role)
        if role < 2:
            side, near, far = up, up * (wide_x - 1), (1 - up) * (wide_x + 1)
            pairs = [(rows_in.at[:, c, near, y, 0], at.at[c, far, y + 1]) for y in range(wide_y)]
        else:
            side, near, far = 2 + up, up * (wide_y - 1), (1 - up) * (wide_y + 1)
            pairs = [(rows_in.at[:, c, x, near, 0], at.at[c, x + 1, far]) for x in range(wide_x)]
        for src, dst in pairs:
            pltpu.make_async_remote_copy(
                src, dst, halo_send.at[c, side], halo_recv.at[c, side], device_id=peer, device_id_type=MESH).start()

    def halo(c, i):
        dx, dy = SIDES[i]
        if dx:
            whole = at.at[c, wide_x + 1 if dx < 0 else 0, inner_y]
        else:
            whole = at.at[c, inner_x, wide_y + 1 if dy < 0 else 0]
        return pltpu.make_async_remote_copy(
            whole, whole, halo_send.at[c, i], halo_recv.at[c, i],
            device_id=neighbour(nx, ny, dx, dy), device_id_type=MESH)

    tells = len(rounds(nx, ny))

    def spread(n):
        if 0 < n <= tells:
            pl.semaphore_wait(heard.at[n - 1], 2)
        if n < tells:
            tell(nx, ny, heard, n)

    pl.semaphore_wait(barrier, met)
    spread(0)
    halo_start(0, 2)
    halo_start(0, 0)
    base_load.wait()
    for side, start in ((0, 0), (1, wide_y - WIDE)):
        for c in range(3):
            edges[side, :, c] = base[c, :, start : start + WIDE, :]
            outer = side * (wide_y - 1)
            for end, x in ((0, 0), (1, wide_x - 1)):
                tips[side, end, c : c + 1] = base[c, x, outer : outer + 1, :]
    for i in range(4):
        base_copy(i).start()
    halo_start(0, 3)
    halo_start(0, 1)
    spread(1)
    for i in (4, 5):
        base_copy(i).start()
    for c in (1, 2):
        for role in ROLES:
            halo_start(c, role)
    load.wait()
    for c in range(3):
        move(c)
    spread(2)

    for c in range(3):
        bext[c, WIDE : WIDE + wide_x, WIDE : WIDE + wide_y, :] = base[c]
    for i in (2, 3):
        base_copy(i).wait_recv()
    for i in (6, 7):
        base_copy(i).start()
    for i in (0, 1, 4, 5):
        base_copy(i).wait_recv()
    near, far = WIDE + wide_x, WIDE + wide_y
    on_x = WIDE - 1 + (1 - odd) * (wide_x + 1)
    off_x = WIDE - 1 + odd * (wide_x + 1)
    for c in range(3):
        for sx, start_x in ((0, 0), (1, near)):
            bext[c, start_x : start_x + WIDE, WIDE:far, :] = bx[sx, c]
        for sy, start_y in ((0, 0), (1, far)):
            bext[c, WIDE:near, start_y : start_y + WIDE, :] = by[sy, :, c]
            close = start_y + (1 - sy) * (WIDE - 1)
            bext[c, off_x, close : close + 1, :] = off_corner[sy, c : c + 1]
    for i in (6, 7):
        base_copy(i).wait_recv()
    for c in range(3):
        for sy, start_y in ((0, 0), (1, far)):
            bext[c, on_x, start_y : start_y + WIDE, :] = on_corner[sy, c]

    ny_total = wide_y * ny
    column = lax.broadcasted_iota(jnp.int32, (wide_y + 2, 128), 0) + (gy * wide_y + ny_total - 1)
    phases = 2.0 * math.pi * WAVENUMBER * lax.rem(column, ny_total).astype(jnp.float32) / float(ny_total)
    forcing = DRIVE_SCALE * jnp.sin(phases)
    for x in range(wide_x + 2):
        for c, value in enumerate(advance_rows(bext, forcing, x, wide_y)):
            adv[c, x, 0 : wide_y + 2, :] = value
    for x in range(wide_x):
        inner = [adv[m, x + 1, 1 : 1 + wide_y, :] for m in range(3)]
        coef[0, x] = ADVECT * adv[0, x + 2, 1 : 1 + wide_y, :] + DIFFUSE
        coef[1, x] = DIFFUSE - ADVECT * adv[0, x, 1 : 1 + wide_y, :]
        coef[2, x] = ADVECT * adv[1, x + 1, 2 : 2 + wide_y, :] + DIFFUSE
        coef[3, x] = DIFFUSE - ADVECT * adv[1, x + 1, 0:wide_y, :]
        coef[4, x] = ADVECT * inner[2] + DIFFUSE
        coef[5, x] = DIFFUSE - ADVECT * inner[2]
        for m in range(3):
            slopes = (
                adv[m, x + 2, 1 : 1 + wide_y, :] - adv[m, x, 1 : 1 + wide_y, :],
                adv[m, x + 1, 2 : 2 + wide_y, :] - adv[m, x + 1, 0:wide_y, :],
                pltpu.roll(inner[m], 127, axis=1) - pltpu.roll(inner[m], 1, axis=1),
            )
            for i in range(3):
                own = 1.0 - 6.0 * DIFFUSE if i == m else 0.0
                coef[6 + 3 * i + m, x] = own - ADVECT * slopes[i]

    spread(3)

    def halves(value):
        first = value.astype(jnp.bfloat16)
        return first, (value - first.astype(jnp.float32)).astype(jnp.bfloat16)

    def keep(where, c, place, value):
        lanes = slice(place * 128, place * 128 + 128)
        where[c, 0:vectors, lanes], where[c, vectors : 2 * vectors, lanes] = halves(value)

    def near_terms(c, x, y, west, east, south, north):
        own = [at[m, x + 1, y + 1] for m in range(3)]
        mine = at[c, x + 1, y + 1]
        k = lambda n: coef[n, x, y : y + 1, :]
        value = pltpu.roll(k(4) * mine, 127, axis=1) + pltpu.roll(k(5) * mine, 1, axis=1)
        for m in range(3):
            value += k(6 + 3 * c + m) * own[m]
        if east:
            value += k(0) * at[c, x + 2, y + 1]
        if west:
            value += k(1) * at[c, x, y + 1]
        if north:
            value += k(2) * at[c, x + 1, y + 2]
        if south:
            value += k(3) * at[c, x + 1, y]
        return value

    def row_of(c, x, y):
        return pl.ds((c * wide_x + x) * vectors * wide_y + y, vectors, stride=wide_y)

    def near_part(c, carry):
        for x in range(wide_x):
            for y in range(wide_y):
                value = near_terms(c, x, y, x > 0, x < wide_x - 1, y > 0, y < wide_y - 1)
                if 0 < x < wide_x - 1 and 0 < y < wide_y - 1:
                    natural[row_of(c, x, y), :] = value
                    keep(inside, c, (x - 1) * (wide_y - 2) + y - 1, value)
                else:
                    part[c, x, y] = value
        return carry

    lax.fori_loop(0, 3, near_part, 0)
    spread(4)

    def square(value):
        return lax.dot_general(value, value, (((1,), (1,)), ((), ())), preferred_element_type=jnp.float32)

    gram = square(inside[0]) + square(inside[1]) + square(inside[2])
    border = [(x, y) for x in range(wide_x) for y in range(wide_y)
              if not (0 < x < wide_x - 1 and 0 < y < wide_y - 1)]
    for c in range(3):
        for i in range(4):
            halo(c, i).wait_recv()
        for place, (x, y) in enumerate(border):
            k = lambda n: coef[n, x, y : y + 1, :]
            value = part[c, x, y]
            if x == 0:
                value += k(1) * at[c, 0, y + 1]
            if x == wide_x - 1:
                value += k(0) * at[c, wide_x + 1, y + 1]
            if y == 0:
                value += k(3) * at[c, x + 1, 0]
            if y == wide_y - 1:
                value += k(2) * at[c, x + 1, wide_y + 1]
            part[c, x, y] = value
            keep(outside, c, place, value)
        gram += square(outside[c])
        spread(5 + c)
    for n in range(8, tells + 1):
        spread(n)

    gram = gram[:vectors] + gram[vectors:]
    gram = gram[:, :vectors] + gram[:, vectors:]
    slots[me] = jnp.concatenate([gram[8 * i : 8 * i + 8] for i in range(4)], axis=1)

    def give(step):
        there = lax.rem(me + step, devices)
        pltpu.make_async_remote_copy(
            slots.at[me], slots.at[me], gram_send, gram_recv,
            device_id=(there // ny, lax.rem(there, ny)), device_id_type=MESH).start()

    each(1, devices, give)

    def place_border(c, carry):
        for x, y in border:
            natural[row_of(c, x, y), :] = part[c, x, y]
        return carry

    lax.fori_loop(0, 3, place_border, 0)

    def convert(n, carry):
        for side in range(2):
            value = natural[pl.ds(pl.multiple_of((2 * n + side) * vectors * wide_y, 256), vectors * wide_y), :]
            lanes = slice(side * 128, side * 128 + 128)
            high[n, :, lanes], low[n, :, lanes] = halves(value)
        return carry

    lax.fori_loop(0, high.shape[0], convert, 0)
    others = slots.at[pl.ds(0, devices - 1)]
    gathered = pltpu.make_async_remote_copy(
        others, others, gram_send, gram_recv, device_id=neighbour(nx, ny, 0, 1), device_id_type=MESH)
    gathered.wait_recv()
    if devices <= 64:
        level = [slots[i] for i in range(devices)]
        while len(level) > 1:
            level = [sum(level[i : i + 2][1:], level[i]) for i in range(0, len(level), 2)]
        summed = level[0]
    else:
        summed = lax.fori_loop(1, devices, lambda i, value: value + slots[i], slots[0])
    total[...] = summed / entries
    gathered.wait_send()
    for i in range(8):
        base_copy(i).wait_send()
    for c in range(3):
        for i in range(4):
            halo(c, i).wait_send()


def eliminate(packed):
    shape = packed.shape
    row, lane = lax.broadcasted_iota(jnp.int32, shape, 0), lax.broadcasted_iota(jnp.int32, shape, 1)
    left = [packed] + [pltpu.roll(packed, 128 - 32 * i, axis=1) for i in range(1, 4)]
    right = [[(lane // 8 + 16 * h == row + 8 * i).astype(jnp.float32) for h in range(2)] for i in range(4)]
    pivots = []
    for p in range(4):
        rest = range(p, 4)
        columns = [
            {i: jnp.broadcast_to(left[i][:, k : k + 1], shape) for i in rest} for k in range(8 * p, 8 * p + 8)]
        pivot = jnp.ones(shape, jnp.float32)
        for j in range(8):
            here = columns[j][p][j : j + 1, :]
            pivot = jnp.where(row == j, here, pivot)
            inverse = 1.0 / here
            columns[j][p] = jnp.where(row > j, columns[j][p], 0.0)
            factor = {i: columns[j][i] * inverse for i in rest}
            for l in range(j + 1, 8):
                across = columns[l][p][j : j + 1, :]
                for i in rest:
                    columns[l][i] = columns[l][i] - factor[i] * across
            across = left[p][j : j + 1, :]
            for i in rest:
                left[i] = left[i] - factor[i] * across
            for h in range(2 if p >= 2 else 1):
                across = right[p][h][j : j + 1, :]
                for i in rest:
                    right[i][h] = right[i][h] - factor[i] * across
        pivots.append(pivot)
    upper = []
    for i in range(4):
        scale = lax.rsqrt(pivots[i])
        upper.append(jnp.where(lane >= row + 8 * i, left[i] * scale, 0.0)[:, :32])
        right[i] = [part * scale for part in right[i]]
    return upper, right


def factor_kernel(total, high, low, q, upper, upon, under, result, factor, out_sem, factor_sem):
    pairs = high.shape[0]
    vectors, wide_y = q.shape[0], q.shape[2]
    above, inverse = eliminate(total[...])
    for i in range(4):
        factor[8 * i : 8 * i + 8, :] = above[i]
    store_factor = pltpu.make_async_copy(factor, upper, factor_sem)
    store_factor.start()
    shape = (8, 128)
    row, lane = lax.broadcasted_iota(jnp.int32, shape, 0), lax.broadcasted_iota(jnp.int32, shape, 1)
    same = (lane % 8 == row).astype(jnp.float32)
    for u in range(vectors // 2):
        below = u >= vectors // 4
        for h in range(2 if below else 1):
            block = inverse[u // 4][h]
            r = 2 * u % 8
            value = jnp.concatenate([block[r : r + 1, :] * same, block[r + 1 : r + 2, :] * same], axis=0)
            first = value.astype(jnp.bfloat16)
            second = (value - first.astype(jnp.float32)).astype(jnp.bfloat16)
            for place, part in enumerate((first, second, first)):
                if below:
                    under[16 * u - 128 : 16 * u - 112, 256 * place + 128 * h : 256 * place + 128 * h + 128] = part
                else:
                    upon[16 * u : 16 * u + 16, 128 * place : 128 * place + 128] = part

    def store(n, side):
        part, some = pl.ds(2 * n, 2), pl.ds(side * (vectors // 2), vectors // 2)
        return pltpu.make_async_copy(result.at[some, part], q.at[some, part], out_sem.at[n, side])

    def pair(n, side):
        first, second = high[n], low[n]
        if side:
            value = jnp.dot(
                under[...], jnp.concatenate([first, first, second], axis=0), preferred_element_type=jnp.float32)
        else:
            value = jnp.dot(
                upon[...], jnp.concatenate([first[:128], first[:128], second[:128]], axis=0),
                preferred_element_type=jnp.float32)
        for part in range(2):
            result[side * 16 : side * 16 + 16, 2 * n + part] = (
                value[:, part * 128 : part * 128 + 128].reshape(vectors // 2, wide_y, 128))
        store(n, side).start()

    def done(n, carry):
        store(n, 0).wait()
        store(n, 1).wait()
        return carry

    for side in range(2):
        for n in range(pairs):
            pair(n, side)
    lax.fori_loop(0, pairs, done, 0)
    store_factor.wait()


def on_device(base_state, adjoint_block):
    nx, ny = lax.axis_size("gx"), lax.axis_size("gy")
    vectors, _, wide_x, wide_y, lanes = adjoint_block.shape
    assert (vectors, wide_y, lanes) == (32, 8, 128)
    entries = float(3 * wide_x * wide_y * lanes * nx * ny)
    f32, bf16, dma = jnp.float32, jnp.bfloat16, pltpu.SemaphoreType.DMA
    vmem, anywhere = pl.BlockSpec(memory_space=pltpu.VMEM), pl.BlockSpec(memory_space=pl.ANY)
    planes = 3 * wide_x
    rows = vectors * planes * wide_y
    inner = (wide_x - 2) * (wide_y - 2)
    half = (planes // 2, vectors * wide_y, 256)
    base_state, rows_of, tiles_of = (
        pltpu.with_memory_space_constraint(part, pltpu.HBM)
        for part in (base_state, adjoint_block.reshape(vectors, 3, wide_x, wide_y, 1, 128), adjoint_block.reshape(rows, 128)))
    high, low, total = pl.pallas_call(
        functools.partial(step_kernel, nx, ny, entries),
        out_shape=(pltpu.VMEM(half, bf16), pltpu.VMEM(half, bf16), pltpu.VMEM((8, 128), f32)),
        in_specs=[anywhere, anywhere, anywhere],
        out_specs=(vmem, vmem, vmem),
        scratch_shapes=[
            pltpu.VMEM(base_state.shape, f32),
            pltpu.VMEM((rows, 128), f32),
            dma((2,)),
            pltpu.VMEM((2, wide_x, 3, WIDE, 128), f32),
            pltpu.VMEM((2, 2, 3, 128), f32),
            pltpu.VMEM((2, 3, WIDE, wide_y, 128), f32),
            pltpu.VMEM((2, wide_x, 3, WIDE, 128), f32),
            pltpu.VMEM((2, 3, WIDE, 128), f32),
            pltpu.VMEM((2, 3, 128), f32),
            pltpu.VMEM((3, wide_x + 4, wide_y + 8, 128), f32),
            pltpu.VMEM((3, wide_x + 2, wide_y + 8, 128), f32),
            pltpu.VMEM((15, wide_x, wide_y, 128), f32),
            pltpu.VMEM((3, wide_x + 2, wide_y + 2, vectors, 128), f32),
            pltpu.VMEM((3, wide_x, wide_y, vectors, 128), f32),
            pltpu.VMEM((3, 2 * vectors, inner * 128), bf16),
            pltpu.VMEM((3, 2 * vectors, (wide_x * wide_y - inner) * 128), bf16),
            pltpu.VMEM((rows, 128), f32),
            pltpu.VMEM((nx * ny, 8, 128), f32),
            dma((8,)), dma((8,)), dma((3, 4)), dma((3, 4)),
            pltpu.SemaphoreType.REGULAR((len(rounds(nx, ny)),)), dma, dma,
        ],
        compiler_params=pltpu.CompilerParams(
            collective_id=0, has_side_effects=True, vmem_limit_bytes=40 * 1024 * 1024),
    )(base_state, tiles_of, rows_of)
    high, low, total = (pltpu.with_memory_space_constraint(part, pltpu.VMEM) for part in (high, low, total))
    q_shape = (vectors, planes, wide_y, 128)
    q, upper = pl.pallas_call(
        factor_kernel,
        out_shape=(jax.ShapeDtypeStruct(q_shape, f32), jax.ShapeDtypeStruct((vectors, vectors), f32)),
        in_specs=[vmem, vmem, vmem],
        out_specs=(anywhere, anywhere),
        scratch_shapes=[
            pltpu.VMEM((vectors * wide_y // 2, 384), bf16),
            pltpu.VMEM((vectors * wide_y // 2, 768), bf16),
            pltpu.VMEM(q_shape, f32),
            pltpu.VMEM((vectors, vectors), f32),
            dma((planes // 2, 2)), dma,
        ],
        compiler_params=pltpu.CompilerParams(vmem_limit_bytes=40 * 1024 * 1024),
    )(total, high, low)
    return (q.reshape(adjoint_block.shape), upper)


def solution(mesh):
    in_specs = (P(None, "gx", "gy", None), P(None, None, "gx", "gy", None))
    out_specs = (P(None, None, "gx", "gy", None), P())
    return jax.shard_map(
        on_device, mesh=mesh, in_specs=in_specs, out_specs=out_specs, check_vma=False
    )
```
